32 devices in a mesh: dp: 8 (over z, x), tensor: 4 (over y, core).
Axes of the slice: x: 2, y: 2, z: 4, core: 2. Of those that a mesh axis runs over, the one named last changes fastest.
Arguments:
- tokens: bfloat16 [16384, 768], P(('dp', 'tensor')), may hold values from -6 to 6
- stack: bfloat16 [4, 16384, 768], P(None, ('dp', 'tensor')), may hold values from -6 to 6
- cotangent: bfloat16 [16384, 768], P(('dp', 'tensor')), may hold values from -6 to 6
- starts: int32 [16, 2], P('dp'), may hold values from 0 to 768
- w_query: bfloat16 [768, 768], P('dp', 'tensor'), may hold values from -0.21875 to 0.21875
- w_key: bfloat16 [768, 768], P('dp', 'tensor'), may hold values from -0.21875 to 0.21875
- w_value: bfloat16 [768, 768], P('dp', 'tensor'), may hold values from -0.21875 to 0.21875
- w_output: bfloat16 [768, 768], P('tensor', 'dp'), may hold values from -0.875 to 0.875
- w_in: bfloat16 [768, 3072], P('dp', 'tensor'), may hold values from -0.21875 to 0.21875
- w_out: bfloat16 [3072, 768], P('tensor', 'dp'), may hold values from -0.109375 to 0.109375
- gain_one: float32 [768], replicated, may hold values from 0.1 to 1.9
- shift_one: float32 [768], replicated, may hold values from -3 to 3
- gain_two: float32 [768], replicated, may hold values from 0.1 to 1.9
- shift_two: float32 [768], replicated, may hold values from -3 to 3
- bias_in: float32 [3072], replicated, may hold values from -3 to 3
- bias_out: float32 [768], replicated, may hold values from -3 to 3
- depth_weights: float32 [5], replicated, may hold values from 0.3 to 1.2
Outputs:
- layer_out: bfloat16 [16384, 768], P(('dp', 'tensor'))
- grad_tokens: float32 [16384, 768], P(('dp', 'tensor'))
- grad_stack: float32 [4, 16384, 768], P(None, ('dp', 'tensor'))
- grad_w_query: float32 [768, 768], P('dp', 'tensor')
- grad_w_key: float32 [768, 768], P('dp', 'tensor')
- grad_w_value: float32 [768, 768], P('dp', 'tensor')
- grad_w_output: float32 [768, 768], P('tensor', 'dp')
- grad_w_in: float32 [768, 3072], P('dp', 'tensor')
- grad_w_out: float32 [3072, 768], P('tensor', 'dp')
- grad_gain_one: float32 [768], replicated
- grad_shift_one: float32 [768], replicated
- grad_gain_two: float32 [768], replicated
- grad_shift_two: float32 [768], replicated
- grad_bias_in: float32 [3072], replicated
- grad_bias_out: float32 [768], replicated
- grad_depth: float32 [5], replicated
The draws below stay inside these ranges and needn't reach their ends.
All inputs are finite; a program needn't handle non-finite values.
Results may differ from the reference program's by a relative error of at most 0.012.
Values may be sent and summed in bfloat16 or wider, within the bound.
A program may use at most 128 MiB of HBM per device.

```python
import math
import jax
import jax.numpy as jnp
from jax import lax

D = 768
FF = 3072
HEADS = 12
HEAD_DIM = 64
LENGTH = 1024
PIECE = 256
PIECES = 2
SEQ_GROUP = 2
SEQS = 16
TOKENS = 16384
N_DP = 8


def set_ends(values, own_key, low, top_value):
    longest = values.shape.index(max(values.shape))
    spots = []
    for shift in (0, 1):
        where = [jax.random.randint(jax.random.fold_in(own_key, axis), (), 0, length) for axis, length in enumerate(values.shape)]
        where[longest] = (where[longest] + shift) % values.shape[longest]
        spots.append(tuple(where))
    return values.at[spots[0]].set(low).at[spots[1]].set(top_value)


def level_of(rng, dims, split, least, high):
    def one(axis_at, blocks):
        heights = jax.random.uniform(jax.random.fold_in(jax.random.fold_in(rng, 6), axis_at), (blocks,), jnp.float32, least / len(split), high / len(split))
        return jnp.repeat(jnp.exp(heights), dims[axis_at] // blocks).reshape((-1,) + (1,) * (len(dims) - axis_at - 1))

    loudness = one(*split[0])
    for cut in split[1:]:
        loudness = loudness * one(*cut)
    return loudness


def centred(own_key, shape, scale, most, shards=(), held_as=jnp.bfloat16):
    loudness = level_of(own_key, shape, shards, -0.22, 0.18) if shards else 1.0
    values = jax.random.normal(own_key, shape, jnp.float32) * scale * loudness
    return jnp.minimum(jnp.maximum(values, -most), most).astype(held_as)


def setup_inputs(seed: int = 0) -> dict:
    key_list = jax.random.split(jax.random.key(seed), 18)
    return {
        "tokens": centred(key_list[0], (TOKENS, D), 1.0, 6.0, ((0, 32),)),
        "stack": centred(key_list[1], (4, TOKENS, D), 1.0, 6.0, ((1, 32),)),
        "cotangent": centred(key_list[2], (TOKENS, D), 1.0, 6.0, ((0, 32),)),
        "starts": set_ends(jax.random.randint(key_list[3], (SEQS, PIECES), 0, LENGTH - PIECE + 1), jax.random.fold_in(key_list[3], 1), 0, LENGTH - PIECE).astype(jnp.int32),
        "w_query": centred(key_list[4], (D, D), D ** -0.5, 0.21875, ((0, 8), (1, 4))),
        "w_key": centred(key_list[5], (D, D), D ** -0.5, 0.21875, ((0, 8), (1, 4))),
        "w_value": centred(key_list[6], (D, D), D ** -0.5, 0.21875, ((0, 8), (1, 4))),
        "w_output": centred(key_list[7], (D, D), (D // 16) ** -0.5, 0.875, ((0, 4), (1, 8))),
        "w_in": centred(key_list[8], (D, FF), D ** -0.5, 0.21875, ((0, 8), (1, 4))),
        "w_out": centred(key_list[9], (FF, D), FF ** -0.5, 0.109375, ((0, 4), (1, 8))),
        "gain_one": jnp.clip(1.0 + 0.18 * jax.random.normal(key_list[10], (D,), jnp.float32), 0.1, 1.9),
        "shift_one": centred(key_list[11], (D,), 0.3, 3.0, (), jnp.float32),
        "gain_two": jnp.clip(1.0 + 0.18 * jax.random.normal(key_list[12], (D,), jnp.float32), 0.1, 1.9),
        "shift_two": centred(key_list[13], (D,), 0.3, 3.0, (), jnp.float32),
        "bias_in": centred(key_list[14], (FF,), 0.5, 3.0, (), jnp.float32),
        "bias_out": centred(key_list[15], (D,), 0.3, 3.0, (), jnp.float32),
        "depth_weights": jnp.clip(jax.random.uniform(key_list[16], (5,), jnp.float32, 0.3, 1.2), 0.3, 1.2),
    }


EPSILON = 1e-05
PRECISE = lax.Precision.HIGHEST
NEGATIVE = -1e+30

@jax.custom_vjp
def low(v):
    return lax.optimization_barrier(v.astype(jnp.bfloat16)).astype(jnp.float32)

@jax.custom_vjp
def low_back(v):
    return v

def low_keep(v):
    return (low(v), None)

def low_pass(kept, grad):
    return (grad,)

def back_keep(v):
    return (v, None)

def back_low(kept, grad):
    return (low(grad),)
low.defvjp(low_keep, low_pass)
low_back.defvjp(back_keep, back_low)

def layer_norm(values, gain, shift):
    centre = values - lax.optimization_barrier(jnp.mean(values, axis=-1, keepdims=True))
    spread = lax.optimization_barrier(jnp.mean(centre * centre, axis=-1, keepdims=True))
    return centre * lax.rsqrt(spread + EPSILON) * gain + shift

def tables(seq_length, head_size):
    half_dim = head_size // 2
    frequency = jnp.exp(-jnp.log(10000.0) * jnp.arange(half_dim, dtype=jnp.float32) * 2.0 / head_size)
    angles = jnp.arange(seq_length, dtype=jnp.float32)[:, None] * frequency[None, :]
    return (jnp.cos(angles), jnp.sin(angles))

def rotate(values, cosine_table, sine_table):
    half_dim = values.shape[-1] // 2
    front_half = values[..., :half_dim]
    back_half = values[..., half_dim:]
    cosines = cosine_table[:, None, :]
    sine_rows = sine_table[:, None, :]
    return jnp.concatenate([front_half * cosines - back_half * sine_rows, back_half * cosines + front_half * sine_rows], axis=-1)

def allowed_mask(starts, seq_length, piece_size):
    position = jnp.arange(seq_length, dtype=jnp.int32)
    inside = (position[None, None, :] >= starts[:, :, None]) & (position[None, None, :] < starts[:, :, None] + piece_size)
    jointly = jnp.any(inside[:, :, :, None] & inside[:, :, None, :], axis=1)
    return jointly | (position[None, :, None] >= position[None, None, :])

def group_block(params, token_rows, starts):
    wq_full, wk_full, wv_full, wo_full, win_full, wout_full, gain_first, shift_first, gain_second, shift_second, hidden_bias, output_bias = params
    seq_count = starts.shape[0]
    cosine_table, sine_table = tables(LENGTH, HEAD_DIM)
    score_scale = 1.0 / math.sqrt(HEAD_DIM)

    def to_heads(matrix):
        return matrix.reshape(seq_count, LENGTH, HEADS, HEAD_DIM)
    normed = low(layer_norm(token_rows, gain_first, shift_first))
    query = low(rotate(to_heads(low_back(jnp.dot(normed, wq_full, precision=PRECISE))), cosine_table, sine_table))
    key_rows = low(rotate(to_heads(low_back(jnp.dot(normed, wk_full, precision=PRECISE))), cosine_table, sine_table))
    value_rows = to_heads(low(low_back(jnp.dot(normed, wv_full, precision=PRECISE))))
    scores = low_back(jnp.einsum('sqhd,skhd->shqk', query, key_rows, precision=PRECISE) * score_scale)
    scores = jnp.where(allowed_mask(starts, LENGTH, PIECE)[:, None], scores, NEGATIVE)
    highest = lax.optimization_barrier(jnp.max(scores, axis=-1, keepdims=True))
    powers = jnp.exp(scores - highest)
    attention = low(powers / lax.optimization_barrier(jnp.sum(powers, axis=-1, keepdims=True)))
    mixed_rows = jnp.einsum('shqk,skhd->sqhd', attention, value_rows, precision=PRECISE).reshape(seq_count * LENGTH, D)
    mixed_rows = low(low_back(mixed_rows))
    middle = token_rows + low_back(jnp.dot(mixed_rows, wo_full, precision=PRECISE))
    second = low(layer_norm(middle, gain_second, shift_second))
    pre_act = low_back(jnp.dot(second, win_full, precision=PRECISE) + hidden_bias)
    activated = low(jax.nn.gelu(pre_act, approximate=True))
    return middle + low_back(jnp.dot(activated, wout_full, precision=PRECISE)) + output_bias

def reference(tokens, stack, cotangent, starts, w_query, w_key, w_value, w_output, w_in, w_out, gain_one, shift_one, gain_two, shift_two, bias_in, bias_out, depth_weights):
    params = (w_query.astype(jnp.float32), w_key.astype(jnp.float32), w_value.astype(jnp.float32), w_output.astype(jnp.float32), w_in.astype(jnp.float32), w_out.astype(jnp.float32), gain_one, shift_one, gain_two, shift_two, bias_in, bias_out)
    token_rows = tokens.astype(jnp.float32)
    earlier = stack.astype(jnp.float32)
    grad_rows = cotangent.astype(jnp.float32)
    grouped_starts = starts.reshape(N_DP, SEQ_GROUP, PIECES)

    def forward(params, token_rows, earlier, depth_weights):

        def one_group(entries):
            return group_block(params, entries[0], entries[1])
        blocks = lax.map(jax.checkpoint(one_group), (token_rows.reshape(N_DP, SEQ_GROUP * LENGTH, D), grouped_starts))
        block_out = blocks.reshape(N_DP * SEQ_GROUP * LENGTH, D)
        return jnp.einsum('k,krd->rd', depth_weights[:4], earlier, precision=PRECISE) + depth_weights[4] * block_out
    result, pullback = jax.vjp(forward, params, token_rows, earlier, depth_weights)
    grad_params, grad_tokens, grad_stack, grad_depth = pullback(grad_rows)
    return (result.astype(jnp.bfloat16), grad_tokens, grad_stack, grad_params[0], grad_params[1], grad_params[2], grad_params[3], grad_params[4], grad_params[5], grad_params[6], grad_params[7], grad_params[8], grad_params[9], grad_params[10], grad_params[11], grad_depth)
```

```python
import functools
import math

import jax
import jax.numpy as jnp
import numpy as np
from jax import lax
from jax.experimental import pallas as pl
from jax.experimental.pallas import tpu as pltpu
from jax.sharding import PartitionSpec as P

HEAD_DIM = 64
PIECE = 256


EPSILON = 1e-05
NEGATIVE = -1e30


def layer_norm(values, gain, shift):
    centre = values - jnp.mean(values, axis=-1, keepdims=True)
    spread = jnp.mean(centre * centre, axis=-1, keepdims=True)
    return centre * lax.rsqrt(spread + EPSILON) * gain + shift


def tables(seq_length, head_size):
    half_dim = head_size // 2
    frequency = jnp.exp(
        -jnp.log(10000.0) * jnp.arange(half_dim, dtype=jnp.float32) * 2.0 / head_size
    )
    angles = jnp.arange(seq_length, dtype=jnp.float32)[:, None] * frequency[None, :]
    return (jnp.cos(angles), jnp.sin(angles))


def rotate(values, cosine_table, sine_table):
    half_dim = values.shape[-1] // 2
    front_half = values[..., :half_dim]
    back_half = values[..., half_dim:]
    cosines = cosine_table[:, None, :]
    sine_rows = sine_table[:, None, :]
    return jnp.concatenate(
        [
            front_half * cosines - back_half * sine_rows,
            back_half * cosines + front_half * sine_rows,
        ],
        axis=-1,
    )


def allowed_mask(starts, seq_length, piece_size):
    position = jnp.arange(seq_length, dtype=jnp.int32)
    inside = (position[None, None, :] >= starts[:, :, None]) & (
        position[None, None, :] < starts[:, :, None] + piece_size
    )
    jointly = jnp.any(inside[:, :, :, None] & inside[:, :, None, :], axis=1)
    return jointly | (position[None, :, None] >= position[None, None, :])


def gelu_tanh(values):
    return jax.nn.gelu(values, approximate=True)


def right_transposed(matrix, weight):
    return lax.dot_general(
        matrix, weight, (((1,), (1,)), ((), ())), preferred_element_type=jnp.float32
    )


def left_transposed(matrix, other):
    return lax.dot_general(
        matrix, other, (((0,), (0,)), ((), ())), preferred_element_type=jnp.float32
    )


def attend_forward(query, key_rows, value_rows, allowed, score_scale):

    def one_sequence(entries):
        query_seq, key_seq, value_seq, allowed_seq = entries
        scores = (
            jnp.einsum("qhd,khd->hqk", query_seq, key_seq, preferred_element_type=jnp.float32)
            * score_scale
        )
        scores = jnp.where(allowed_seq[None], scores, NEGATIVE)
        highest = jnp.max(scores, axis=-1, keepdims=True)
        powers = jnp.exp(scores - highest)
        row_total = jnp.sum(powers, axis=-1, keepdims=True)
        attention = (powers / row_total).astype(jnp.bfloat16)
        mixed_rows = jnp.einsum(
            "hqk,khd->qhd", attention, value_seq, preferred_element_type=jnp.float32
        )
        return (mixed_rows.astype(jnp.bfloat16), highest + jnp.log(row_total))

    return lax.map(one_sequence, (query, key_rows, value_rows, allowed))


def attend_backward(query, key_rows, value_rows, grad_mixed, log_totals, allowed, score_scale):

    def one_sequence(entries):
        query_seq, key_seq, value_seq, grad_seq, log_seq, allowed_seq = entries
        scores = (
            jnp.einsum("qhd,khd->hqk", query_seq, key_seq, preferred_element_type=jnp.float32)
            * score_scale
        )
        scores = jnp.where(allowed_seq[None], scores, NEGATIVE)
        attention = jnp.exp(scores - log_seq)
        grad_value = jnp.einsum(
            "hqk,qhd->khd",
            attention.astype(jnp.bfloat16),
            grad_seq,
            preferred_element_type=jnp.float32,
        )
        grad_attention = jnp.einsum(
            "qhd,khd->hqk", grad_seq, value_seq, preferred_element_type=jnp.float32
        )
        row_delta = jnp.sum(attention * grad_attention, axis=-1, keepdims=True)
        grad_scores = (attention * (grad_attention - row_delta)).astype(jnp.bfloat16)
        grad_query = (
            jnp.einsum("hqk,khd->qhd", grad_scores, key_seq, preferred_element_type=jnp.float32)
            * score_scale
        )
        grad_key = (
            jnp.einsum("hqk,qhd->khd", grad_scores, query_seq, preferred_element_type=jnp.float32)
            * score_scale
        )
        return (grad_query, grad_key, grad_value.astype(jnp.bfloat16))

    return lax.map(one_sequence, (query, key_rows, value_rows, grad_mixed, log_totals, allowed))


def plain_device(
    tokens,
    stack,
    cotangent,
    starts,
    w_query,
    w_key,
    w_value,
    w_output,
    w_in,
    w_out,
    gain_one,
    shift_one,
    gain_two,
    shift_two,
    bias_in,
    bias_out,
    depth_weights,
):
    rows_here = tokens.shape[0]
    features = tokens.shape[1]
    groups = lax.axis_size("tensor")
    position = lax.axis_index("tensor")
    seq_count = starts.shape[0]
    seq_length = rows_here * groups // seq_count
    score_scale = 1.0 / math.sqrt(HEAD_DIM)
    local_heads = w_query.shape[1] // HEAD_DIM
    hidden = w_in.shape[1]
    cosine_table, sine_table = tables(seq_length, HEAD_DIM)
    allowed = allowed_mask(starts, seq_length, PIECE)

    def to_heads(matrix):
        return matrix.reshape(seq_count, seq_length, local_heads, HEAD_DIM)

    def from_heads(blocks):
        return blocks.reshape(seq_count * seq_length, local_heads * HEAD_DIM)

    def share_rows(local_rows):
        return lax.all_gather(local_rows, "tensor", axis=0, tiled=True)

    def share_grad(local_rows):
        return lax.all_gather(local_rows, "tensor", axis=0, tiled=True)

    def merge_rows(source, weight):
        return lax.psum_scatter(
            jnp.dot(source, weight, preferred_element_type=jnp.float32),
            "tensor",
            scatter_dimension=0,
            tiled=True,
        )

    def return_rows(pairs):
        running = jnp.zeros((lax.axis_size("tensor") * rows_here, features), jnp.float32)
        for source, weight in pairs:
            running = running + right_transposed(source, weight)
        return lax.psum_scatter(running, "tensor", scatter_dimension=0, tiled=True)

    query_w, key_w, value_w, output_w = (
        lax.all_gather(w_query, "dp", axis=0, tiled=True),
        lax.all_gather(w_key, "dp", axis=0, tiled=True),
        lax.all_gather(w_value, "dp", axis=0, tiled=True),
        lax.all_gather(w_output, "dp", axis=1, tiled=True),
    )
    inner_w, outer_w = (
        lax.all_gather(w_in, "dp", axis=0, tiled=True),
        lax.all_gather(w_out, "dp", axis=1, tiled=True),
    )
    token_rows = tokens.astype(jnp.float32)
    normed_one = layer_norm(token_rows, gain_one, shift_one).astype(jnp.bfloat16)
    normed_all = share_rows(normed_one)
    query = rotate(
        to_heads(jnp.dot(normed_all, query_w, preferred_element_type=jnp.float32)),
        cosine_table,
        sine_table,
    ).astype(jnp.bfloat16)
    key_rows = rotate(
        to_heads(jnp.dot(normed_all, key_w, preferred_element_type=jnp.float32)),
        cosine_table,
        sine_table,
    ).astype(jnp.bfloat16)
    value_rows = to_heads(jnp.dot(normed_all, value_w, preferred_element_type=jnp.float32)).astype(
        jnp.bfloat16
    )
    mixed_heads, log_totals = attend_forward(query, key_rows, value_rows, allowed, score_scale)
    mixed_flat = from_heads(mixed_heads)
    middle = token_rows + merge_rows(mixed_flat, output_w)
    normed_two = layer_norm(middle, gain_two, shift_two).astype(jnp.bfloat16)
    second_all = share_rows(normed_two)
    bias_slice = lax.dynamic_slice_in_dim(bias_in, position * hidden, hidden)
    pre_act = jnp.dot(second_all, inner_w, preferred_element_type=jnp.float32) + bias_slice
    activated = gelu_tanh(pre_act).astype(jnp.bfloat16)
    block_out = middle + merge_rows(activated, outer_w) + bias_out
    averaged = depth_weights[4] * block_out
    for layer_index in range(4):
        averaged = averaged + depth_weights[layer_index] * stack[layer_index].astype(jnp.float32)
    layer_out = averaged.astype(jnp.bfloat16)
    grad_rows = cotangent.astype(jnp.float32)
    grad_stack = jnp.stack([depth_weights[layer_index] * grad_rows for layer_index in range(4)])
    depth_terms = jnp.stack(
        [jnp.sum(stack[layer_index].astype(jnp.float32) * grad_rows) for layer_index in range(4)]
        + [jnp.sum(block_out * grad_rows)]
    )
    grad_block = depth_weights[4] * grad_rows
    grad_bias_out = jnp.sum(grad_block, axis=0)
    grad_sent = share_grad(grad_block.astype(jnp.bfloat16))
    grad_outer = left_transposed(activated, grad_sent)
    grad_act = right_transposed(grad_sent, outer_w)
    grad_pre = jax.vjp(gelu_tanh, pre_act)[1](grad_act)[0].astype(jnp.bfloat16)
    grad_bias_slice = jnp.sum(grad_pre.astype(jnp.float32), axis=0)
    bias_full = lax.dynamic_update_slice_in_dim(
        jnp.zeros((bias_in.shape[0],), jnp.float32), grad_bias_slice, position * hidden, 0
    )
    grad_inner = left_transposed(second_all, grad_pre)
    grad_norm_two = return_rows(((grad_pre, inner_w),))
    layer_two = jax.vjp(layer_norm, middle, gain_two, shift_two)[1](grad_norm_two)
    grad_middle = grad_block + layer_two[0]
    grad_attn_sent = share_grad(grad_middle.astype(jnp.bfloat16))
    grad_output_w = left_transposed(mixed_flat, grad_attn_sent)
    grad_mixed = right_transposed(grad_attn_sent, output_w).astype(jnp.bfloat16)
    grad_query, grad_key, grad_value = attend_backward(
        query, key_rows, value_rows, to_heads(grad_mixed), log_totals, allowed, score_scale
    )
    grad_query = from_heads(rotate(grad_query, cosine_table, -sine_table)).astype(jnp.bfloat16)
    grad_key = from_heads(rotate(grad_key, cosine_table, -sine_table)).astype(jnp.bfloat16)
    grad_value = from_heads(grad_value)
    grad_query_w = left_transposed(normed_all, grad_query)
    grad_key_w = left_transposed(normed_all, grad_key)
    grad_value_w = left_transposed(normed_all, grad_value)
    grad_norm_one = return_rows(((grad_query, query_w), (grad_key, key_w), (grad_value, value_w)))
    layer_one = jax.vjp(layer_norm, token_rows, gain_one, shift_one)[1](grad_norm_one)
    grad_tokens = grad_middle + layer_one[0]
    grad_w_query, grad_w_key, grad_w_value, grad_w_output, grad_w_in, grad_w_out = (
        lax.psum_scatter(grad_query_w, "dp", scatter_dimension=0, tiled=True),
        lax.psum_scatter(grad_key_w, "dp", scatter_dimension=0, tiled=True),
        lax.psum_scatter(grad_value_w, "dp", scatter_dimension=0, tiled=True),
        lax.psum_scatter(grad_output_w, "dp", scatter_dimension=1, tiled=True),
        lax.psum_scatter(grad_inner, "dp", scatter_dimension=0, tiled=True),
        lax.psum_scatter(grad_outer, "dp", scatter_dimension=1, tiled=True),
    )
    summed = lax.psum(
        (
            layer_one[1],
            layer_one[2],
            layer_two[1],
            layer_two[2],
            bias_full,
            grad_bias_out,
            depth_terms,
        ),
        ("dp", "tensor"),
    )
    return (
        layer_out,
        grad_tokens,
        grad_stack,
        grad_w_query,
        grad_w_key,
        grad_w_value,
        grad_w_output,
        grad_w_in,
        grad_w_out,
        summed[0],
        summed[1],
        summed[2],
        summed[3],
        summed[4],
        summed[5],
        summed[6],
    )


BF = jnp.bfloat16
F32 = jnp.float32
MESH = pl.DeviceIdType.MESH
BLOCK = 256
EXPONENT_SCALE = math.log2(math.e) / math.sqrt(HEAD_DIM)


def dot(left, right, left_axis, right_axis):
    return lax.dot_general(
        left, right, (((left_axis,), (right_axis,)), ((), ())), preferred_element_type=F32
    )


def norm_parts(values):
    centre = values - jnp.mean(values, axis=-1, keepdims=True)
    inverse = lax.rsqrt(jnp.mean(centre * centre, axis=-1, keepdims=True) + EPSILON)
    return centre * inverse, inverse


def norm_back(grad, gain, unit, inverse):
    scaled = grad * gain
    first = jnp.mean(scaled, axis=-1, keepdims=True)
    second = jnp.mean(scaled * unit, axis=-1, keepdims=True)
    return inverse * (scaled - first - unit * second)


def gelu_pair(values):
    root = math.sqrt(2.0 / math.pi)
    square = values * values
    bend = jnp.tanh(root * values * (1.0 + 0.044715 * square))
    half = 0.5 * (1.0 + bend)
    slope = half + 0.5 * root * values * (1.0 - bend * bend) * (1.0 + 3 * 0.044715 * square)
    return values * half, slope


def column_sum(values):
    return jnp.sum(values, axis=0, keepdims=True)


def rotary_tables(length):
    half = HEAD_DIM // 2
    frequency = np.exp(-np.log(10000.0) * np.arange(half) * 2.0 / HEAD_DIM)
    angles = np.arange(length)[:, None] * frequency[None, :]
    return np.cos(angles).astype(np.float32), np.sin(angles).astype(np.float32)


def fused_body(
    nz,
    rows,
    features,
    shard,
    tokens,
    cotangent,
    stack,
    packed,
    vectors,
    bias_in,
    depth,
    starts,
    cosine,
    sine,
    cosine_t,
    sine_t,
    layer_out,
    grad_tokens,
    grad_packed,
    grad_vectors,
    G,
    D,
    RY,
    RX,
    RZ,
    A,
    C,
    GM,
    GL,
    K,
    V,
    KT,
    QT,
    OT,
    LS,
    MB,
    Z,
    GP,
    GOT,
    GT,
    WO,
    R32,
    AVG,
    SR,
    XR,
    SB,
    XB,
    XG,
    XA,
    VS,
    VR,
    VZ,
    GKA,
    GVA,
    local_sem,
    ag_send,
    ag_recv,
    rs_send,
    rs_recv,
    sib_send,
    sib_recv,
    vec_send,
    vec_recv,
):
    length = 2 * rows
    heads = 3
    width = heads * HEAD_DIM
    dp = lax.axis_index("dp")
    t = lax.axis_index("tensor")
    z = dp // 2
    x = lax.rem(dp, 2)
    low = lax.rem(t, 2)
    pair = t // 2
    other = 1 - low
    sib = (dp, t + 1 - 2 * low)
    ypeer = (dp, lax.rem(t + 2, 4))
    xpeer = (dp + 1 - 2 * x, t)

    def zpeer(j):
        return (lax.rem(z + j, nz) * 2 + x, t)

    def remote(src, dst, send, recv, peer):
        return pltpu.make_async_remote_copy(
            src_ref=src, dst_ref=dst, send_sem=send, recv_sem=recv,
            device_id=peer, device_id_type=MESH,
        )

    def gather_z(k):
        return [
            remote(G.at[k, 0, z, x], G.at[k, 0, z, x], ag_send.at[k, j], ag_recv.at[k, j], zpeer(j + 1))
            for j in range(nz - 1)
        ]

    def gather_z_in(k):
        return [
            remote(
                G.at[k, 0, z, x], G.at[k, 0, lax.rem(z + nz - 1 - j, nz), x],
                ag_send.at[k, j], ag_recv.at[k, j], zpeer(j + 1),
            )
            for j in range(nz - 1)
        ]

    def gather_x(k):
        return remote(
            G.at[k, 0, :, x], G.at[k, 0, :, x], ag_send.at[k, nz - 1], ag_recv.at[k, nz - 1], xpeer
        )

    def gather_y(k):
        return remote(G.at[k, 0], G.at[k, 1], ag_send.at[k, nz], ag_recv.at[k, nz], ypeer)

    def gather_step(k, step):
        if step == 0:
            for c in gather_z(k):
                c.start()
        elif step == 1:
            for c in gather_z_in(k):
                c.wait_recv()
            gather_x(k).start()
        elif step == 2:
            gather_x(k).wait_recv()
            gather_y(k).start()
        elif step == 3:
            gather_y(k).wait_recv()
        else:
            for c in gather_z(k):
                c.wait_send()
            gather_x(k).wait_send()
            gather_y(k).wait_send()

    def reduce_y(k):
        return remote(D.at[k, 1], RY.at[k], rs_send.at[k, 0], rs_recv.at[k, 0], ypeer)

    def reduce_x(k):
        return remote(D.at[k, 0, :, 1 - x], RX.at[k], rs_send.at[k, 1], rs_recv.at[k, 1], xpeer)

    def reduce_z(k):
        return [
            remote(
                D.at[k, 0, lax.rem(z + j + 1, nz), x], RZ.at[k, j],
                rs_send.at[k, 2 + j], rs_recv.at[k, 2 + j], zpeer(j + 1),
            )
            for j in range(nz - 1)
        ]

    def reduce_step(k, step):
        if step == 0:
            reduce_y(k).start()
        elif step == 1:
            reduce_y(k).wait_recv()

            def add_y(i, carry):
                D[k, 0, i, 1 - x] = (D[k, 0, i, 1 - x].astype(F32) + RY[k, i, 1 - x].astype(F32)).astype(BF)
                return carry

            lax.fori_loop(0, nz, add_y, 0)
            reduce_x(k).start()

            def add_own(i, carry):
                D[k, 0, i, x] = (D[k, 0, i, x].astype(F32) + RY[k, i, x].astype(F32)).astype(BF)
                return carry

            lax.fori_loop(0, nz, add_own, 0)
        elif step == 2:
            reduce_x(k).wait_recv()

            def add_x(i, carry):
                D[k, 0, i, x] = (D[k, 0, i, x].astype(F32) + RX[k, i].astype(F32)).astype(BF)
                return carry

            lax.fori_loop(0, nz, add_x, 0)
            for c in reduce_z(k):
                c.start()
        elif step == 3:
            for c in reduce_z(k):
                c.wait_recv()
            total = D[k, 0, z, x].astype(F32)
            for j in range(nz - 1):
                total = total + RZ[k, j].astype(F32)
            grad_packed[k] = total
        else:
            reduce_y(k).wait_send()
            reduce_x(k).wait_send()
            for c in reduce_z(k):
                c.wait_send()

    def sib_copy(n, src, dst):
        return remote(src, dst, sib_send.at[n], sib_recv.at[n], sib)

    send_a = sib_copy(0, A.at[low], A.at[low])
    take_a = sib_copy(0, A.at[low], A.at[other])
    send_gm = sib_copy(1, GM.at[low], GM.at[low])
    take_gm = sib_copy(1, GM.at[low], GM.at[other])
    part_r = sib_copy(2, SR, XR)
    send_c = sib_copy(3, C.at[low], C.at[low])
    take_c = sib_copy(3, C.at[low], C.at[other])
    part_g = sib_copy(4, SB, XG)
    send_gl = sib_copy(5, GL.at[low], GL.at[low])
    take_gl = sib_copy(5, GL.at[low], GL.at[other])
    part_b = sib_copy(6, SB, XB)
    part_a = sib_copy(7, SB, XA)

    stack_in = pltpu.make_async_copy(stack, Z, local_sem.at[0])
    stack_in.start()
    barrier = pltpu.get_barrier_semaphore()
    partners = [sib, ypeer, xpeer] + [zpeer(j + 1) for j in range(nz - 1)]
    for peer in partners:
        pl.semaphore_signal(barrier, inc=1, device_id=peer, device_id_type=MESH)
    for k in range(3):
        G[k, 0, z, x] = packed[k]
    pl.semaphore_wait(barrier, len(partners))
    gather_step(0, 0)

    gain_one, shift_one = vectors[0:1, :], vectors[1:2, :]
    gain_two, shift_two = vectors[2:3, :], vectors[3:4, :]
    bias_out = vectors[4:5, :]
    piece = 128
    pieces = rows // piece

    def chunk(i):
        return pl.ds(pl.multiple_of(i * piece, piece), piece)

    def first_norm(i, carry):
        unit, _ = norm_parts(tokens[chunk(i), :].astype(F32))
        A[low, chunk(i), :] = (unit * gain_one + shift_one).astype(BF)
        GM[low, chunk(i), :] = (depth[4] * cotangent[chunk(i), :].astype(F32)).astype(BF)
        return carry

    lax.fori_loop(0, pieces, first_norm, 0)
    send_a.start()
    send_gm.start()

    s0, s1 = starts[pair, 0], starts[pair, 1]
    blocks = length // BLOCK
    for block in range(blocks):
        key = block * BLOCK + lax.broadcasted_iota(jnp.int32, (2 * BLOCK, BLOCK), 0)
        query = block * BLOCK + lax.broadcasted_iota(jnp.int32, (2 * BLOCK, BLOCK), 1)
        fine = key <= query
        for s in (s0, s1):
            fine = fine | ((key >= s) & (key < s + PIECE) & (query >= s) & (query < s + PIECE))
        MB[block] = jnp.where(fine, 0.0, NEGATIVE)
    VS[...] = jnp.zeros_like(VS)
    for s in range(2):
        for h in range(heads):
            V[heads * s + h, :, HEAD_DIM:] = jnp.where(
                lax.broadcasted_iota(jnp.int32, (length, HEAD_DIM), 1) == 0, 1.0, 0.0
            ).astype(BF)

    gather_step(0, 1)
    gather_step(1, 0)

    stack_in.wait()

    def earlier(i, sums):
        grad = cotangent[chunk(i), :].astype(F32)
        mean = jnp.zeros((piece, features), F32)
        new = [sums[0] + column_sum(grad)]
        for k in range(4):
            layer = Z[k, chunk(i), :].astype(F32)
            mean = mean + depth[k] * layer
            new.append(sums[k + 1] + column_sum(layer * grad))
        AVG[chunk(i), :] = mean
        return tuple(new)

    zero_row = jnp.zeros((1, features), F32)
    sums = lax.fori_loop(0, pieces, earlier, (zero_row,) * 5)
    VS[4:5, :] = depth[4] * sums[0]
    for k in range(4):
        VS[5 + k : 6 + k, :] = sums[k + 1]

    gather_step(0, 2)
    take_a.wait_recv()

    def whole(ref, *index):
        value = ref[index]
        return value.reshape(value.shape[-4] * value.shape[-3] * value.shape[-2], value.shape[-1])

    lane = lax.broadcasted_iota(jnp.int32, (rows, 128), 1)
    front = lax.rem(lane, HEAD_DIM) < HEAD_DIM // 2

    def project(slot):
        weight = whole(G, 0, slot)
        flipped = weight[:, 512:768].T
        WO[slot * width : (slot + 1) * width, :] = flipped[64:256, :]
        for half in range(2):
            span = slice(half * rows, (half + 1) * rows)
            result = dot(A[half], weight[:, :640], 1, 0)
            turned = []
            for tile in range(3):
                part = result[:, tile * 128 : (tile + 1) * 128]
                partner = jnp.where(front, pltpu.roll(part, 96, 1), pltpu.roll(part, 32, 1))
                turned.append((part * cosine[span, :] + partner * sine[span, :]).astype(BF))
            for h in range(heads):
                n = heads * slot + h
                at = h * HEAD_DIM
                QT[n, :, span] = turned[at // 128][:, at % 128 : at % 128 + HEAD_DIM].T
                at = width + h * HEAD_DIM
                K[n, span, :] = turned[at // 128][:, at % 128 : at % 128 + HEAD_DIM]
                at = 2 * width + h * HEAD_DIM
                V[n, span, :HEAD_DIM] = result[:, at : at + HEAD_DIM].astype(BF)
                KT[n, :, span] = K[n, span, :].T

    def attend(n):
        for block in range(blocks):
            lo = block * BLOCK
            top = min(lo + 2 * BLOCK, length)
            half, at = lo // rows, lo % rows
            score = dot(K[n, 0:top, :], QT[n, :, lo : lo + BLOCK], 1, 0) * EXPONENT_SCALE
            tail = score[lo:] + MB[block, 0 : top - lo, :]
            score = jnp.concatenate([score[:lo], tail], axis=0) if lo else tail
            highest = jnp.max(score, axis=0, keepdims=True)
            power = jnp.exp2(score - highest).astype(BF)
            mixed = dot(V[n, 0:top, :], power, 0, 0)
            total = mixed[HEAD_DIM : HEAD_DIM + 1, :]
            OT[half, n, :, at : at + BLOCK] = (mixed[:HEAD_DIM, :] / total).astype(BF)
            LS[n, :, lo : lo + BLOCK] = highest + jnp.log2(total)

    project(0)

    def attend_first(h, carry):
        attend(h)

        @pl.when(h == 0)
        def _():
            gather_step(1, 1)

        return carry

    lax.fori_loop(0, heads, attend_first, 0)
    gather_step(0, 3)
    project(1)
    gather_step(2, 0)

    def attend_second(h, carry):
        attend(heads + h)

        @pl.when(h == 0)
        def _():
            gather_step(1, 2)

        @pl.when(h == 2)
        def _():
            gather_step(2, 1)

        return carry

    lax.fori_loop(0, heads, attend_second, 0)

    def mixed_rows(half):
        return OT[half].reshape(2 * width, rows)

    SR[...] = dot(mixed_rows(other), WO[...], 0, 0)
    part_r.start()
    R32[...] = dot(mixed_rows(low), WO[...], 0, 0)
    part_r.wait_recv()

    def second_norm(i, carry):
        middle = tokens[chunk(i), :].astype(F32) + R32[chunk(i), :] + XR[chunk(i), :]
        R32[chunk(i), :] = middle
        unit, _ = norm_parts(middle)
        C[low, chunk(i), :] = (unit * gain_two + shift_two).astype(BF)
        return carry

    lax.fori_loop(0, pieces, second_norm, 0)
    send_c.start()
    gather_step(1, 3)
    gather_step(2, 2)

    def hidden_bias(slot):
        return bias_in[pl.ds(lax.rem(t + 2 * slot, 4), 1), :]

    def inner(half):
        def one(slot, carry):
            pre = dot(C[half], whole(G, 1, slot), 1, 0) + hidden_bias(slot)
            act, slope = gelu_pair(pre)
            Z[2 * slot + half] = act.astype(BF)
            GP[2 * slot + half] = slope.astype(BF)
            return carry

        lax.fori_loop(0, 2, one, 0)

    inner(low)
    take_c.wait_recv()
    inner(other)
    take_gm.wait_recv()

    def both(ref):
        return ref[...].reshape(length, features)

    def put_rows(k, slot, first, value):
        D[k, slot, first : first + nz // 2] = value.astype(BF).reshape(nz // 2, 2, shard, features)

    def outer_product(k, slot, left, right):
        half_rows = features // 2
        for part in range(2):
            value = dot(left[:, part * half_rows : (part + 1) * half_rows], right, 0, 0)
            put_rows(k, slot, part * (nz // 2), value)

    def hidden_rows(ref, slot):
        return ref[2 * slot : 2 * slot + 2].reshape(length, features)

    outer_product(2, 1, both(GM), hidden_rows(Z, 1))
    reduce_step(2, 0)
    outer_product(2, 0, both(GM), hidden_rows(Z, 0))
    gather_step(2, 3)

    def back_hidden(half):
        def one(slot, carry):
            grad = dot(GM[half], whole(G, 2, slot), 1, 0) * GP[2 * slot + half].astype(F32)
            grad = grad.astype(BF)
            GP[2 * slot + half] = grad
            row = pl.ds(9 + lax.rem(t + 2 * slot, 4), 1)
            VS[row, :] = VS[row, :] + column_sum(grad.astype(F32))
            return carry

        lax.fori_loop(0, 2, one, 0)

    def back_inner(half):
        return dot(GP[half], whole(G, 1, 0), 1, 1) + dot(GP[2 + half], whole(G, 1, 1), 1, 1)

    back_hidden(other)
    SB[...] = back_inner(other).astype(BF)
    part_g.start()
    back_hidden(low)
    grad_tokens[...] = back_inner(low)
    part_g.wait_recv()

    def second_back(i, carry):
        unit, inverse = norm_parts(R32[chunk(i), :])
        grad = grad_tokens[chunk(i), :] + XG[chunk(i), :].astype(F32)
        whole_grad = depth[4] * cotangent[chunk(i), :].astype(F32) + norm_back(
            grad, gain_two, unit, inverse
        )
        grad_tokens[chunk(i), :] = whole_grad
        GL[low, chunk(i), :] = whole_grad.astype(BF)
        return (carry[0] + column_sum(grad * unit), carry[1] + column_sum(grad))

    sums = lax.fori_loop(0, pieces, second_back, (zero_row, zero_row))
    VS[2:3, :] = sums[0]
    VS[3:4, :] = sums[1]
    send_gl.start()
    reduce_step(2, 1)
    outer_product(1, 1, both(C), hidden_rows(GP, 1))
    reduce_step(1, 0)
    outer_product(1, 0, both(C), hidden_rows(GP, 0))

    def outer(half):
        return dot(Z[half], whole(G, 2, 0), 1, 1) + dot(Z[2 + half], whole(G, 2, 1), 1, 1)

    part_g.wait_send()
    SB[...] = outer(other).astype(BF)
    part_b.start()
    R32[...] = R32[...] + outer(low) + bias_out
    part_b.wait_recv()

    def finish_block(i, total):
        value = R32[chunk(i), :] + XB[chunk(i), :].astype(F32)
        layer_out[chunk(i), :] = (AVG[chunk(i), :] + depth[4] * value).astype(BF)
        return total + column_sum(value * cotangent[chunk(i), :].astype(F32))

    VS[13:14, :] = lax.fori_loop(0, pieces, finish_block, zero_row)

    take_gl.wait_recv()
    reduce_step(2, 2)
    for half in range(2):
        GOT[half] = dot(WO[...], GL[half], 1, 1).astype(BF).reshape(2 * heads, HEAD_DIM, rows)

    def grad_output(slot):
        value = sum(
            dot(OT[half, heads * slot : heads * slot + heads].reshape(width, rows), GL[half], 1, 0)
            for half in range(2)
        )
        D[0, slot, :, :, :, 3 * width :] = value.T.astype(BF).reshape(nz, 2, shard, width)

    grad_output(1)
    grad_output(0)

    def unturn(value, span):
        front_half, back_half = value[: HEAD_DIM // 2], value[HEAD_DIM // 2 :]
        cosines, sines = cosine_t[:, span], sine_t[:, span]
        return jnp.concatenate(
            [front_half * cosines + back_half * sines, back_half * cosines - front_half * sines],
            axis=0,
        )

    scale = 1.0 / math.sqrt(HEAD_DIM)

    def attend_back(slot, h):
        n = heads * slot + h

        def place(which):
            return pl.ds(pl.multiple_of(which * width + h * HEAD_DIM, HEAD_DIM), HEAD_DIM)

        GKA[...] = jnp.zeros_like(GKA)
        GVA[...] = jnp.zeros_like(GVA)
        for block in range(blocks):
            lo = block * BLOCK
            top = min(lo + 2 * BLOCK, length)
            half, at = lo // rows, lo % rows
            here = slice(at, at + BLOCK)
            grad_t = GOT[half, n, :, here]
            delta = jnp.sum(
                OT[half, n, :, here].astype(F32) * grad_t.astype(F32), axis=0, keepdims=True
            )
            score = dot(K[n, 0:top, :], QT[n, :, lo : lo + BLOCK], 1, 0) * EXPONENT_SCALE
            score = score - LS[n, :, lo : lo + BLOCK]
            tail = score[lo:] + MB[block, 0 : top - lo, :]
            score = jnp.concatenate([score[:lo], tail], axis=0) if lo else tail
            power = jnp.exp2(score)
            grad_power = dot(V[n, 0:top, :HEAD_DIM], grad_t, 1, 0)
            grad_score = (power * (grad_power - delta)).astype(BF)
            GVA[:, 0:top] += dot(grad_t, power.astype(BF), 1, 1)
            GKA[:, 0:top] += dot(QT[n, :, lo : lo + BLOCK], grad_score, 1, 1)
            grad_query = dot(KT[n, :, 0:top], grad_score, 1, 0) * scale
            GT[slot, half, place(0), here] = unturn(grad_query, slice(lo, lo + BLOCK)).astype(BF)
        for half in range(2):
            span = slice(half * rows, (half + 1) * rows)
            GT[slot, half, place(1), :] = unturn(GKA[:, span] * scale, span).astype(BF)
            GT[slot, half, place(2), :] = GVA[:, span].astype(BF)

    def grad_project(slot):
        half_rows = features // 2
        for part in range(2):
            cols = slice(part * half_rows, (part + 1) * half_rows)
            value = dot(A[0, :, cols], GT[slot, 0], 0, 1) + dot(A[1, :, cols], GT[slot, 1], 0, 1)
            first = part * (nz // 2)
            D[0, slot, first : first + nz // 2, :, :, : 3 * width] = value.astype(BF).reshape(
                nz // 2, 2, shard, 3 * width
            )

    def back_second(h, carry):
        attend_back(1, h)

        @pl.when(h == 0)
        def _():
            reduce_step(1, 1)

        @pl.when(h == 1)
        def _():
            reduce_step(2, 3)

        return carry

    lax.fori_loop(0, heads, back_second, 0)
    grad_project(1)
    reduce_step(0, 0)

    def back_first(h, carry):
        attend_back(0, h)

        @pl.when(h == 0)
        def _():
            reduce_step(1, 2)

        @pl.when(h == 2)
        def _():
            reduce_step(1, 3)

        return carry

    lax.fori_loop(0, heads, back_first, 0)
    grad_project(0)
    reduce_step(0, 1)

    def back_project(half):
        return sum(dot(GT[s, half], whole(G, 0, s)[:, : 3 * width], 0, 1) for s in range(2))

    part_b.wait_send()
    SB[...] = back_project(other).astype(BF)
    part_a.start()
    part_r.wait_send()
    SR[...] = back_project(low)
    part_a.wait_recv()

    def first_back(i, carry):
        unit, inverse = norm_parts(tokens[chunk(i), :].astype(F32))
        grad = SR[chunk(i), :] + XA[chunk(i), :].astype(F32)
        grad_tokens[chunk(i), :] = grad_tokens[chunk(i), :] + norm_back(grad, gain_one, unit, inverse)
        return (carry[0] + column_sum(grad * unit), carry[1] + column_sum(grad))

    sums = lax.fori_loop(0, pieces, first_back, (zero_row, zero_row))
    VS[0:1, :] = sums[0]
    VS[1:2, :] = sums[1]

    def vector_round(n, src, peer):
        copy = remote(src, VR.at[n], vec_send.at[n], vec_recv.at[n], peer)
        copy.start()
        return copy

    round_s = vector_round(0, VS, sib)
    reduce_step(0, 2)
    round_s.wait_recv()
    VZ[nz] = VS[...] + VR[0]
    round_y = vector_round(1, VZ.at[nz], ypeer)
    round_y.wait_recv()
    VZ[nz + 1] = VZ[nz] + VR[1]
    round_x = vector_round(2, VZ.at[nz + 1], xpeer)
    round_x.wait_recv()
    VZ[z] = VZ[nz + 1] + VR[2]
    rounds_z = [
        remote(VZ.at[z], VZ.at[z], vec_send.at[3 + j], vec_recv.at[3 + j], zpeer(j + 1))
        for j in range(nz - 1)
    ]
    for c in rounds_z:
        c.start()
    for j in range(nz - 1):
        remote(
            VZ.at[z], VZ.at[lax.rem(z + nz - 1 - j, nz)],
            vec_send.at[3 + j], vec_recv.at[3 + j], zpeer(j + 1),
        ).wait_recv()
    total = VZ[0]
    for j in range(1, nz):
        total = total + VZ[j]
    grad_vectors[...] = total
    reduce_step(0, 3)

    for k in range(3):
        gather_step(k, 4)
        reduce_step(k, 4)
    for c in [send_a, send_gm, send_c, send_gl, part_a, round_s, round_y, round_x] + rounds_z:
        c.wait_send()


def fused_device(
    tokens,
    stack,
    cotangent,
    starts,
    w_query,
    w_key,
    w_value,
    w_output,
    w_in,
    w_out,
    gain_one,
    shift_one,
    gain_two,
    shift_two,
    bias_in,
    bias_out,
    depth_weights,
):
    rows, features = tokens.shape
    shard = w_query.shape[0]
    nz = lax.axis_size("dp") // 2
    length = 2 * rows
    width = w_query.shape[1]
    heads = width // HEAD_DIM
    packed = jnp.stack(
        [jnp.concatenate([w_query, w_key, w_value, w_output.T], axis=1), w_in, w_out.T]
    )
    zero = jnp.zeros_like(gain_one)
    vectors = jnp.stack([gain_one, shift_one, gain_two, shift_two, bias_out, zero, zero, zero])
    cos_np, sin_np = rotary_tables(length)
    cosine = jnp.asarray(np.tile(cos_np, (1, 4)))
    sine = jnp.asarray(np.tile(np.concatenate([-sin_np, sin_np], axis=1), (1, 2)))
    shape = jax.ShapeDtypeStruct
    vmem = pl.BlockSpec(memory_space=pltpu.VMEM)
    smem = pl.BlockSpec(memory_space=pltpu.SMEM)
    hbm = pl.BlockSpec(memory_space=pl.ANY)
    dma = pltpu.SemaphoreType.DMA
    scratch = [
        pltpu.VMEM((3, 2, nz, 2, shard, features), BF),
        pltpu.VMEM((3, 2, nz, 2, shard, features), BF),
        pltpu.VMEM((3, nz, 2, shard, features), BF),
        pltpu.VMEM((3, nz, shard, features), BF),
        pltpu.VMEM((3, nz - 1, shard, features), BF),
        pltpu.VMEM((2, rows, features), BF),
        pltpu.VMEM((2, rows, features), BF),
        pltpu.VMEM((2, rows, features), BF),
        pltpu.VMEM((2, rows, features), BF),
        pltpu.VMEM((2 * heads, length, HEAD_DIM), BF),
        pltpu.VMEM((2 * heads, length, 2 * HEAD_DIM), BF),
        pltpu.VMEM((2 * heads, HEAD_DIM, length), BF),
        pltpu.VMEM((2 * heads, HEAD_DIM, length), BF),
        pltpu.VMEM((2, 2 * heads, HEAD_DIM, rows), BF),
        pltpu.VMEM((2 * heads, 1, length), F32),
        pltpu.VMEM((length // BLOCK, 2 * BLOCK, BLOCK), F32),
        pltpu.VMEM((4, rows, features), BF),
        pltpu.VMEM((4, rows, features), BF),
        pltpu.VMEM((2, 2 * heads, HEAD_DIM, rows), BF),
        pltpu.VMEM((2, 2, 3 * width, rows), BF),
        pltpu.VMEM((2 * width, features), BF),
        pltpu.VMEM((rows, features), F32),
        pltpu.VMEM((rows, features), F32),
        pltpu.VMEM((rows, features), F32),
        pltpu.VMEM((rows, features), F32),
        pltpu.VMEM((rows, features), BF),
        pltpu.VMEM((rows, features), BF),
        pltpu.VMEM((rows, features), BF),
        pltpu.VMEM((rows, features), BF),
        pltpu.VMEM((16, features), F32),
        pltpu.VMEM((3, 16, features), F32),
        pltpu.VMEM((nz + 2, 16, features), F32),
        pltpu.VMEM((HEAD_DIM, length), F32),
        pltpu.VMEM((HEAD_DIM, length), F32),
        dma((1,)),
        dma((3, nz + 1)),
        dma((3, nz + 1)),
        dma((3, nz + 1)),
        dma((3, nz + 1)),
        dma((8,)),
        dma((8,)),
        dma((nz + 2,)),
        dma((nz + 2,)),
    ]
    layer_out, grad_tokens, grad_packed, grad_vectors = pl.pallas_call(
        functools.partial(fused_body, nz, rows, features, shard),
        out_shape=[
            shape((rows, features), BF),
            shape((rows, features), F32),
            shape((3, shard, features), F32),
            shape((16, features), F32),
        ],
        in_specs=[vmem, vmem, hbm, vmem, vmem, vmem, smem, smem, vmem, vmem, vmem, vmem],
        out_specs=[vmem] * 4,
        scratch_shapes=scratch,
        compiler_params=pltpu.CompilerParams(
            collective_id=0, has_side_effects=True, vmem_limit_bytes=64 * 1024 * 1024
        ),
    )(
        tokens,
        cotangent,
        stack,
        packed,
        vectors,
        bias_in.reshape(4, features),
        depth_weights,
        starts,
        cosine,
        sine,
        jnp.asarray(cos_np.T.copy()),
        jnp.asarray(sin_np.T.copy()),
    )
    grad_stack = depth_weights[:4, None, None] * cotangent.astype(F32)[None]
    heads_part = grad_packed[0]
    grad_depth = jnp.sum(jnp.concatenate([grad_vectors[5:9], grad_vectors[13:14]]), axis=1)
    return (
        layer_out,
        grad_tokens,
        grad_stack,
        heads_part[:, :width],
        heads_part[:, width : 2 * width],
        heads_part[:, 2 * width : 3 * width],
        heads_part[:, 3 * width :].T,
        grad_packed[1],
        grad_packed[2].T,
        grad_vectors[0],
        grad_vectors[1],
        grad_vectors[2],
        grad_vectors[3],
        grad_vectors[9:13].reshape(-1),
        grad_vectors[4],
        grad_depth,
    )


def per_device(*arrays):
    rows, features = arrays[0].shape
    shard, width = arrays[4].shape
    dp = lax.axis_size("dp")
    fits = (
        shard % 16 == 0
        and dp % 4 == 0
        and lax.axis_size("tensor") == 4
        and arrays[3].shape[0] == 2
        and arrays[8].shape[1] == features
        and 4 * width == features
        and shard * dp == features
    )
    return fused_device(*arrays) if fits else plain_device(*arrays)


def solution(mesh):
    in_specs = (
        P(("dp", "tensor"), None),
        P(None, ("dp", "tensor"), None),
        P(("dp", "tensor"), None),
        P("dp", None),
        P("dp", "tensor"),
        P("dp", "tensor"),
        P("dp", "tensor"),
        P("tensor", "dp"),
        P("dp", "tensor"),
        P("tensor", "dp"),
        P(),
        P(),
        P(),
        P(),
        P(),
        P(),
        P(),
    )
    out_specs = (
        P(("dp", "tensor"), None),
        P(("dp", "tensor"), None),
        P(None, ("dp", "tensor"), None),
        P("dp", "tensor"),
        P("dp", "tensor"),
        P("dp", "tensor"),
        P("tensor", "dp"),
        P("dp", "tensor"),
        P("tensor", "dp"),
        P(),
        P(),
        P(),
        P(),
        P(),
        P(),
        P(),
    )
    return jax.shard_map(
        per_device, mesh=mesh, in_specs=in_specs, out_specs=out_specs, check_vma=False
    )
```

```python
import functools
import math

import jax
import jax.numpy as jnp
import numpy as np
from jax import lax
from jax.experimental import pallas as pl
from jax.experimental.pallas import tpu as pltpu
from jax.sharding import PartitionSpec as P

HEAD_DIM = 64
PIECE = 256


EPSILON = 1e-05
NEGATIVE = -1e30


def layer_norm(values, gain, shift):
    centre = values - jnp.mean(values, axis=-1, keepdims=True)
    spread = jnp.mean(centre * centre, axis=-1, keepdims=True)
    return centre * lax.rsqrt(spread + EPSILON) * gain + shift


def tables(seq_length, head_size):
    half_dim = head_size // 2
    frequency = jnp.exp(
        -jnp.log(10000.0) * jnp.arange(half_dim, dtype=jnp.float32) * 2.0 / head_size
    )
    angles = jnp.arange(seq_length, dtype=jnp.float32)[:, None] * frequency[None, :]
    return (jnp.cos(angles), jnp.sin(angles))


def rotate(values, cosine_table, sine_table):
    half_dim = values.shape[-1] // 2
    front_half = values[..., :half_dim]
    back_half = values[..., half_dim:]
    cosines = cosine_table[:, None, :]
    sine_rows = sine_table[:, None, :]
    return jnp.concatenate(
        [
            front_half * cosines - back_half * sine_rows,
            back_half * cosines + front_half * sine_rows,
        ],
        axis=-1,
    )


def allowed_mask(starts, seq_length, piece_size):
    position = jnp.arange(seq_length, dtype=jnp.int32)
    inside = (position[None, None, :] >= starts[:, :, None]) & (
        position[None, None, :] < starts[:, :, None] + piece_size
    )
    jointly = jnp.any(inside[:, :, :, None] & inside[:, :, None, :], axis=1)
    return jointly | (position[None, :, None] >= position[None, None, :])


def gelu_tanh(values):
    return jax.nn.gelu(values, approximate=True)


def right_transposed(matrix, weight):
    return lax.dot_general(
        matrix, weight, (((1,), (1,)), ((), ())), preferred_element_type=jnp.float32
    )


def left_transposed(matrix, other):
    return lax.dot_general(
        matrix, other, (((0,), (0,)), ((), ())), preferred_element_type=jnp.float32
    )


def attend_forward(query, key_rows, value_rows, allowed, score_scale):

    def one_sequence(entries):
        query_seq, key_seq, value_seq, allowed_seq = entries
        scores = (
            jnp.einsum("qhd,khd->hqk", query_seq, key_seq, preferred_element_type=jnp.float32)
            * score_scale
        )
        scores = jnp.where(allowed_seq[None], scores, NEGATIVE)
        highest = jnp.max(scores, axis=-1, keepdims=True)
        powers = jnp.exp(scores - highest)
        row_total = jnp.sum(powers, axis=-1, keepdims=True)
        attention = (powers / row_total).astype(jnp.bfloat16)
        mixed_rows = jnp.einsum(
            "hqk,khd->qhd", attention, value_seq, preferred_element_type=jnp.float32
        )
        return (mixed_rows.astype(jnp.bfloat16), highest + jnp.log(row_total))

    return lax.map(one_sequence, (query, key_rows, value_rows, allowed))


def attend_backward(query, key_rows, value_rows, grad_mixed, log_totals, allowed, score_scale):

    def one_sequence(entries):
        query_seq, key_seq, value_seq, grad_seq, log_seq, allowed_seq = entries
        scores = (
            jnp.einsum("qhd,khd->hqk", query_seq, key_seq, preferred_element_type=jnp.float32)
            * score_scale
        )
        scores = jnp.where(allowed_seq[None], scores, NEGATIVE)
        attention = jnp.exp(scores - log_seq)
        grad_value = jnp.einsum(
            "hqk,qhd->khd",
            attention.astype(jnp.bfloat16),
            grad_seq,
            preferred_element_type=jnp.float32,
        )
        grad_attention = jnp.einsum(
            "qhd,khd->hqk", grad_seq, value_seq, preferred_element_type=jnp.float32
        )
        row_delta = jnp.sum(attention * grad_attention, axis=-1, keepdims=True)
        grad_scores = (attention * (grad_attention - row_delta)).astype(jnp.bfloat16)
        grad_query = (
            jnp.einsum("hqk,khd->qhd", grad_scores, key_seq, preferred_element_type=jnp.float32)
            * score_scale
        )
        grad_key = (
            jnp.einsum("hqk,qhd->khd", grad_scores, query_seq, preferred_element_type=jnp.float32)
            * score_scale
        )
        return (grad_query, grad_key, grad_value.astype(jnp.bfloat16))

    return lax.map(one_sequence, (query, key_rows, value_rows, grad_mixed, log_totals, allowed))


def plain_device(
    tokens,
    stack,
    cotangent,
    starts,
    w_query,
    w_key,
    w_value,
    w_output,
    w_in,
    w_out,
    gain_one,
    shift_one,
    gain_two,
    shift_two,
    bias_in,
    bias_out,
    depth_weights,
):
    rows_here = tokens.shape[0]
    features = tokens.shape[1]
    groups = lax.axis_size("tensor")
    position = lax.axis_index("tensor")
    seq_count = starts.shape[0]
    seq_length = rows_here * groups // seq_count
    score_scale = 1.0 / math.sqrt(HEAD_DIM)
    local_heads = w_query.shape[1] // HEAD_DIM
    hidden = w_in.shape[1]
    cosine_table, sine_table = tables(seq_length, HEAD_DIM)
    allowed = allowed_mask(starts, seq_length, PIECE)

    def to_heads(matrix):
        return matrix.reshape(seq_count, seq_length, local_heads, HEAD_DIM)

    def from_heads(blocks):
        return blocks.reshape(seq_count * seq_length, local_heads * HEAD_DIM)

    def share_rows(local_rows):
        return lax.all_gather(local_rows, "tensor", axis=0, tiled=True)

    def share_grad(local_rows):
        return lax.all_gather(local_rows, "tensor", axis=0, tiled=True)

    def merge_rows(source, weight):
        return lax.psum_scatter(
            jnp.dot(source, weight, preferred_element_type=jnp.float32),
            "tensor",
            scatter_dimension=0,
            tiled=True,
        )

    def return_rows(pairs):
        running = jnp.zeros((lax.axis_size("tensor") * rows_here, features), jnp.float32)
        for source, weight in pairs:
            running = running + right_transposed(source, weight)
        return lax.psum_scatter(running, "tensor", scatter_dimension=0, tiled=True)

    query_w, key_w, value_w, output_w = (
        lax.all_gather(w_query, "dp", axis=0, tiled=True),
        lax.all_gather(w_key, "dp", axis=0, tiled=True),
        lax.all_gather(w_value, "dp", axis=0, tiled=True),
        lax.all_gather(w_output, "dp", axis=1, tiled=True),
    )
    inner_w, outer_w = (
        lax.all_gather(w_in, "dp", axis=0, tiled=True),
        lax.all_gather(w_out, "dp", axis=1, tiled=True),
    )
    token_rows = tokens.astype(jnp.float32)
    normed_one = layer_norm(token_rows, gain_one, shift_one).astype(jnp.bfloat16)
    normed_all = share_rows(normed_one)
    query = rotate(
        to_heads(jnp.dot(normed_all, query_w, preferred_element_type=jnp.float32)),
        cosine_table,
        sine_table,
    ).astype(jnp.bfloat16)
    key_rows = rotate(
        to_heads(jnp.dot(normed_all, key_w, preferred_element_type=jnp.float32)),
        cosine_table,
        sine_table,
    ).astype(jnp.bfloat16)
    value_rows = to_heads(jnp.dot(normed_all, value_w, preferred_element_type=jnp.float32)).astype(
        jnp.bfloat16
    )
    mixed_heads, log_totals = attend_forward(query, key_rows, value_rows, allowed, score_scale)
    mixed_flat = from_heads(mixed_heads)
    middle = token_rows + merge_rows(mixed_flat, output_w)
    normed_two = layer_norm(middle, gain_two, shift_two).astype(jnp.bfloat16)
    second_all = share_rows(normed_two)
    bias_slice = lax.dynamic_slice_in_dim(bias_in, position * hidden, hidden)
    pre_act = jnp.dot(second_all, inner_w, preferred_element_type=jnp.float32) + bias_slice
    activated = gelu_tanh(pre_act).astype(jnp.bfloat16)
    block_out = middle + merge_rows(activated, outer_w) + bias_out
    averaged = depth_weights[4] * block_out
    for layer_index in range(4):
        averaged = averaged + depth_weights[layer_index] * stack[layer_index].astype(jnp.float32)
    layer_out = averaged.astype(jnp.bfloat16)
    grad_rows = cotangent.astype(jnp.float32)
    grad_stack = jnp.stack([depth_weights[layer_index] * grad_rows for layer_index in range(4)])
    depth_terms = jnp.stack(
        [jnp.sum(stack[layer_index].astype(jnp.float32) * grad_rows) for layer_index in range(4)]
        + [jnp.sum(block_out * grad_rows)]
    )
    grad_block = depth_weights[4] * grad_rows
    grad_bias_out = jnp.sum(grad_block, axis=0)
    grad_sent = share_grad(grad_block.astype(jnp.bfloat16))
    grad_outer = left_transposed(activated, grad_sent)
    grad_act = right_transposed(grad_sent, outer_w)
    grad_pre = jax.vjp(gelu_tanh, pre_act)[1](grad_act)[0].astype(jnp.bfloat16)
    grad_bias_slice = jnp.sum(grad_pre.astype(jnp.float32), axis=0)
    bias_full = lax.dynamic_update_slice_in_dim(
        jnp.zeros((bias_in.shape[0],), jnp.float32), grad_bias_slice, position * hidden, 0
    )
    grad_inner = left_transposed(second_all, grad_pre)
    grad_norm_two = return_rows(((grad_pre, inner_w),))
    layer_two = jax.vjp(layer_norm, middle, gain_two, shift_two)[1](grad_norm_two)
    grad_middle = grad_block + layer_two[0]
    grad_attn_sent = share_grad(grad_middle.astype(jnp.bfloat16))
    grad_output_w = left_transposed(mixed_flat, grad_attn_sent)
    grad_mixed = right_transposed(grad_attn_sent, output_w).astype(jnp.bfloat16)
    grad_query, grad_key, grad_value = attend_backward(
        query, key_rows, value_rows, to_heads(grad_mixed), log_totals, allowed, score_scale
    )
    grad_query = from_heads(rotate(grad_query, cosine_table, -sine_table)).astype(jnp.bfloat16)
    grad_key = from_heads(rotate(grad_key, cosine_table, -sine_table)).astype(jnp.bfloat16)
    grad_value = from_heads(grad_value)
    grad_query_w = left_transposed(normed_all, grad_query)
    grad_key_w = left_transposed(normed_all, grad_key)
    grad_value_w = left_transposed(normed_all, grad_value)
    grad_norm_one = return_rows(((grad_query, query_w), (grad_key, key_w), (grad_value, value_w)))
    layer_one = jax.vjp(layer_norm, token_rows, gain_one, shift_one)[1](grad_norm_one)
    grad_tokens = grad_middle + layer_one[0]
    grad_w_query, grad_w_key, grad_w_value, grad_w_output, grad_w_in, grad_w_out = (
        lax.psum_scatter(grad_query_w, "dp", scatter_dimension=0, tiled=True),
        lax.psum_scatter(grad_key_w, "dp", scatter_dimension=0, tiled=True),
        lax.psum_scatter(grad_value_w, "dp", scatter_dimension=0, tiled=True),
        lax.psum_scatter(grad_output_w, "dp", scatter_dimension=1, tiled=True),
        lax.psum_scatter(grad_inner, "dp", scatter_dimension=0, tiled=True),
        lax.psum_scatter(grad_outer, "dp", scatter_dimension=1, tiled=True),
    )
    summed = lax.psum(
        (
            layer_one[1],
            layer_one[2],
            layer_two[1],
            layer_two[2],
            bias_full,
            grad_bias_out,
            depth_terms,
        ),
        ("dp", "tensor"),
    )
    return (
        layer_out,
        grad_tokens,
        grad_stack,
        grad_w_query,
        grad_w_key,
        grad_w_value,
        grad_w_output,
        grad_w_in,
        grad_w_out,
        summed[0],
        summed[1],
        summed[2],
        summed[3],
        summed[4],
        summed[5],
        summed[6],
    )


BF = jnp.bfloat16
F32 = jnp.float32
MESH = pl.DeviceIdType.MESH
BLOCK = 256
EXPONENT_SCALE = math.log2(math.e) / math.sqrt(HEAD_DIM)


PLAN = (
    (
        ("A", 0, 0, 128),
        ("A", 0, 128, 128),
        ("A", 0, 256, 128),
        ("A", 0, 384, 128),
        ("A", 0, 512, 128),
        ("B", 0, 640, 128),
        ("A", 1, 0, 128),
        ("A", 1, 128, 128),
        ("A", 1, 256, 128),
        ("B", 1, 384, 128),
        ("B", 1, 512, 128),
        ("B", 1, 640, 128),
        ("A", 2, 0, 128),
        ("A", 2, 128, 128),
        ("A", 2, 256, 128),
        ("B", 2, 384, 128),
        ("B", 2, 512, 128),
        ("B", 2, 640, 128),
    ),
    (
        ("A", 2, 0, 128),
        ("A", 2, 128, 128),
        ("A", 2, 256, 128),
        ("B", 2, 384, 128),
        ("B", 2, 512, 128),
        ("B", 2, 640, 128),
        ("A", 1, 0, 128),
        ("A", 1, 128, 128),
        ("A", 1, 256, 128),
        ("B", 1, 384, 128),
        ("B", 1, 512, 128),
        ("B", 1, 640, 128),
        ("A", 0, 0, 128),
        ("A", 0, 128, 128),
        ("A", 0, 256, 128),
        ("A", 0, 384, 128),
        ("A", 0, 512, 128),
        ("B", 0, 640, 128),
    ),
    {
        "norm": ((1, 0, 0), (1, 1, 0), (1, 2, 0), (1, 3, 0), (1, 4, 0), (1, 5, 0), (1, 6, 0), (1, 7, 0), (1, 8, 0), (1, 9, 0), (1, 10, 0), (1, 11, 0), (1, 12, 0), (1, 13, 0), (1, 15, 0), (1, 16, 0), (1, 17, 0),),
        "mask0": ((1, 5, 1), (1, 9, 1), (1, 0, 1), (1, 10, 1),),
        "mask1": ((1, 11, 1),),
        "mask2": ((1, 15, 1),),
        "mask3": ((1, 16, 1),),
        "stack0": ((1, 1, 1), (1, 17, 1),),
        "stack2": ((1, 0, 2), (1, 2, 1),),
        "proj0.0": ((1, 1, 2), (1, 3, 1), (1, 2, 2), (1, 4, 1), (1, 0, 3), (1, 3, 2), (1, 6, 1), (1, 4, 2),),
        "proj0.1": ((1, 7, 1),),
        "att0.0": ((1, 1, 3), (1, 6, 2), (1, 8, 1),),
        "att0.3": ((1, 12, 1),),
        "att1.1": ((1, 7, 2),),
        "att1.3": ((1, 2, 3), (1, 13, 1),),
        "att2.0": ((1, 8, 2),),
        "proj1.0": ((1, 12, 2), (1, 3, 3), (1, 5, 2), (1, 13, 2), (1, 4, 3),),
        "proj1.1": ((1, 9, 2), (1, 14, 0),),
        "att3.0": ((1, 5, 3),),
        "att3.3": ((1, 6, 3),),
        "att4.0": ((1, 10, 2),),
        "att5.0": ((1, 9, 3),),
        "att5.3": ((1, 7, 3), (1, 11, 2),),
        "ln2": ((1, 8, 3), (1, 10, 3), (1, 15, 2),),
        "in0": ((1, 11, 3),),
        "in2": ((1, 12, 3), (1, 16, 2),),
        "dc0": ((1, 15, 3),),
        "dc1": ((1, 13, 3), (1, 17, 2),),
        "dc2": ((0, 0, 0), (0, 1, 0), (0, 2, 0),),
        "dc3": ((1, 14, 1),),
        "bh0": ((1, 16, 3), (0, 3, 0), (0, 4, 0), (0, 5, 0), (1, 17, 3), (0, 0, 1), (1, 14, 2),),
        "bh1": ((0, 1, 1), (0, 3, 1), (0, 2, 1), (0, 4, 1), (0, 3, 2), (1, 14, 3),),
        "bh2": ((0, 3, 3), (0, 5, 1),),
        "bh3": ((0, 0, 2), (0, 4, 2),),
        "bi1": ((0, 1, 2),),
        "lnb2": ((0, 2, 2), (0, 4, 3),),
        "db0": ((0, 5, 2),),
        "db1": ((0, 0, 3),),
        "db2": ((0, 6, 0), (0, 7, 0), (0, 5, 3), (0, 8, 0),),
        "db3": ((0, 1, 3),),
        "go": ((0, 9, 0), (0, 10, 0), (0, 11, 0),),
        "dwo": ((0, 2, 3),),
        "ab0.0": ((0, 17, 0),),
        "ab0.2": ((0, 6, 1),),
        "ab1.1": ((0, 9, 1),),
        "ab1.3": ((0, 7, 1),),
        "ab2.3": ((0, 10, 1),),
        "da1": ((0, 8, 1), (0, 9, 2),),
        "ab3.0": ((0, 12, 0), (0, 13, 0), (0, 14, 0), (0, 15, 0), (0, 16, 0),),
        "ab3.2": ((0, 9, 3), (0, 11, 1),),
        "ab4.0": ((0, 10, 2),),
        "ab4.3": ((0, 17, 1),),
        "ab5.2": ((0, 6, 2), (0, 11, 2),),
        "da2": ((0, 7, 2),),
        "bp0": ((0, 12, 1), (0, 8, 2), (0, 13, 1),),
        "bp1": ((0, 17, 2),),
        "lnb1": ((0, 6, 3), (0, 14, 1), (0, 12, 2),),
        "vs0": ((0, 7, 3), (0, 13, 2),),
        "vs1": ((0, 8, 3), (0, 15, 1), (0, 14, 2),),
        "out1": ((0, 12, 3),),
        "fin": ((0, 10, 3), (0, 11, 3), (0, 13, 3), (0, 14, 3), (0, 15, 2), (0, 16, 1), (0, 17, 3),),
        "end": ((0, 15, 3), (0, 16, 2), (0, 16, 3),),
    },
)


def dot(left, right, left_axis, right_axis):
    return lax.dot_general(
        left, right, (((left_axis,), (right_axis,)), ((), ())), preferred_element_type=F32
    )


def norm_parts(values):
    centre = values - jnp.mean(values, axis=-1, keepdims=True)
    inverse = lax.rsqrt(jnp.mean(centre * centre, axis=-1, keepdims=True) + EPSILON)
    return centre * inverse, inverse


def norm_back(grad, gain, unit, inverse):
    scaled = grad * gain
    first = jnp.mean(scaled, axis=-1, keepdims=True)
    second = jnp.mean(scaled * unit, axis=-1, keepdims=True)
    return inverse * (scaled - first - unit * second)


def gelu_pair(values):
    root = math.sqrt(2.0 / math.pi)
    square = values * values
    bend = jnp.tanh(root * values * (1.0 + 0.044715 * square))
    half = 0.5 * (1.0 + bend)
    slope = half + 0.5 * root * values * (1.0 - bend * bend) * (1.0 + 3 * 0.044715 * square)
    return values * half, slope


def column_sum(values):
    return jnp.sum(values, axis=0, keepdims=True)


def rotary_tables(length):
    half = HEAD_DIM // 2
    frequency = np.exp(-np.log(10000.0) * np.arange(half) * 2.0 / HEAD_DIM)
    angles = np.arange(length)[:, None] * frequency[None, :]
    return np.cos(angles).astype(np.float32), np.sin(angles).astype(np.float32)


def fused_body(
    nz,
    rows,
    features,
    shard,
    plan,
    tokens_hbm,
    cotangent_hbm,
    stack,
    w_query,
    w_key,
    w_value,
    w_output,
    w_in,
    w_out,
    gain_one,
    shift_one,
    gain_two,
    shift_two,
    bias_in,
    bias_out,
    depth,
    starts,
    cosine_t,
    sine_t,
    layer_out,
    grad_tokens,
    grad_packed,
    grad_vectors,
    G,
    D,
    RY,
    RX,
    RZ,
    A,
    C,
    GM,
    K,
    V,
    KT,
    QT,
    OT,
    LS,
    MB,
    Z,
    GP,
    GOT,
    GT,
    WO,
    R32,
    AVG,
    SR,
    XR,
    SB,
    XG,
    VS,
    VR,
    VZ,
    GKA,
    GVA,
    tokens,
    cotangent,
    cosine,
    sine,
    BI,
    local_sem,
    ag_send,
    ag_recv,
    rs_send,
    rs_recv,
    sib_send,
    sib_recv,
    vec_send,
    vec_recv,
):
    length = 2 * rows
    heads = 3
    width = heads * HEAD_DIM
    gathers, reduces, schedule = plan
    dp = lax.axis_index("dp")
    t = lax.axis_index("tensor")
    z = dp // 2
    x = lax.rem(dp, 2)
    low = lax.rem(t, 2)
    pair = t // 2
    other = 1 - low
    sib = (dp, t + 1 - 2 * low)
    ypeer = (dp, lax.rem(t + 2, 4))
    xpeer = (dp + 1 - 2 * x, t)

    def zpeer(j):
        return (lax.rem(z + j, nz) * 2 + x, t)

    def remote(src, dst, send, recv, peer):
        return pltpu.make_async_remote_copy(
            src_ref=src, dst_ref=dst, send_sem=send, recv_sem=recv,
            device_id=peer, device_id_type=MESH,
        )

    everything = slice(None)

    def gather_copies(f, stage):
        kind, k, first, count = gathers[f]
        cols = pl.ds(first, count)
        axis = ("zxy" if kind == "A" else "yzx")[stage]
        if axis == "z":
            slot = 0 if kind == "A" else everything
            mine = G.at[k, slot, z, x, :, cols]
            sent, taken = [], []
            for j in range(nz - 1):
                sems = (ag_send.at[f, j], ag_recv.at[f, j], zpeer(j + 1))
                sent.append(lambda mine=mine, sems=sems: remote(mine, mine, *sems))
                from_z = lax.rem(z + nz - 1 - j, nz)
                taken.append(
                    lambda mine=mine, sems=sems, from_z=from_z: remote(
                        mine, G.at[k, slot, from_z, x, :, cols], *sems
                    )
                )
            return sent, taken
        if axis == "x":
            slot = 0 if kind == "A" else everything
            ref = G.at[k, slot, :, x, :, cols]
            copy = lambda: remote(ref, ref, ag_send.at[f, nz - 1], ag_recv.at[f, nz - 1], xpeer)
            return [copy], [copy]
        sems = (ag_send.at[f, nz], ag_recv.at[f, nz], ypeer)
        if kind == "A":
            copy = lambda: remote(G.at[k, 0, :, :, :, cols], G.at[k, 1, :, :, :, cols], *sems)
        else:
            copy = lambda: remote(G.at[k, 0, z, x, :, cols], G.at[k, 1, z, x, :, cols], *sems)
        return [copy], [copy]

    def gather_step(f, stage):
        if stage == 4:
            for past in range(3):
                for copy in gather_copies(f, past)[0]:
                    copy().wait_send()
            return
        if stage > 0:
            for copy in gather_copies(f, stage - 1)[1]:
                copy().wait_recv()
        if stage < 3:
            for copy in gather_copies(f, stage)[0]:
                copy().start()

    def reduce_copies(f, stage):
        kind, k, first, count = reduces[f]
        cols = pl.ds(first, count)
        axis = ("yxz" if kind == "A" else "xzy")[stage]

        def sems(n):
            return rs_send.at[f, n], rs_recv.at[f, n]

        if axis == "z":
            slot = 0 if kind == "A" else everything
            land = 0 if kind == "A" else everything
            return [
                lambda j=j: remote(
                    D.at[k, slot, lax.rem(z + j + 1, nz), x, :, cols],
                    RZ.at[k, j, land, :, cols], *sems(j), zpeer(j + 1),
                )
                for j in range(nz - 1)
            ]
        if axis == "x":
            if kind == "A":
                return [
                    lambda: remote(
                        D.at[k, 0, :, 1 - x, :, cols], RX.at[k, :, :, cols], *sems(nz - 1), xpeer
                    )
                ]
            return [
                lambda: remote(
                    D.at[k, :, :, 1 - x, :, cols], RY.at[k, :, :, :, cols], *sems(nz - 1), xpeer
                )
            ]
        if kind == "A":
            return [
                lambda side=side, n=n: remote(
                    D.at[k, 1, :, side, :, cols], RY.at[k, side, :, :, cols], *sems(nz + n), ypeer
                )
                for n, side in enumerate((1 - x, x))
            ]
        return [lambda: remote(D.at[k, 1, z, x, :, cols], RX.at[k, 0, :, cols], *sems(nz), ypeer)]

    def reduce_step(f, stage):
        kind, k, first, count = reduces[f]
        cols = pl.ds(first, count)
        if stage == 4:
            for past in range(3):
                for copy in reduce_copies(f, past):
                    copy().wait_send()
            return
        before = reduce_copies(f, stage - 1) if stage else []
        after = reduce_copies(f, stage) if stage < 3 else []

        def add(target, source):
            target[...] = (target[...].astype(F32) + source[...].astype(F32)).astype(BF)

        if kind == "A" and stage == 1:
            before[0]().wait_recv()
            add(D.at[k, 0, :, 1 - x, :, cols], RY.at[k, 1 - x, :, :, cols])
            after[0]().start()
            before[1]().wait_recv()
            add(D.at[k, 0, :, x, :, cols], RY.at[k, x, :, :, cols])
            return
        for copy in before:
            copy().wait_recv()
        if kind == "A" and stage == 2:
            add(D.at[k, 0, :, x, :, cols], RX.at[k, :, :, cols])
        elif kind == "B" and stage == 1:
            add(D.at[k, :, :, x, :, cols], RY.at[k, :, :, :, cols])
        elif kind == "B" and stage == 2:
            total = D[k, :, z, x, :, cols].astype(F32)
            for j in range(nz - 1):
                total = total + RZ[k, j, :, :, cols].astype(F32)
            D[k, 1, z, x, :, cols] = total[1].astype(BF)
            grad_packed[k, :, cols] = total[0]
        elif kind == "A" and stage == 3:
            total = D[k, 0, z, x, :, cols].astype(F32)
            for j in range(nz - 1):
                total = total + RZ[k, j, 0, :, cols].astype(F32)
            grad_packed[k, :, cols] = total
        elif kind == "B" and stage == 3:
            grad_packed[k, :, cols] = grad_packed[k, :, cols] + RX[k, 0, :, cols].astype(F32)
        for copy in after:
            copy().start()

    def tick(name):
        for gather, flow, stage in schedule.get(name, ()):
            if gather:
                gather_step(flow, stage)
            else:
                reduce_step(flow, stage)

    def tick_at(prefix, index, count, suffix=""):
        for i in range(count):
            name = prefix + str(i) + suffix
            if schedule.get(name):

                @pl.when(index == i)
                def _(name=name):
                    tick(name)

    def sib_copy(n, src, dst):
        return remote(src, dst, sib_send.at[n], sib_recv.at[n], sib)

    send_a = sib_copy(0, A.at[low], A.at[low])
    take_a = sib_copy(0, A.at[low], A.at[other])
    send_gm = sib_copy(1, GM.at[low], GM.at[low])
    take_gm = sib_copy(1, GM.at[low], GM.at[other])
    part_r = sib_copy(2, SR, XR)
    send_c = sib_copy(3, C.at[low], C.at[low])
    take_c = sib_copy(3, C.at[low], C.at[other])
    part_g = sib_copy(4, SB, XG)
    send_gl = sib_copy(5, GM.at[low], GM.at[low])
    take_gl = sib_copy(5, GM.at[low], GM.at[other])
    part_b = sib_copy(6, SB, XG)
    part_a = sib_copy(7, SB, XG)

    loads = [
        pltpu.make_async_copy(tokens_hbm, tokens, local_sem.at[0]),
        pltpu.make_async_copy(cotangent_hbm, cotangent, local_sem.at[1]),
        pltpu.make_async_copy(stack, Z, local_sem.at[2]),
    ]
    for load in loads:
        load.start()
    barrier = pltpu.get_barrier_semaphore()
    partners = [sib, ypeer, xpeer] + [zpeer(j + 1) for j in range(nz - 1)]
    for peer in partners:
        pl.semaphore_signal(barrier, inc=1, device_id=peer, device_id_type=MESH)
    G[0, 0, z, x] = jnp.concatenate(
        [w_query[...], w_key[...], w_value[...], w_output[...].T], axis=1
    )
    G[1, 0, z, x] = w_in[...]
    G[2, 0, z, x] = w_out[...].T
    pl.semaphore_wait(barrier, len(partners))
    tick("norm")

    gain_one, shift_one = gain_one[...], shift_one[...]
    gain_two, shift_two = gain_two[...], shift_two[...]
    piece = 128
    pieces = rows // piece

    def chunk(i):
        return pl.ds(pl.multiple_of(i * piece, piece), piece)

    loads[0].wait()
    loads[1].wait()

    def first_norm(i, carry):
        unit, _ = norm_parts(tokens[chunk(i), :].astype(F32))
        A[low, chunk(i), :] = (unit * gain_one + shift_one).astype(BF)
        GM[low, chunk(i), :] = (depth[4] * cotangent[chunk(i), :].astype(F32)).astype(BF)
        return carry

    lax.fori_loop(0, pieces, first_norm, 0)
    send_a.start()
    send_gm.start()
    for n in range(4):
        BI[n : n + 1, :] = bias_in[:, n * features : (n + 1) * features]
    cosine[...] = jnp.concatenate([cosine_t[...]] * 4, axis=0).T
    sine[...] = jnp.concatenate([-sine_t[...], sine_t[...]] * 2, axis=0).T

    s0, s1 = starts[pair, 0], starts[pair, 1]
    blocks = length // BLOCK
    for block in range(blocks):
        tick("mask" + str(block))
        key = block * BLOCK + lax.broadcasted_iota(jnp.int32, (2 * BLOCK, BLOCK), 0)
        query = block * BLOCK + lax.broadcasted_iota(jnp.int32, (2 * BLOCK, BLOCK), 1)
        fine = key <= query
        for s in (s0, s1):
            fine = fine | ((key >= s) & (key < s + PIECE) & (query >= s) & (query < s + PIECE))
        MB[block] = jnp.where(fine, 0.0, NEGATIVE)
    VS[...] = jnp.zeros_like(VS)
    for s in range(2):
        for h in range(heads):
            V[heads * s + h, :, HEAD_DIM:] = jnp.where(
                lax.broadcasted_iota(jnp.int32, (length, HEAD_DIM), 1) == 0, 1.0, 0.0
            ).astype(BF)

    loads[2].wait()

    def earlier(i, sums):
        tick_at("stack", i, pieces)
        grad = cotangent[chunk(i), :].astype(F32)
        mean = jnp.zeros((piece, features), F32)
        new = [sums[0] + column_sum(grad)]
        for k in range(4):
            layer = Z[k, chunk(i), :].astype(F32)
            mean = mean + depth[k] * layer
            new.append(sums[k + 1] + column_sum(layer * grad))
        AVG[chunk(i), :] = mean
        return tuple(new)

    zero_row = jnp.zeros((1, features), F32)
    sums = lax.fori_loop(0, pieces, earlier, (zero_row,) * 5)
    VS[4:5, :] = depth[4] * sums[0]
    for k in range(4):
        VS[5 + k : 6 + k, :] = sums[k + 1]

    take_a.wait_recv()

    def whole(ref, *index):
        value = ref[index]
        return value.reshape(value.shape[-4] * value.shape[-3] * value.shape[-2], value.shape[-1])

    lane = lax.broadcasted_iota(jnp.int32, (rows, 128), 1)
    front = lax.rem(lane, HEAD_DIM) < HEAD_DIM // 2

    def project(slot):
        for half in range(2):
            tick_at("proj", slot, 2, "." + str(half))
            weight = whole(G, 0, slot, everything, everything, everything, slice(0, 640))
            span = slice(half * rows, (half + 1) * rows)
            result = dot(A[half], weight, 1, 0)
            turned = []
            for tile in range(3):
                part = result[:, tile * 128 : (tile + 1) * 128]
                partner = jnp.where(front, pltpu.roll(part, 96, 1), pltpu.roll(part, 32, 1))
                turned.append((part * cosine[span, :] + partner * sine[span, :]).astype(BF))
            for h in range(heads):
                n = heads * slot + h
                at = h * HEAD_DIM
                QT[n, :, span] = turned[at // 128][:, at % 128 : at % 128 + HEAD_DIM].T
                at = width + h * HEAD_DIM
                key = turned[at // 128][:, at % 128 : at % 128 + HEAD_DIM]
                K[n, span, :] = key
                KT[n, :, span] = key.T
                at = 2 * width + h * HEAD_DIM
                V[n, span, :HEAD_DIM] = result[:, at : at + HEAD_DIM].astype(BF)

    def attend(n, carry):
        @pl.when(lax.rem(n, heads) == 0)
        def _():
            project(n // heads)

        for block in range(blocks):
            tick_at("att", n, 2 * heads, "." + str(block))
            lo = block * BLOCK
            top = min(lo + 2 * BLOCK, length)
            half, at = lo // rows, lo % rows
            score = dot(K[n, 0:top, :], QT[n, :, lo : lo + BLOCK], 1, 0) * EXPONENT_SCALE
            tail = score[lo:] + MB[block, 0 : top - lo, :]
            score = jnp.concatenate([score[:lo], tail], axis=0) if lo else tail
            highest = jnp.max(score, axis=0, keepdims=True)
            power = jnp.exp2(score - highest).astype(BF)
            mixed = dot(V[n, 0:top, :], power, 0, 0)
            total = mixed[HEAD_DIM : HEAD_DIM + 1, :]
            OT[half, n, :, at : at + BLOCK] = (mixed[:HEAD_DIM, :] / total).astype(BF)
            LS[n, :, lo : lo + BLOCK] = highest + jnp.log2(total)
        return carry

    lax.fori_loop(0, 2 * heads, attend, 0)
    tick("wo")
    for slot in range(2):
        flipped = whole(G, 0, slot, everything, everything, everything, slice(512, 768)).T
        WO[slot * width : (slot + 1) * width, :] = flipped[64:256, :]

    def mixed_rows(half):
        return OT[half].reshape(2 * width, rows)

    tick("r.other")
    SR[...] = dot(mixed_rows(other), WO[...], 0, 0)
    part_r.start()
    tick("r.low")
    R32[...] = dot(mixed_rows(low), WO[...], 0, 0)
    part_r.wait_recv()
    tick("ln2")

    def second_norm(i, carry):
        middle = tokens[chunk(i), :].astype(F32) + R32[chunk(i), :] + XR[chunk(i), :]
        R32[chunk(i), :] = middle
        unit, _ = norm_parts(middle)
        C[low, chunk(i), :] = (unit * gain_two + shift_two).astype(BF)
        return carry

    lax.fori_loop(0, pieces, second_norm, 0)
    send_c.start()
    def hidden_bias(slot):
        return BI[pl.ds(lax.rem(t + 2 * slot, 4), 1), :]

    def inner(i, carry):
        tick_at("in", i, 4)

        @pl.when(i == 2)
        def _():
            take_c.wait_recv()

        half, slot = lax.rem(low + i // 2, 2), lax.rem(i, 2)
        pre = dot(C[half], whole(G, 1, slot), 1, 0) + hidden_bias(slot)
        act, slope = gelu_pair(pre)
        Z[2 * slot + half] = act.astype(BF)
        GP[2 * slot + half] = slope.astype(BF)
        return carry

    lax.fori_loop(0, 4, inner, 0)
    take_gm.wait_recv()

    def outer_products(name, k, left, right):
        half_rows = features // 2

        def one(i, carry):
            tick_at(name, i, 4)
            slot, part = 1 - i // 2, lax.rem(i, 2)
            cols = pl.ds(pl.multiple_of(part * half_rows, 128), half_rows)
            value = dot(
                left[:, :, cols].reshape(length, half_rows),
                right[pl.ds(2 * slot, 2)].reshape(length, features),
                0,
                0,
            )
            D[k, slot, pl.ds(part * (nz // 2), nz // 2)] = value.astype(BF).reshape(
                nz // 2, 2, shard, features
            )
            return carry

        lax.fori_loop(0, 4, one, 0)

    outer_products("dc", 2, GM, Z)

    def back(i, carry):
        half = lax.rem(other + i, 2)

        def one(slot, total):
            tick_at("bh", 2 * i + slot, 4)
            grad = dot(GM[half], whole(G, 2, slot), 1, 0)
            total = total + column_sum(grad * Z[2 * slot + half].astype(F32))
            grad = (grad * GP[2 * slot + half].astype(F32)).astype(BF)
            GP[2 * slot + half] = grad
            row = pl.ds(9 + lax.rem(t + 2 * slot, 4), 1)
            VS[row, :] = VS[row, :] + column_sum(grad.astype(F32))
            return total

        carry = lax.fori_loop(0, 2, one, carry)
        tick_at("bi", i, 2)
        grad_tokens[...] = dot(GP[half], whole(G, 1, 0), 1, 1) + dot(
            GP[2 + half], whole(G, 1, 1), 1, 1
        )

        @pl.when(i == 0)
        def _():
            SB[...] = grad_tokens[...].astype(BF)
            part_g.start()

        return carry

    VS[13:14, :] = lax.fori_loop(0, 2, back, zero_row) / depth[4]
    part_g.wait_recv()
    send_gm.wait_send()
    tick("lnb2")

    def second_back(i, carry):
        middle = R32[chunk(i), :]
        unit, inverse = norm_parts(middle)
        grad = grad_tokens[chunk(i), :] + XG[chunk(i), :].astype(F32)
        coming = cotangent[chunk(i), :].astype(F32)
        whole_grad = depth[4] * coming + norm_back(grad, gain_two, unit, inverse)
        grad_tokens[chunk(i), :] = whole_grad
        GM[low, chunk(i), :] = whole_grad.astype(BF)
        return (
            carry[0] + column_sum(grad * unit),
            carry[1] + column_sum(grad),
            carry[2] + column_sum(coming * (middle + bias_out[...])),
        )

    sums = lax.fori_loop(0, pieces, second_back, (zero_row,) * 3)
    VS[2:3, :] = sums[0]
    VS[3:4, :] = sums[1]
    send_gl.start()
    VS[13:14, :] = VS[13:14, :] + sums[2]
    outer_products("db", 1, C, GP)

    take_gl.wait_recv()
    tick("go")

    def grad_mixed(half, carry):
        GOT[half] = dot(WO[...], GM[half], 1, 1).astype(BF).reshape(2 * heads, HEAD_DIM, rows)
        return carry

    lax.fori_loop(0, 2, grad_mixed, 0)
    tick("dwo")
    for slot in range(2):
        value = sum(
            dot(OT[half, heads * slot : heads * slot + heads].reshape(width, rows), GM[half], 1, 0)
            for half in range(2)
        )
        D[0, slot, :, :, :, 3 * width :] = value.T.astype(BF).reshape(nz, 2, shard, width)

    def unturn(value, span):
        front_half, back_half = value[: HEAD_DIM // 2], value[HEAD_DIM // 2 :]
        cosines, sines = cosine_t[:, span], sine_t[:, span]
        return jnp.concatenate(
            [front_half * cosines + back_half * sines, back_half * cosines - front_half * sines],
            axis=0,
        )

    scale = 1.0 / math.sqrt(HEAD_DIM)

    def attend_back(i, carry):
        slot, h = 1 - i // heads, lax.rem(i, heads)
        n = heads * slot + h

        def place(which):
            return pl.ds(pl.multiple_of(which * width + h * HEAD_DIM, HEAD_DIM), HEAD_DIM)

        GKA[...] = jnp.zeros_like(GKA)
        GVA[...] = jnp.zeros_like(GVA)
        for block in range(blocks):
            tick_at("ab", i, 2 * heads, "." + str(block))
            lo = block * BLOCK
            top = min(lo + 2 * BLOCK, length)
            half, at = lo // rows, lo % rows
            here = slice(at, at + BLOCK)
            grad_t = GOT[half, n, :, here]
            delta = jnp.sum(
                OT[half, n, :, here].astype(F32) * grad_t.astype(F32), axis=0, keepdims=True
            )
            score = dot(K[n, 0:top, :], QT[n, :, lo : lo + BLOCK], 1, 0) * EXPONENT_SCALE
            score = score - LS[n, :, lo : lo + BLOCK]
            tail = score[lo:] + MB[block, 0 : top - lo, :]
            score = jnp.concatenate([score[:lo], tail], axis=0) if lo else tail
            power = jnp.exp2(score)
            grad_power = dot(V[n, 0:top, :HEAD_DIM], grad_t, 1, 0)
            grad_score = (power * (grad_power - delta)).astype(BF)
            GVA[:, 0:top] += dot(grad_t, power.astype(BF), 1, 1)
            GKA[:, 0:top] += dot(QT[n, :, lo : lo + BLOCK], grad_score, 1, 1)
            grad_query = dot(KT[n, :, 0:top], grad_score, 1, 0) * scale
            GT[slot, half, place(0), here] = unturn(grad_query, slice(lo, lo + BLOCK)).astype(BF)
        for half in range(2):
            span = slice(half * rows, (half + 1) * rows)
            GT[slot, half, place(1), :] = unturn(GKA[:, span] * scale, span).astype(BF)
            GT[slot, half, place(2), :] = GVA[:, span].astype(BF)

        @pl.when(h == heads - 1)
        def _():
            for part in range(2):
                tick_at("da", 2 * (1 - slot) + part, 4)
                half_rows = features // 2
                cols = slice(part * half_rows, (part + 1) * half_rows)
                value = dot(A[0, :, cols], GT[slot, 0], 0, 1) + dot(
                    A[1, :, cols], GT[slot, 1], 0, 1
                )
                first = part * (nz // 2)
                D[0, slot, first : first + nz // 2, :, :, : 3 * width] = value.astype(BF).reshape(
                    nz // 2, 2, shard, 3 * width
                )

        return carry

    lax.fori_loop(0, 2 * heads, attend_back, 0)

    def back_project(half):
        return sum(dot(GT[s, half], whole(G, 0, s)[:, : 3 * width], 0, 1) for s in range(2))

    part_g.wait_send()
    part_r.wait_send()

    def back_projects(i, carry):
        tick_at("bp", i, 2)
        SR[...] = back_project(lax.rem(other + i, 2))

        @pl.when(i == 0)
        def _():
            SB[...] = SR[...].astype(BF)
            part_a.start()

        return carry

    lax.fori_loop(0, 2, back_projects, 0)
    part_a.wait_recv()
    tick("lnb1")

    def first_back(i, carry):
        unit, inverse = norm_parts(tokens[chunk(i), :].astype(F32))
        grad = SR[chunk(i), :] + XG[chunk(i), :].astype(F32)
        grad_tokens[chunk(i), :] = grad_tokens[chunk(i), :] + norm_back(grad, gain_one, unit, inverse)
        return (carry[0] + column_sum(grad * unit), carry[1] + column_sum(grad))

    sums = lax.fori_loop(0, pieces, first_back, (zero_row, zero_row))
    VS[0:1, :] = sums[0]
    VS[1:2, :] = sums[1]

    def vector_round(n, src, peer):
        copy = remote(src, VR.at[n], vec_send.at[n], vec_recv.at[n], peer)
        copy.start()
        return copy

    round_s = vector_round(0, VS, sib)
    tick("vs0")
    round_s.wait_recv()
    VZ[nz] = VS[...] + VR[0]
    round_y = vector_round(1, VZ.at[nz], ypeer)
    tick("vs1")

    part_a.wait_send()

    def outer(half):
        return dot(Z[half], whole(G, 2, 0), 1, 1) + dot(Z[2 + half], whole(G, 2, 1), 1, 1)

    def outers(i, carry):
        tick_at("out", i, 2)
        SR[...] = outer(lax.rem(other + i, 2))

        @pl.when(i == 0)
        def _():
            SB[...] = SR[...].astype(BF)
            part_b.start()

        return carry

    lax.fori_loop(0, 1, outers, 0)
    round_y.wait_recv()
    VZ[nz + 1] = VZ[nz] + VR[1]
    round_x = vector_round(2, VZ.at[nz + 1], xpeer)
    lax.fori_loop(1, 2, outers, 0)
    part_b.wait_recv()
    round_x.wait_recv()
    VZ[z] = VZ[nz + 1] + VR[2]
    rounds_z = [
        remote(VZ.at[z], VZ.at[z], vec_send.at[3 + j], vec_recv.at[3 + j], zpeer(j + 1))
        for j in range(nz - 1)
    ]
    for c in rounds_z:
        c.start()
    tick("fin")

    def finish_block(i, carry):
        value = R32[chunk(i), :] + SR[chunk(i), :] + XG[chunk(i), :].astype(F32) + bias_out[...]
        layer_out[chunk(i), :] = (AVG[chunk(i), :] + depth[4] * value).astype(BF)
        return carry

    lax.fori_loop(0, pieces, finish_block, 0)
    tick("vs2")
    for j in range(nz - 1):
        remote(
            VZ.at[z], VZ.at[lax.rem(z + nz - 1 - j, nz)],
            vec_send.at[3 + j], vec_recv.at[3 + j], zpeer(j + 1),
        ).wait_recv()
    total = VZ[0]
    for j in range(1, nz):
        total = total + VZ[j]
    grad_vectors[...] = total
    for f in range(len(gathers)):
        gather_step(f, 4)
    tick("end")
    for f in range(len(reduces)):
        reduce_step(f, 4)
    for c in [send_a, send_c, send_gl, part_b, round_s, round_y, round_x] + rounds_z:
        c.wait_send()


def spread_body(width, cotangent, packed, sums, depth, stack, wq, wk, wv, wo, wi, wu, *rest):
    for k in range(4):
        stack[k] = depth[k] * cotangent[...].astype(F32)

    @pl.when(pl.program_id(0) == 0)
    def _():
        gain_one, shift_one, gain_two, shift_two, bias_in, bias_out, grad_depth = rest
        for n, ref in enumerate((wq, wk, wv)):
            ref[...] = packed[0, :, n * width : (n + 1) * width]
        wo[...] = packed[0, :, 3 * width :].T
        wi[...] = packed[1]
        wu[...] = packed[2].T
        for n, ref in enumerate((gain_one, shift_one, gain_two, shift_two, bias_out)):
            ref[...] = sums[n : n + 1, :]
        bias_in[...] = jnp.concatenate([sums[9 + n : 10 + n, :] for n in range(4)], axis=1)
        lane = lax.broadcasted_iota(jnp.int32, (1, 5), 1)
        total = jnp.zeros((1, 5), F32)
        for n, row in enumerate((5, 6, 7, 8, 13)):
            total = jnp.where(lane == n, jnp.sum(sums[row : row + 1, :]), total)
        grad_depth[...] = total


def fused_device(
    tokens,
    stack,
    cotangent,
    starts,
    w_query,
    w_key,
    w_value,
    w_output,
    w_in,
    w_out,
    gain_one,
    shift_one,
    gain_two,
    shift_two,
    bias_in,
    bias_out,
    depth_weights,
):
    rows, features = tokens.shape
    shard = w_query.shape[0]
    nz = lax.axis_size("dp") // 2
    length = 2 * rows
    width = w_query.shape[1]
    heads = width // HEAD_DIM
    cos_np, sin_np = rotary_tables(length)
    gathers, reduces, schedule = PLAN
    shape = jax.ShapeDtypeStruct
    vmem = pl.BlockSpec(memory_space=pltpu.VMEM)
    smem = pl.BlockSpec(memory_space=pltpu.SMEM)
    hbm = pl.BlockSpec(memory_space=pl.ANY)
    dma = pltpu.SemaphoreType.DMA
    scratch = [
        pltpu.VMEM((3, 2, nz, 2, shard, features), BF),
        pltpu.VMEM((3, 2, nz, 2, shard, features), BF),
        pltpu.VMEM((3, 2, nz, shard, features), BF),
        pltpu.VMEM((3, nz, shard, features), BF),
        pltpu.VMEM((3, nz - 1, 2, shard, features), BF),
        pltpu.VMEM((2, rows, features), BF),
        pltpu.VMEM((2, rows, features), BF),
        pltpu.VMEM((2, rows, features), BF),
        pltpu.VMEM((2 * heads, length, HEAD_DIM), BF),
        pltpu.VMEM((2 * heads, length, 2 * HEAD_DIM), BF),
        pltpu.VMEM((2 * heads, HEAD_DIM, length), BF),
        pltpu.VMEM((2 * heads, HEAD_DIM, length), BF),
        pltpu.VMEM((2, 2 * heads, HEAD_DIM, rows), BF),
        pltpu.VMEM((2 * heads, 1, length), F32),
        pltpu.VMEM((length // BLOCK, 2 * BLOCK, BLOCK), F32),
        pltpu.VMEM((4, rows, features), BF),
        pltpu.VMEM((4, rows, features), BF),
        pltpu.VMEM((2, 2 * heads, HEAD_DIM, rows), BF),
        pltpu.VMEM((2, 2, 3 * width, rows), BF),
        pltpu.VMEM((2 * width, features), BF),
        pltpu.VMEM((rows, features), F32),
        pltpu.VMEM((rows, features), F32),
        pltpu.VMEM((rows, features), F32),
        pltpu.VMEM((rows, features), F32),
        pltpu.VMEM((rows, features), BF),
        pltpu.VMEM((rows, features), BF),
        pltpu.VMEM((16, features), F32),
        pltpu.VMEM((3, 16, features), F32),
        pltpu.VMEM((nz + 2, 16, features), F32),
        pltpu.VMEM((HEAD_DIM, length), F32),
        pltpu.VMEM((HEAD_DIM, length), F32),
        pltpu.VMEM((rows, features), BF),
        pltpu.VMEM((rows, features), BF),
        pltpu.VMEM((length, 2 * HEAD_DIM), F32),
        pltpu.VMEM((length, 2 * HEAD_DIM), F32),
        pltpu.VMEM((4, features), F32),
        dma((3,)),
        dma((len(gathers), nz + 1)),
        dma((len(gathers), nz + 1)),
        dma((len(reduces), nz + 2)),
        dma((len(reduces), nz + 2)),
        dma((8,)),
        dma((8,)),
        dma((nz + 2,)),
        dma((nz + 2,)),
    ]

    def row(vector):
        return vector.reshape(1, -1)

    layer_out, grad_tokens, packed, sums = pl.pallas_call(
        functools.partial(fused_body, nz, rows, features, shard, PLAN),
        out_shape=[
            shape((rows, features), BF),
            shape((rows, features), F32),
            shape((3, shard, features), F32),
            shape((16, features), F32),
        ],
        in_specs=[hbm] * 3 + [vmem] * 12 + [smem] * 2 + [vmem] * 2,
        out_specs=[vmem] * 4,
        scratch_shapes=scratch,
        compiler_params=pltpu.CompilerParams(
            collective_id=0, has_side_effects=True, vmem_limit_bytes=64 * 1024 * 1024
        ),
    )(
        tokens,
        cotangent,
        stack,
        w_query,
        w_key,
        w_value,
        w_output,
        w_in,
        w_out,
        row(gain_one),
        row(shift_one),
        row(gain_two),
        row(shift_two),
        row(bias_in),
        row(bias_out),
        depth_weights,
        starts,
        jnp.asarray(cos_np.T.copy()),
        jnp.asarray(sin_np.T.copy()),
    )

    part = rows // 4
    sizes = (
        [(shard, width)] * 3
        + [(width, shard), (shard, features), (features, shard)]
        + [(1, features)] * 4
        + [(1, 4 * features), (1, features), (1, 5)]
    )

    def fixed(size):
        return pl.BlockSpec(size, lambda i: (0,) * len(size))

    outs = pl.pallas_call(
        functools.partial(spread_body, width),
        grid=(4,),
        out_shape=[shape((4, rows, features), F32)] + [shape(size, F32) for size in sizes],
        in_specs=[
            pl.BlockSpec((part, features), lambda i: (i, 0)),
            fixed((3, shard, features)),
            fixed((16, features)),
            smem,
        ],
        out_specs=[pl.BlockSpec((4, part, features), lambda i: (0, i, 0))]
        + [fixed(size) for size in sizes],
        compiler_params=pltpu.CompilerParams(vmem_limit_bytes=32 * 1024 * 1024),
    )(cotangent, packed, sums, depth_weights)
    return (layer_out, grad_tokens, *outs[:7], *[vector.reshape(-1) for vector in outs[7:]])


def per_device(*arrays):
    rows, features = arrays[0].shape
    shard, width = arrays[4].shape
    dp = lax.axis_size("dp")
    fits = (
        shard % 16 == 0
        and dp % 4 == 0
        and lax.axis_size("tensor") == 4
        and arrays[3].shape[0] == 2
        and arrays[8].shape[1] == features
        and 4 * width == features
        and shard * dp == features
    )
    return fused_device(*arrays) if fits else plain_device(*arrays)


def solution(mesh):
    in_specs = (
        P(("dp", "tensor"), None),
        P(None, ("dp", "tensor"), None),
        P(("dp", "tensor"), None),
        P("dp", None),
        P("dp", "tensor"),
        P("dp", "tensor"),
        P("dp", "tensor"),
        P("tensor", "dp"),
        P("dp", "tensor"),
        P("tensor", "dp"),
        P(),
        P(),
        P(),
        P(),
        P(),
        P(),
        P(),
    )
    out_specs = (
        P(("dp", "tensor"), None),
        P(("dp", "tensor"), None),
        P(None, ("dp", "tensor"), None),
        P("dp", "tensor"),
        P("dp", "tensor"),
        P("dp", "tensor"),
        P("tensor", "dp"),
        P("dp", "tensor"),
        P("tensor", "dp"),
        P(),
        P(),
        P(),
        P(),
        P(),
        P(),
        P(),
    )
    return jax.shard_map(
        per_device, mesh=mesh, in_specs=in_specs, out_specs=out_specs, check_vma=False
    )
```

```python
import functools
import math

import jax
import jax.numpy as jnp
import numpy as np
from jax import lax
from jax.experimental import pallas as pl
from jax.experimental.pallas import tpu as pltpu
from jax.sharding import PartitionSpec as P

HEAD_DIM = 64
PIECE = 256


EPSILON = 1e-05
NEGATIVE = -1e30


def layer_norm(values, gain, shift):
    centre = values - jnp.mean(values, axis=-1, keepdims=True)
    spread = jnp.mean(centre * centre, axis=-1, keepdims=True)
    return centre * lax.rsqrt(spread + EPSILON) * gain + shift


def tables(seq_length, head_size):
    half_dim = head_size // 2
    frequency = jnp.exp(
        -jnp.log(10000.0) * jnp.arange(half_dim, dtype=jnp.float32) * 2.0 / head_size
    )
    angles = jnp.arange(seq_length, dtype=jnp.float32)[:, None] * frequency[None, :]
    return (jnp.cos(angles), jnp.sin(angles))


def rotate(values, cosine_table, sine_table):
    half_dim = values.shape[-1] // 2
    front_half = values[..., :half_dim]
    back_half = values[..., half_dim:]
    cosines = cosine_table[:, None, :]
    sine_rows = sine_table[:, None, :]
    return jnp.concatenate(
        [
            front_half * cosines - back_half * sine_rows,
            back_half * cosines + front_half * sine_rows,
        ],
        axis=-1,
    )


def allowed_mask(starts, seq_length, piece_size):
    position = jnp.arange(seq_length, dtype=jnp.int32)
    inside = (position[None, None, :] >= starts[:, :, None]) & (
        position[None, None, :] < starts[:, :, None] + piece_size
    )
    jointly = jnp.any(inside[:, :, :, None] & inside[:, :, None, :], axis=1)
    return jointly | (position[None, :, None] >= position[None, None, :])


def gelu_tanh(values):
    return jax.nn.gelu(values, approximate=True)


def right_transposed(matrix, weight):
    return lax.dot_general(
        matrix, weight, (((1,), (1,)), ((), ())), preferred_element_type=jnp.float32
    )


def left_transposed(matrix, other):
    return lax.dot_general(
        matrix, other, (((0,), (0,)), ((), ())), preferred_element_type=jnp.float32
    )


def attend_forward(query, key_rows, value_rows, allowed, score_scale):

    def one_sequence(entries):
        query_seq, key_seq, value_seq, allowed_seq = entries
        scores = (
            jnp.einsum("qhd,khd->hqk", query_seq, key_seq, preferred_element_type=jnp.float32)
            * score_scale
        )
        scores = jnp.where(allowed_seq[None], scores, NEGATIVE)
        highest = jnp.max(scores, axis=-1, keepdims=True)
        powers = jnp.exp(scores - highest)
        row_total = jnp.sum(powers, axis=-1, keepdims=True)
        attention = (powers / row_total).astype(jnp.bfloat16)
        mixed_rows = jnp.einsum(
            "hqk,khd->qhd", attention, value_seq, preferred_element_type=jnp.float32
        )
        return (mixed_rows.astype(jnp.bfloat16), highest + jnp.log(row_total))

    return lax.map(one_sequence, (query, key_rows, value_rows, allowed))


def attend_backward(query, key_rows, value_rows, grad_mixed, log_totals, allowed, score_scale):

    def one_sequence(entries):
        query_seq, key_seq, value_seq, grad_seq, log_seq, allowed_seq = entries
        scores = (
            jnp.einsum("qhd,khd->hqk", query_seq, key_seq, preferred_element_type=jnp.float32)
            * score_scale
        )
        scores = jnp.where(allowed_seq[None], scores, NEGATIVE)
        attention = jnp.exp(scores - log_seq)
        grad_value = jnp.einsum(
            "hqk,qhd->khd",
            attention.astype(jnp.bfloat16),
            grad_seq,
            preferred_element_type=jnp.float32,
        )
        grad_attention = jnp.einsum(
            "qhd,khd->hqk", grad_seq, value_seq, preferred_element_type=jnp.float32
        )
        row_delta = jnp.sum(attention * grad_attention, axis=-1, keepdims=True)
        grad_scores = (attention * (grad_attention - row_delta)).astype(jnp.bfloat16)
        grad_query = (
            jnp.einsum("hqk,khd->qhd", grad_scores, key_seq, preferred_element_type=jnp.float32)
            * score_scale
        )
        grad_key = (
            jnp.einsum("hqk,qhd->khd", grad_scores, query_seq, preferred_element_type=jnp.float32)
            * score_scale
        )
        return (grad_query, grad_key, grad_value.astype(jnp.bfloat16))

    return lax.map(one_sequence, (query, key_rows, value_rows, grad_mixed, log_totals, allowed))


def plain_device(
    tokens,
    stack,
    cotangent,
    starts,
    w_query,
    w_key,
    w_value,
    w_output,
    w_in,
    w_out,
    gain_one,
    shift_one,
    gain_two,
    shift_two,
    bias_in,
    bias_out,
    depth_weights,
):
    rows_here = tokens.shape[0]
    features = tokens.shape[1]
    groups = lax.axis_size("tensor")
    position = lax.axis_index("tensor")
    seq_count = starts.shape[0]
    seq_length = rows_here * groups // seq_count
    score_scale = 1.0 / math.sqrt(HEAD_DIM)
    local_heads = w_query.shape[1] // HEAD_DIM
    hidden = w_in.shape[1]
    cosine_table, sine_table = tables(seq_length, HEAD_DIM)
    allowed = allowed_mask(starts, seq_length, PIECE)

    def to_heads(matrix):
        return matrix.reshape(seq_count, seq_length, local_heads, HEAD_DIM)

    def from_heads(blocks):
        return blocks.reshape(seq_count * seq_length, local_heads * HEAD_DIM)

    def share_rows(local_rows):
        return lax.all_gather(local_rows, "tensor", axis=0, tiled=True)

    def share_grad(local_rows):
        return lax.all_gather(local_rows, "tensor", axis=0, tiled=True)

    def merge_rows(source, weight):
        return lax.psum_scatter(
            jnp.dot(source, weight, preferred_element_type=jnp.float32),
            "tensor",
            scatter_dimension=0,
            tiled=True,
        )

    def return_rows(pairs):
        running = jnp.zeros((lax.axis_size("tensor") * rows_here, features), jnp.float32)
        for source, weight in pairs:
            running = running + right_transposed(source, weight)
        return lax.psum_scatter(running, "tensor", scatter_dimension=0, tiled=True)

    query_w, key_w, value_w, output_w = (
        lax.all_gather(w_query, "dp", axis=0, tiled=True),
        lax.all_gather(w_key, "dp", axis=0, tiled=True),
        lax.all_gather(w_value, "dp", axis=0, tiled=True),
        lax.all_gather(w_output, "dp", axis=1, tiled=True),
    )
    inner_w, outer_w = (
        lax.all_gather(w_in, "dp", axis=0, tiled=True),
        lax.all_gather(w_out, "dp", axis=1, tiled=True),
    )
    token_rows = tokens.astype(jnp.float32)
    normed_one = layer_norm(token_rows, gain_one, shift_one).astype(jnp.bfloat16)
    normed_all = share_rows(normed_one)
    query = rotate(
        to_heads(jnp.dot(normed_all, query_w, preferred_element_type=jnp.float32)),
        cosine_table,
        sine_table,
    ).astype(jnp.bfloat16)
    key_rows = rotate(
        to_heads(jnp.dot(normed_all, key_w, preferred_element_type=jnp.float32)),
        cosine_table,
        sine_table,
    ).astype(jnp.bfloat16)
    value_rows = to_heads(jnp.dot(normed_all, value_w, preferred_element_type=jnp.float32)).astype(
        jnp.bfloat16
    )
    mixed_heads, log_totals = attend_forward(query, key_rows, value_rows, allowed, score_scale)
    mixed_flat = from_heads(mixed_heads)
    middle = token_rows + merge_rows(mixed_flat, output_w)
    normed_two = layer_norm(middle, gain_two, shift_two).astype(jnp.bfloat16)
    second_all = share_rows(normed_two)
    bias_slice = lax.dynamic_slice_in_dim(bias_in, position * hidden, hidden)
    pre_act = jnp.dot(second_all, inner_w, preferred_element_type=jnp.float32) + bias_slice
    activated = gelu_tanh(pre_act).astype(jnp.bfloat16)
    block_out = middle + merge_rows(activated, outer_w) + bias_out
    averaged = depth_weights[4] * block_out
    for layer_index in range(4):
        averaged = averaged + depth_weights[layer_index] * stack[layer_index].astype(jnp.float32)
    layer_out = averaged.astype(jnp.bfloat16)
    grad_rows = cotangent.astype(jnp.float32)
    grad_stack = jnp.stack([depth_weights[layer_index] * grad_rows for layer_index in range(4)])
    depth_terms = jnp.stack(
        [jnp.sum(stack[layer_index].astype(jnp.float32) * grad_rows) for layer_index in range(4)]
        + [jnp.sum(block_out * grad_rows)]
    )
    grad_block = depth_weights[4] * grad_rows
    grad_bias_out = jnp.sum(grad_block, axis=0)
    grad_sent = share_grad(grad_block.astype(jnp.bfloat16))
    grad_outer = left_transposed(activated, grad_sent)
    grad_act = right_transposed(grad_sent, outer_w)
    grad_pre = jax.vjp(gelu_tanh, pre_act)[1](grad_act)[0].astype(jnp.bfloat16)
    grad_bias_slice = jnp.sum(grad_pre.astype(jnp.float32), axis=0)
    bias_full = lax.dynamic_update_slice_in_dim(
        jnp.zeros((bias_in.shape[0],), jnp.float32), grad_bias_slice, position * hidden, 0
    )
    grad_inner = left_transposed(second_all, grad_pre)
    grad_norm_two = return_rows(((grad_pre, inner_w),))
    layer_two = jax.vjp(layer_norm, middle, gain_two, shift_two)[1](grad_norm_two)
    grad_middle = grad_block + layer_two[0]
    grad_attn_sent = share_grad(grad_middle.astype(jnp.bfloat16))
    grad_output_w = left_transposed(mixed_flat, grad_attn_sent)
    grad_mixed = right_transposed(grad_attn_sent, output_w).astype(jnp.bfloat16)
    grad_query, grad_key, grad_value = attend_backward(
        query, key_rows, value_rows, to_heads(grad_mixed), log_totals, allowed, score_scale
    )
    grad_query = from_heads(rotate(grad_query, cosine_table, -sine_table)).astype(jnp.bfloat16)
    grad_key = from_heads(rotate(grad_key, cosine_table, -sine_table)).astype(jnp.bfloat16)
    grad_value = from_heads(grad_value)
    grad_query_w = left_transposed(normed_all, grad_query)
    grad_key_w = left_transposed(normed_all, grad_key)
    grad_value_w = left_transposed(normed_all, grad_value)
    grad_norm_one = return_rows(((grad_query, query_w), (grad_key, key_w), (grad_value, value_w)))
    layer_one = jax.vjp(layer_norm, token_rows, gain_one, shift_one)[1](grad_norm_one)
    grad_tokens = grad_middle + layer_one[0]
    grad_w_query, grad_w_key, grad_w_value, grad_w_output, grad_w_in, grad_w_out = (
        lax.psum_scatter(grad_query_w, "dp", scatter_dimension=0, tiled=True),
        lax.psum_scatter(grad_key_w, "dp", scatter_dimension=0, tiled=True),
        lax.psum_scatter(grad_value_w, "dp", scatter_dimension=0, tiled=True),
        lax.psum_scatter(grad_output_w, "dp", scatter_dimension=1, tiled=True),
        lax.psum_scatter(grad_inner, "dp", scatter_dimension=0, tiled=True),
        lax.psum_scatter(grad_outer, "dp", scatter_dimension=1, tiled=True),
    )
    summed = lax.psum(
        (
            layer_one[1],
            layer_one[2],
            layer_two[1],
            layer_two[2],
            bias_full,
            grad_bias_out,
            depth_terms,
        ),
        ("dp", "tensor"),
    )
    return (
        layer_out,
        grad_tokens,
        grad_stack,
        grad_w_query,
        grad_w_key,
        grad_w_value,
        grad_w_output,
        grad_w_in,
        grad_w_out,
        summed[0],
        summed[1],
        summed[2],
        summed[3],
        summed[4],
        summed[5],
        summed[6],
    )


BF = jnp.bfloat16
F32 = jnp.float32
MESH = pl.DeviceIdType.MESH
BLOCK = 256
EXPONENT_SCALE = math.log2(math.e) / math.sqrt(HEAD_DIM)


PLAN = (
    (
        ("A", 0, 0, 128),
        ("A", 0, 128, 128),
        ("A", 0, 256, 128),
        ("A", 0, 384, 128),
        ("A", 0, 512, 128),
        ("B", 0, 640, 128),
        ("A", 1, 0, 256),
        ("B", 1, 256, 128),
        ("A", 1, 384, 128),
        ("A", 1, 512, 128),
        ("B", 1, 640, 128),
        ("A", 2, 0, 128),
        ("B", 2, 128, 128),
        ("A", 2, 256, 128),
        ("A", 2, 384, 128),
        ("B", 2, 512, 128),
        ("B", 2, 640, 128),
    ),
    (
        ("B", 2, 0, 128),
        ("B", 2, 128, 128),
        ("A", 2, 256, 256),
        ("A", 2, 512, 128),
        ("B", 2, 640, 128),
        ("B", 1, 0, 128),
        ("B", 1, 128, 128),
        ("B", 1, 256, 128),
        ("A", 1, 384, 128),
        ("A", 1, 512, 128),
        ("A", 1, 640, 128),
        ("A", 0, 0, 256),
        ("A", 0, 256, 128),
        ("A", 0, 384, 128),
        ("A", 0, 512, 128),
        ("B", 0, 640, 128),
    ),
    {
        "norm": ((1, 0, 0), (1, 5, 0), (1, 7, 0), (1, 10, 0), (1, 12, 0), (1, 15, 0), (1, 16, 0),),
        "mask0": ((1, 1, 0),),
        "mask2": ((1, 2, 0),),
        "mask3": ((1, 0, 1),),
        "stack1": ((1, 3, 0),),
        "stack3": ((1, 1, 1),),
        "proj0.0": ((1, 0, 2), (1, 4, 0), (1, 2, 1), (1, 5, 1), (1, 3, 1), (1, 1, 2), (1, 4, 1), (1, 6, 0), (1, 0, 3), (1, 2, 2), (1, 5, 2), (1, 7, 1), (1, 1, 3), (1, 3, 2), (1, 6, 1), (1, 8, 0), (1, 2, 3), (1, 5, 3), (1, 4, 2),),
        "proj0.1": ((1, 9, 0),),
        "att0.0": ((1, 7, 2),),
        "att0.2": ((1, 3, 3), (1, 10, 1),),
        "att1.0": ((1, 6, 2),),
        "att1.2": ((1, 8, 1),),
        "att2.1": ((1, 4, 3), (1, 9, 1), (1, 11, 0),),
        "att2.3": ((1, 7, 3),),
        "proj1.0": ((1, 12, 1),),
        "proj1.1": ((1, 10, 2),),
        "att3.3": ((1, 8, 2),),
        "att4.0": ((1, 11, 1), (1, 13, 0),),
        "att5.0": ((1, 6, 3), (1, 14, 0),),
        "att5.1": ((1, 10, 3), (1, 12, 2),),
        "att5.2": ((1, 9, 2),),
        "att5.3": ((1, 15, 1),),
        "ln2": ((1, 8, 3), (1, 11, 2), (1, 13, 1),),
        "in0": ((1, 14, 1), (1, 16, 1), (1, 12, 3),),
        "in1": ((1, 9, 3),),
        "in2": ((1, 15, 2),),
        "in3": ((1, 13, 2),),
        "dc1": ((1, 11, 3),),
        "dc2": ((1, 14, 2), (1, 16, 2),),
        "bh0": ((1, 15, 3), (1, 13, 3), (0, 0, 0), (0, 2, 0), (1, 16, 3),),
        "bh1": ((1, 14, 3), (0, 1, 0),),
        "bh3": ((0, 0, 1),),
        "bi1": ((0, 3, 0), (0, 4, 0),),
        "db0": ((0, 1, 1), (0, 2, 1),),
        "db2": ((0, 0, 2), (0, 8, 0),),
        "db3": ((0, 4, 1),),
        "go": ((0, 3, 1),),
        "dwo": ((0, 0, 3),),
        "ab0.0": ((0, 1, 2), (0, 5, 0), (0, 9, 0),),
        "ab0.1": ((0, 2, 2),),
        "ab1.0": ((0, 1, 3),),
        "ab1.2": ((0, 4, 2), (0, 6, 0), (0, 10, 0),),
        "ab1.3": ((0, 3, 2),),
        "ab2.2": ((0, 5, 1),),
        "ab2.3": ((0, 2, 3), (0, 4, 3), (0, 7, 0),),
        "ab3.0": ((0, 3, 3), (0, 11, 0),),
        "ab3.1": ((0, 6, 1),),
        "ab3.3": ((0, 8, 1),),
        "ab4.2": ((0, 9, 1),),
        "ab4.3": ((0, 7, 1),),
        "ab5.1": ((0, 10, 1),),
        "ab5.3": ((0, 5, 2), (0, 12, 0),),
        "da2": ((0, 15, 0),),
        "da3": ((0, 8, 2),),
        "bp1": ((0, 5, 3), (0, 9, 2),),
        "lnb1": ((0, 6, 2), (0, 7, 2), (0, 10, 2), (0, 11, 1), (0, 13, 0),),
        "vs0": ((0, 8, 3), (0, 15, 1),),
        "vs1": ((0, 6, 3), (0, 7, 3), (0, 9, 3), (0, 12, 1), (0, 14, 0),),
        "out1": ((0, 10, 3), (0, 11, 2),),
        "fin": ((0, 13, 1),),
        "vs2": ((0, 15, 2),),
        "end": ((0, 12, 2), (0, 14, 1), (0, 15, 3), (0, 13, 2), (0, 11, 3), (0, 14, 2), (0, 12, 3), (0, 13, 3), (0, 14, 3),),
    },
)


def dot(left, right, left_axis, right_axis):
    return lax.dot_general(
        left, right, (((left_axis,), (right_axis,)), ((), ())), preferred_element_type=F32
    )


def norm_parts(values):
    centre = values - jnp.mean(values, axis=-1, keepdims=True)
    inverse = lax.rsqrt(jnp.mean(centre * centre, axis=-1, keepdims=True) + EPSILON)
    return centre * inverse, inverse


def norm_back(grad, gain, unit, inverse):
    scaled = grad * gain
    first = jnp.mean(scaled, axis=-1, keepdims=True)
    second = jnp.mean(scaled * unit, axis=-1, keepdims=True)
    return inverse * (scaled - first - unit * second)


def gelu_pair(values):
    root = math.sqrt(2.0 / math.pi)
    square = values * values
    bend = jnp.tanh(root * values * (1.0 + 0.044715 * square))
    half = 0.5 * (1.0 + bend)
    slope = half + 0.5 * root * values * (1.0 - bend * bend) * (1.0 + 3 * 0.044715 * square)
    return values * half, slope


def column_sum(values):
    return jnp.sum(values, axis=0, keepdims=True)


def rotary_tables(length):
    half = HEAD_DIM // 2
    frequency = np.exp(-np.log(10000.0) * np.arange(half) * 2.0 / HEAD_DIM)
    angles = np.arange(length)[:, None] * frequency[None, :]
    return np.cos(angles).astype(np.float32), np.sin(angles).astype(np.float32)


def fused_body(
    nz,
    rows,
    features,
    shard,
    plan,
    tokens_hbm,
    cotangent_hbm,
    stack,
    w_query,
    w_key,
    w_value,
    w_output,
    w_in,
    w_out,
    gain_one,
    shift_one,
    gain_two,
    shift_two,
    bias_in,
    bias_out,
    depth,
    starts,
    cosine_t,
    sine_t,
    layer_out,
    grad_tokens,
    grad_packed,
    grad_vectors,
    G,
    D,
    RY,
    RX,
    RZ,
    A,
    C,
    GM,
    K,
    V,
    KT,
    QT,
    OT,
    LS,
    MB,
    Z,
    GP,
    GOT,
    GT,
    WO,
    R32,
    AVG,
    SR,
    XR,
    SB,
    XG,
    VS,
    VR,
    VZ,
    GKA,
    GVA,
    tokens,
    cotangent,
    cosine,
    sine,
    BI,
    local_sem,
    ag_send,
    ag_recv,
    rs_send,
    rs_recv,
    sib_send,
    sib_recv,
    vec_send,
    vec_recv,
):
    length = 2 * rows
    heads = 3
    width = heads * HEAD_DIM
    gathers, reduces, schedule = plan
    dp = lax.axis_index("dp")
    t = lax.axis_index("tensor")
    z = dp // 2
    x = lax.rem(dp, 2)
    low = lax.rem(t, 2)
    pair = t // 2
    other = 1 - low
    sib = (dp, t + 1 - 2 * low)
    ypeer = (dp, lax.rem(t + 2, 4))
    xpeer = (dp + 1 - 2 * x, t)

    def zpeer(j):
        return (lax.rem(z + j, nz) * 2 + x, t)

    def remote(src, dst, send, recv, peer):
        return pltpu.make_async_remote_copy(
            src_ref=src, dst_ref=dst, send_sem=send, recv_sem=recv,
            device_id=peer, device_id_type=MESH,
        )

    everything = slice(None)

    def gather_copies(f, stage):
        kind, k, first, count = gathers[f]
        cols = pl.ds(first, count)
        axis = ("zxy" if kind == "A" else "yzx")[stage]
        if axis == "z":
            slot = 0 if kind == "A" else everything
            mine = G.at[k, slot, z, x, :, cols]
            sent, taken = [], []
            for j in range(nz - 1):
                sems = (ag_send.at[f, j], ag_recv.at[f, j], zpeer(j + 1))
                sent.append(lambda mine=mine, sems=sems: remote(mine, mine, *sems))
                from_z = lax.rem(z + nz - 1 - j, nz)
                taken.append(
                    lambda mine=mine, sems=sems, from_z=from_z: remote(
                        mine, G.at[k, slot, from_z, x, :, cols], *sems
                    )
                )
            return sent, taken
        if axis == "x":
            slot = 0 if kind == "A" else everything
            ref = G.at[k, slot, :, x, :, cols]
            copy = lambda: remote(ref, ref, ag_send.at[f, nz - 1], ag_recv.at[f, nz - 1], xpeer)
            return [copy], [copy]
        sems = (ag_send.at[f, nz], ag_recv.at[f, nz], ypeer)
        if kind == "A":
            copy = lambda: remote(G.at[k, 0, :, :, :, cols], G.at[k, 1, :, :, :, cols], *sems)
        else:
            copy = lambda: remote(G.at[k, 0, z, x, :, cols], G.at[k, 1, z, x, :, cols], *sems)
        return [copy], [copy]

    def gather_step(f, stage):
        if stage == 4:
            for past in range(3):
                for copy in gather_copies(f, past)[0]:
                    copy().wait_send()
            return
        if stage > 0:
            for copy in gather_copies(f, stage - 1)[1]:
                copy().wait_recv()
        if stage < 3:
            for copy in gather_copies(f, stage)[0]:
                copy().start()

    def reduce_copies(f, stage):
        kind, k, first, count = reduces[f]
        cols = pl.ds(first, count)
        axis = ("yxz" if kind == "A" else "xzy")[stage]

        def sems(n):
            return rs_send.at[f, n], rs_recv.at[f, n]

        if axis == "z":
            slot = 0 if kind == "A" else everything
            land = 0 if kind == "A" else everything
            return [
                lambda j=j: remote(
                    D.at[k, slot, lax.rem(z + j + 1, nz), x, :, cols],
                    RZ.at[k, j, land, :, cols], *sems(j), zpeer(j + 1),
                )
                for j in range(nz - 1)
            ]
        if axis == "x":
            if kind == "A":
                return [
                    lambda: remote(
                        D.at[k, 0, :, 1 - x, :, cols], RX.at[k, :, :, cols], *sems(nz - 1), xpeer
                    )
                ]
            return [
                lambda: remote(
                    D.at[k, :, :, 1 - x, :, cols], RY.at[k, :, :, :, cols], *sems(nz - 1), xpeer
                )
            ]
        if kind == "A":
            return [
                lambda side=side, n=n: remote(
                    D.at[k, 1, :, side, :, cols], RY.at[k, side, :, :, cols], *sems(nz + n), ypeer
                )
                for n, side in enumerate((1 - x, x))
            ]
        return [lambda: remote(D.at[k, 1, z, x, :, cols], RX.at[k, 0, :, cols], *sems(nz), ypeer)]

    def reduce_step(f, stage):
        kind, k, first, count = reduces[f]
        cols = pl.ds(first, count)
        if stage == 4:
            for past in range(3):
                for copy in reduce_copies(f, past):
                    copy().wait_send()
            return
        before = reduce_copies(f, stage - 1) if stage else []
        after = reduce_copies(f, stage) if stage < 3 else []

        def add(target, source):
            target[...] = (target[...].astype(F32) + source[...].astype(F32)).astype(BF)

        if kind == "A" and stage == 1:
            before[0]().wait_recv()
            add(D.at[k, 0, :, 1 - x, :, cols], RY.at[k, 1 - x, :, :, cols])
            after[0]().start()
            before[1]().wait_recv()
            add(D.at[k, 0, :, x, :, cols], RY.at[k, x, :, :, cols])
            return
        for copy in before:
            copy().wait_recv()
        if kind == "A" and stage == 2:
            add(D.at[k, 0, :, x, :, cols], RX.at[k, :, :, cols])
        elif kind == "B" and stage == 1:
            add(D.at[k, :, :, x, :, cols], RY.at[k, :, :, :, cols])
        elif kind == "B" and stage == 2:
            total = D[k, :, z, x, :, cols].astype(F32)
            for j in range(nz - 1):
                total = total + RZ[k, j, :, :, cols].astype(F32)
            D[k, 1, z, x, :, cols] = total[1].astype(BF)
            grad_packed[k, :, cols] = total[0]
        elif kind == "A" and stage == 3:
            total = D[k, 0, z, x, :, cols].astype(F32)
            for j in range(nz - 1):
                total = total + RZ[k, j, 0, :, cols].astype(F32)
            grad_packed[k, :, cols] = total
        elif kind == "B" and stage == 3:
            grad_packed[k, :, cols] = grad_packed[k, :, cols] + RX[k, 0, :, cols].astype(F32)
        for copy in after:
            copy().start()

    def tick(name):
        for gather, flow, stage in schedule.get(name, ()):
            if gather:
                gather_step(flow, stage)
            else:
                reduce_step(flow, stage)

    def tick_at(prefix, index, count, suffix=""):
        for i in range(count):
            name = prefix + str(i) + suffix
            if schedule.get(name):

                @pl.when(index == i)
                def _(name=name):
                    tick(name)

    def sib_copy(n, src, dst):
        return remote(src, dst, sib_send.at[n], sib_recv.at[n], sib)

    send_a = sib_copy(0, A.at[low], A.at[low])
    take_a = sib_copy(0, A.at[low], A.at[other])
    send_gm = sib_copy(1, GM.at[low], GM.at[low])
    take_gm = sib_copy(1, GM.at[low], GM.at[other])
    part_r = sib_copy(2, SR, XR)
    send_c = sib_copy(3, C.at[low], C.at[low])
    take_c = sib_copy(3, C.at[low], C.at[other])
    part_g = sib_copy(4, SB, XG)
    send_gl = sib_copy(5, GM.at[low], GM.at[low])
    take_gl = sib_copy(5, GM.at[low], GM.at[other])
    part_b = sib_copy(6, SB, XG)
    part_a = sib_copy(7, SB, XG)

    loads = [
        pltpu.make_async_copy(tokens_hbm, tokens, local_sem.at[0]),
        pltpu.make_async_copy(cotangent_hbm, cotangent, local_sem.at[1]),
        pltpu.make_async_copy(stack, Z, local_sem.at[2]),
    ]
    for load in loads:
        load.start()
    barrier = pltpu.get_barrier_semaphore()
    partners = [sib, ypeer, xpeer] + [zpeer(j + 1) for j in range(nz - 1)]
    for peer in partners:
        pl.semaphore_signal(barrier, inc=1, device_id=peer, device_id_type=MESH)
    G[0, 0, z, x] = jnp.concatenate(
        [w_query[...], w_key[...], w_value[...], w_output[...].T], axis=1
    )
    G[1, 0, z, x] = w_in[...]
    G[2, 0, z, x] = w_out[...]
    pl.semaphore_wait(barrier, len(partners))
    tick("norm")

    gain_one, shift_one, gain_two, shift_two, bias_out = (
        ref[...].reshape(1, features)
        for ref in (gain_one, shift_one, gain_two, shift_two, bias_out)
    )
    piece = 128
    pieces = rows // piece

    def chunk(i):
        return pl.ds(pl.multiple_of(i * piece, piece), piece)

    loads[0].wait()
    loads[1].wait()

    def first_norm(i, carry):
        unit, _ = norm_parts(tokens[chunk(i), :].astype(F32))
        A[low, chunk(i), :] = (unit * gain_one + shift_one).astype(BF)
        GM[low, chunk(i), :] = (depth[4] * cotangent[chunk(i), :].astype(F32)).astype(BF)
        return carry

    lax.fori_loop(0, pieces, first_norm, 0)
    send_a.start()
    send_gm.start()
    for n in range(4):
        BI[n : n + 1, :] = bias_in[:, n * features : (n + 1) * features]
    cosine[...] = jnp.concatenate([cosine_t[...]] * 4, axis=0).T
    sine[...] = jnp.concatenate([-sine_t[...], sine_t[...]] * 2, axis=0).T

    s0, s1 = starts[pair, 0], starts[pair, 1]
    blocks = length // BLOCK
    for block in range(blocks):
        tick("mask" + str(block))
        key = block * BLOCK + lax.broadcasted_iota(jnp.int32, (2 * BLOCK, BLOCK), 0)
        query = block * BLOCK + lax.broadcasted_iota(jnp.int32, (2 * BLOCK, BLOCK), 1)
        fine = key <= query
        for s in (s0, s1):
            fine = fine | ((key >= s) & (key < s + PIECE) & (query >= s) & (query < s + PIECE))
        MB[block] = jnp.where(fine, 0.0, NEGATIVE)
    VS[...] = jnp.zeros_like(VS)
    for s in range(2):
        for h in range(heads):
            V[heads * s + h, :, HEAD_DIM:] = jnp.where(
                lax.broadcasted_iota(jnp.int32, (length, HEAD_DIM), 1) == 0, 1.0, 0.0
            ).astype(BF)

    loads[2].wait()

    def earlier(i, sums):
        tick_at("stack", i, pieces)
        grad = cotangent[chunk(i), :].astype(F32)
        mean = jnp.zeros((piece, features), F32)
        new = [sums[0] + column_sum(grad)]
        for k in range(4):
            layer = Z[k, chunk(i), :].astype(F32)
            mean = mean + depth[k] * layer
            new.append(sums[k + 1] + column_sum(layer * grad))
        AVG[chunk(i), :] = mean
        return tuple(new)

    zero_row = jnp.zeros((1, features), F32)
    sums = lax.fori_loop(0, pieces, earlier, (zero_row,) * 5)
    VS[4:5, :] = depth[4] * sums[0]
    for k in range(4):
        VS[5 + k : 6 + k, :] = sums[k + 1]

    take_a.wait_recv()

    def whole(ref, *index):
        value = ref[index]
        return value.reshape(value.shape[-4] * value.shape[-3] * value.shape[-2], value.shape[-1])

    lane = lax.broadcasted_iota(jnp.int32, (rows, 128), 1)
    front = lax.rem(lane, HEAD_DIM) < HEAD_DIM // 2

    def project(slot):
        for half in range(2):
            tick_at("proj", slot, 2, "." + str(half))
            weight = whole(G, 0, slot, everything, everything, everything, slice(0, 640))
            span = slice(half * rows, (half + 1) * rows)
            result = dot(A[half], weight, 1, 0)
            turned = []
            for tile in range(3):
                part = result[:, tile * 128 : (tile + 1) * 128]
                partner = jnp.where(front, pltpu.roll(part, 96, 1), pltpu.roll(part, 32, 1))
                turned.append((part * cosine[span, :] + partner * sine[span, :]).astype(BF))
            for h in range(heads):
                n = heads * slot + h
                at = h * HEAD_DIM
                QT[n, :, span] = turned[at // 128][:, at % 128 : at % 128 + HEAD_DIM].T
                at = width + h * HEAD_DIM
                key = turned[at // 128][:, at % 128 : at % 128 + HEAD_DIM]
                K[n, span, :] = key
                KT[n, :, span] = key.T
                at = 2 * width + h * HEAD_DIM
                V[n, span, :HEAD_DIM] = result[:, at : at + HEAD_DIM].astype(BF)

    def attend(n, carry):
        @pl.when(lax.rem(n, heads) == 0)
        def _():
            project(n // heads)

        for block in range(blocks):
            tick_at("att", n, 2 * heads, "." + str(block))
            lo = block * BLOCK
            top = min(lo + 2 * BLOCK, length)
            half, at = lo // rows, lo % rows
            score = dot(K[n, 0:top, :], QT[n, :, lo : lo + BLOCK], 1, 0) * EXPONENT_SCALE
            tail = score[lo:] + MB[block, 0 : top - lo, :]
            score = jnp.concatenate([score[:lo], tail], axis=0) if lo else tail
            highest = jnp.max(score, axis=0, keepdims=True)
            power = jnp.exp2(score - highest).astype(BF)
            mixed = dot(V[n, 0:top, :], power, 0, 0)
            total = mixed[HEAD_DIM : HEAD_DIM + 1, :]
            OT[half, n, :, at : at + BLOCK] = (mixed[:HEAD_DIM, :] / total).astype(BF)
            LS[n, :, lo : lo + BLOCK] = highest + jnp.log2(total)
        return carry

    lax.fori_loop(0, 2 * heads, attend, 0)
    tick("wo")
    for slot in range(2):
        flipped = whole(G, 0, slot, everything, everything, everything, slice(512, 768)).T
        WO[slot * width : (slot + 1) * width, :] = flipped[64:256, :]

    def mixed_rows(half):
        return OT[half].reshape(2 * width, rows)

    tick("r.other")
    SR[...] = dot(mixed_rows(other), WO[...], 0, 0)
    part_r.start()
    tick("r.low")
    R32[...] = dot(mixed_rows(low), WO[...], 0, 0)
    part_r.wait_recv()
    tick("ln2")

    def second_norm(i, carry):
        middle = tokens[chunk(i), :].astype(F32) + R32[chunk(i), :] + XR[chunk(i), :]
        R32[chunk(i), :] = middle
        unit, _ = norm_parts(middle)
        C[low, chunk(i), :] = (unit * gain_two + shift_two).astype(BF)
        return carry

    lax.fori_loop(0, pieces, second_norm, 0)
    send_c.start()
    def hidden_bias(slot):
        return BI[pl.ds(lax.rem(t + 2 * slot, 4), 1), :]

    def inner(i, carry):
        tick_at("in", i, 4)

        @pl.when(i == 2)
        def _():
            take_c.wait_recv()

        half, slot = lax.rem(low + i // 2, 2), lax.rem(i, 2)
        pre = dot(C[half], whole(G, 1, slot), 1, 0) + hidden_bias(slot)
        act, slope = gelu_pair(pre)
        Z[2 * slot + half] = act.astype(BF)
        GP[2 * slot + half] = slope.astype(BF)
        return carry

    lax.fori_loop(0, 4, inner, 0)
    take_gm.wait_recv()

    def outer_products(name, k, left, right):
        half_rows = features // 2

        def one(i, carry):
            tick_at(name, i, 4)
            slot, part = 1 - i // 2, lax.rem(i, 2)
            cols = pl.ds(pl.multiple_of(part * half_rows, 128), half_rows)
            value = dot(
                left[:, :, cols].reshape(length, half_rows),
                right[pl.ds(2 * slot, 2)].reshape(length, features),
                0,
                0,
            )
            D[k, slot, pl.ds(part * (nz // 2), nz // 2)] = value.astype(BF).reshape(
                nz // 2, 2, shard, features
            )
            return carry

        lax.fori_loop(0, 4, one, 0)

    outer_products("dc", 2, GM, Z)

    def back(i, carry):
        half = lax.rem(other + i, 2)

        def one(slot, total):
            tick_at("bh", 2 * i + slot, 4)
            grad = dot(GM[half], whole(G, 2, slot), 1, 0)
            total = total + column_sum(grad * Z[2 * slot + half].astype(F32))
            grad = (grad * GP[2 * slot + half].astype(F32)).astype(BF)
            GP[2 * slot + half] = grad
            row = pl.ds(9 + lax.rem(t + 2 * slot, 4), 1)
            VS[row, :] = VS[row, :] + column_sum(grad.astype(F32))
            return total

        carry = lax.fori_loop(0, 2, one, carry)
        tick_at("bi", i, 2)
        grad_tokens[...] = dot(GP[half], whole(G, 1, 0), 1, 1) + dot(
            GP[2 + half], whole(G, 1, 1), 1, 1
        )

        @pl.when(i == 0)
        def _():
            SB[...] = grad_tokens[...].astype(BF)
            part_g.start()

        return carry

    VS[13:14, :] = lax.fori_loop(0, 2, back, zero_row) / depth[4]
    part_g.wait_recv()
    send_gm.wait_send()
    tick("lnb2")

    def second_back(i, carry):
        middle = R32[chunk(i), :]
        unit, inverse = norm_parts(middle)
        grad = grad_tokens[chunk(i), :] + XG[chunk(i), :].astype(F32)
        coming = cotangent[chunk(i), :].astype(F32)
        whole_grad = depth[4] * coming + norm_back(grad, gain_two, unit, inverse)
        grad_tokens[chunk(i), :] = whole_grad
        GM[low, chunk(i), :] = whole_grad.astype(BF)
        return (
            carry[0] + column_sum(grad * unit),
            carry[1] + column_sum(grad),
            carry[2] + column_sum(coming * (middle + bias_out)),
        )

    sums = lax.fori_loop(0, pieces, second_back, (zero_row,) * 3)
    VS[2:3, :] = sums[0]
    VS[3:4, :] = sums[1]
    send_gl.start()
    VS[13:14, :] = VS[13:14, :] + sums[2]
    outer_products("db", 1, C, GP)

    take_gl.wait_recv()
    tick("go")

    def grad_mixed(half, carry):
        GOT[half] = dot(WO[...], GM[half], 1, 1).astype(BF).reshape(2 * heads, HEAD_DIM, rows)
        return carry

    lax.fori_loop(0, 2, grad_mixed, 0)
    tick("dwo")
    for slot in range(2):
        value = sum(
            dot(OT[half, heads * slot : heads * slot + heads].reshape(width, rows), GM[half], 1, 0)
            for half in range(2)
        )
        D[0, slot, :, :, :, 3 * width :] = value.T.astype(BF).reshape(nz, 2, shard, width)

    def unturn(value, span):
        front_half, back_half = value[: HEAD_DIM // 2], value[HEAD_DIM // 2 :]
        cosines, sines = cosine_t[:, span], sine_t[:, span]
        return jnp.concatenate(
            [front_half * cosines + back_half * sines, back_half * cosines - front_half * sines],
            axis=0,
        )

    scale = 1.0 / math.sqrt(HEAD_DIM)

    def attend_back(i, carry):
        slot, h = 1 - i // heads, lax.rem(i, heads)
        n = heads * slot + h

        def place(which):
            return pl.ds(pl.multiple_of(which * width + h * HEAD_DIM, HEAD_DIM), HEAD_DIM)

        GKA[...] = jnp.zeros_like(GKA)
        GVA[...] = jnp.zeros_like(GVA)
        for block in range(blocks):
            tick_at("ab", i, 2 * heads, "." + str(block))
            lo = block * BLOCK
            top = min(lo + 2 * BLOCK, length)
            half, at = lo // rows, lo % rows
            here = slice(at, at + BLOCK)
            grad_t = GOT[half, n, :, here]
            delta = jnp.sum(
                OT[half, n, :, here].astype(F32) * grad_t.astype(F32), axis=0, keepdims=True
            )
            score = dot(K[n, 0:top, :], QT[n, :, lo : lo + BLOCK], 1, 0) * EXPONENT_SCALE
            score = score - LS[n, :, lo : lo + BLOCK]
            tail = score[lo:] + MB[block, 0 : top - lo, :]
            score = jnp.concatenate([score[:lo], tail], axis=0) if lo else tail
            power = jnp.exp2(score)
            grad_power = dot(V[n, 0:top, :HEAD_DIM], grad_t, 1, 0)
            grad_score = (power * (grad_power - delta)).astype(BF)
            GVA[:, 0:top] += dot(grad_t, power.astype(BF), 1, 1)
            GKA[:, 0:top] += dot(QT[n, :, lo : lo + BLOCK], grad_score, 1, 1)
            grad_query = dot(KT[n, :, 0:top], grad_score, 1, 0) * scale
            GT[slot, half, place(0), here] = unturn(grad_query, slice(lo, lo + BLOCK)).astype(BF)
        for half in range(2):
            span = slice(half * rows, (half + 1) * rows)
            GT[slot, half, place(1), :] = unturn(GKA[:, span] * scale, span).astype(BF)
            GT[slot, half, place(2), :] = GVA[:, span].astype(BF)

        @pl.when(h == heads - 1)
        def _():
            for part in range(2):
                tick_at("da", 2 * (1 - slot) + part, 4)
                half_rows = features // 2
                cols = slice(part * half_rows, (part + 1) * half_rows)
                value = dot(A[0, :, cols], GT[slot, 0], 0, 1) + dot(
                    A[1, :, cols], GT[slot, 1], 0, 1
                )
                first = part * (nz // 2)
                D[0, slot, first : first + nz // 2, :, :, : 3 * width] = value.astype(BF).reshape(
                    nz // 2, 2, shard, 3 * width
                )

        return carry

    lax.fori_loop(0, 2 * heads, attend_back, 0)

    def back_project(half):
        return sum(dot(GT[s, half], whole(G, 0, s)[:, : 3 * width], 0, 1) for s in range(2))

    part_g.wait_send()
    part_r.wait_send()

    def back_projects(i, carry):
        tick_at("bp", i, 2)
        SR[...] = back_project(lax.rem(other + i, 2))

        @pl.when(i == 0)
        def _():
            SB[...] = SR[...].astype(BF)
            part_a.start()

        return carry

    lax.fori_loop(0, 2, back_projects, 0)
    part_a.wait_recv()
    tick("lnb1")

    def first_back(i, carry):
        unit, inverse = norm_parts(tokens[chunk(i), :].astype(F32))
        grad = SR[chunk(i), :] + XG[chunk(i), :].astype(F32)
        grad_tokens[chunk(i), :] = grad_tokens[chunk(i), :] + norm_back(grad, gain_one, unit, inverse)
        return (carry[0] + column_sum(grad * unit), carry[1] + column_sum(grad))

    sums = lax.fori_loop(0, pieces, first_back, (zero_row, zero_row))
    VS[0:1, :] = sums[0]
    VS[1:2, :] = sums[1]

    def vector_round(n, src, peer):
        copy = remote(src, VR.at[n], vec_send.at[n], vec_recv.at[n], peer)
        copy.start()
        return copy

    round_s = vector_round(0, VS, sib)
    tick("vs0")
    round_s.wait_recv()
    VZ[nz] = VS[...] + VR[0]
    round_y = vector_round(1, VZ.at[nz], ypeer)
    tick("vs1")

    part_a.wait_send()

    def outer(half):
        return dot(Z[half], whole(G, 2, 0), 1, 1) + dot(Z[2 + half], whole(G, 2, 1), 1, 1)

    def outers(i, carry):
        tick_at("out", i, 2)
        SR[...] = outer(lax.rem(other + i, 2))

        @pl.when(i == 0)
        def _():
            SB[...] = SR[...].astype(BF)
            part_b.start()

        return carry

    lax.fori_loop(0, 1, outers, 0)
    round_y.wait_recv()
    VZ[nz + 1] = VZ[nz] + VR[1]
    round_x = vector_round(2, VZ.at[nz + 1], xpeer)
    lax.fori_loop(1, 2, outers, 0)
    part_b.wait_recv()
    round_x.wait_recv()
    VZ[z] = VZ[nz + 1] + VR[2]
    rounds_z = [
        remote(VZ.at[z], VZ.at[z], vec_send.at[3 + j], vec_recv.at[3 + j], zpeer(j + 1))
        for j in range(nz - 1)
    ]
    for c in rounds_z:
        c.start()
    tick("fin")

    def finish_block(i, carry):
        value = R32[chunk(i), :] + SR[chunk(i), :] + XG[chunk(i), :].astype(F32) + bias_out
        layer_out[chunk(i), :] = (AVG[chunk(i), :] + depth[4] * value).astype(BF)
        return carry

    lax.fori_loop(0, pieces, finish_block, 0)
    tick("vs2")
    for j in range(nz - 1):
        remote(
            VZ.at[z], VZ.at[lax.rem(z + nz - 1 - j, nz)],
            vec_send.at[3 + j], vec_recv.at[3 + j], zpeer(j + 1),
        ).wait_recv()
    total = VZ[0]
    for j in range(1, nz):
        total = total + VZ[j]
    grad_vectors[...] = total
    for f in range(len(gathers)):
        gather_step(f, 4)
    tick("end")
    for f in range(len(reduces)):
        reduce_step(f, 4)
    for c in [send_a, send_c, send_gl, part_b, round_s, round_y, round_x] + rounds_z:
        c.wait_send()


def spread_body(width, cotangent, average, tokens, packed, sums, depth, *outs):
    layer_out, grad_tokens, stack, wq, wk, wv, wo, wi, wu = outs[:9]
    gain_one, shift_one, gain_two, shift_two, bias_in, bias_out, grad_depth = outs[9:]
    layer_out[...] = average[...]
    grad_tokens[...] = tokens[...]
    for k in range(4):
        stack[k] = depth[k] * cotangent[...].astype(F32)

    @pl.when(pl.program_id(0) == 0)
    def _():
        for n, ref in enumerate((wq, wk, wv)):
            ref[...] = packed[0, :, n * width : (n + 1) * width]
        wo[...] = packed[0, :, 3 * width :].T
        wi[...] = packed[1]
        wu[...] = packed[2]
        for n, ref in enumerate((gain_one, shift_one, gain_two, shift_two, bias_out)):
            ref[...] = sums[n, :]
        bias_in[...] = jnp.concatenate([sums[9 + n : 10 + n, :] for n in range(4)], axis=1)
        lane = lax.broadcasted_iota(jnp.int32, (1, 5), 1)
        total = jnp.zeros((1, 5), F32)
        for n, row in enumerate((5, 6, 7, 8, 13)):
            total = jnp.where(lane == n, jnp.sum(sums[row : row + 1, :]), total)
        grad_depth[...] = total


def fused_device(
    tokens,
    stack,
    cotangent,
    starts,
    w_query,
    w_key,
    w_value,
    w_output,
    w_in,
    w_out,
    gain_one,
    shift_one,
    gain_two,
    shift_two,
    bias_in,
    bias_out,
    depth_weights,
):
    rows, features = tokens.shape
    shard = w_query.shape[0]
    nz = lax.axis_size("dp") // 2
    length = 2 * rows
    width = w_query.shape[1]
    heads = width // HEAD_DIM
    cos_np, sin_np = rotary_tables(length)
    gathers, reduces, schedule = PLAN
    shape = jax.ShapeDtypeStruct
    vmem = pl.BlockSpec(memory_space=pltpu.VMEM)
    smem = pl.BlockSpec(memory_space=pltpu.SMEM)
    hbm = pl.BlockSpec(memory_space=pl.ANY)
    dma = pltpu.SemaphoreType.DMA
    scratch = [
        pltpu.VMEM((3, 2, nz, 2, shard, features), BF),
        pltpu.VMEM((3, 2, nz, 2, shard, features), BF),
        pltpu.VMEM((3, 2, nz, shard, features), BF),
        pltpu.VMEM((3, nz, shard, features), BF),
        pltpu.VMEM((3, nz - 1, 2, shard, features), BF),
        pltpu.VMEM((2, rows, features), BF),
        pltpu.VMEM((2, rows, features), BF),
        pltpu.VMEM((2, rows, features), BF),
        pltpu.VMEM((2 * heads, length, HEAD_DIM), BF),
        pltpu.VMEM((2 * heads, length, 2 * HEAD_DIM), BF),
        pltpu.VMEM((2 * heads, HEAD_DIM, length), BF),
        pltpu.VMEM((2 * heads, HEAD_DIM, length), BF),
        pltpu.VMEM((2, 2 * heads, HEAD_DIM, rows), BF),
        pltpu.VMEM((2 * heads, 1, length), F32),
        pltpu.VMEM((length // BLOCK, 2 * BLOCK, BLOCK), F32),
        pltpu.VMEM((4, rows, features), BF),
        pltpu.VMEM((4, rows, features), BF),
        pltpu.VMEM((2, 2 * heads, HEAD_DIM, rows), BF),
        pltpu.VMEM((2, 2, 3 * width, rows), BF),
        pltpu.VMEM((2 * width, features), BF),
        pltpu.VMEM((rows, features), F32),
        pltpu.VMEM((rows, features), F32),
        pltpu.VMEM((rows, features), F32),
        pltpu.VMEM((rows, features), F32),
        pltpu.VMEM((rows, features), BF),
        pltpu.VMEM((rows, features), BF),
        pltpu.VMEM((16, features), F32),
        pltpu.VMEM((3, 16, features), F32),
        pltpu.VMEM((nz + 2, 16, features), F32),
        pltpu.VMEM((HEAD_DIM, length), F32),
        pltpu.VMEM((HEAD_DIM, length), F32),
        pltpu.VMEM((rows, features), BF),
        pltpu.VMEM((rows, features), BF),
        pltpu.VMEM((length, 2 * HEAD_DIM), F32),
        pltpu.VMEM((length, 2 * HEAD_DIM), F32),
        pltpu.VMEM((4, features), F32),
        dma((3,)),
        dma((len(gathers), nz + 1)),
        dma((len(gathers), nz + 1)),
        dma((len(reduces), nz + 2)),
        dma((len(reduces), nz + 2)),
        dma((8,)),
        dma((8,)),
        dma((nz + 2,)),
        dma((nz + 2,)),
    ]

    layer_out, grad_tokens, packed, sums = pl.pallas_call(
        functools.partial(fused_body, nz, rows, features, shard, PLAN),
        out_shape=[
            shape((rows, features), BF),
            shape((rows, features), F32),
            shape((3, shard, features), F32),
            shape((16, features), F32),
        ],
        in_specs=[hbm] * 3 + [vmem] * 12 + [smem] * 2 + [vmem] * 2,
        out_specs=[vmem] * 4,
        scratch_shapes=scratch,
        compiler_params=pltpu.CompilerParams(
            collective_id=0, has_side_effects=True, vmem_limit_bytes=64 * 1024 * 1024
        ),
    )(
        tokens,
        cotangent,
        stack,
        w_query,
        w_key,
        w_value,
        w_output,
        w_in,
        w_out.T,
        gain_one,
        shift_one,
        gain_two,
        shift_two,
        bias_in.reshape(1, -1),
        bias_out,
        depth_weights,
        starts,
        jnp.asarray(cos_np.T.copy()),
        jnp.asarray(sin_np.T.copy()),
    )

    steps = 4
    part = rows // steps
    sizes = (
        [(shard, width)] * 3
        + [(width, shard), (shard, features), (shard, features)]
        + [(features,)] * 4
        + [(1, 4 * features), (features,), (1, 5)]
    )

    def fixed(size):
        return pl.BlockSpec(size, lambda i: (0,) * len(size))

    by_rows = pl.BlockSpec((part, features), lambda i: (i, 0))
    outs = pl.pallas_call(
        functools.partial(spread_body, width),
        grid=(steps,),
        out_shape=[
            shape((rows, features), BF),
            shape((rows, features), F32),
            shape((4, rows, features), F32),
        ]
        + [shape(size, F32) for size in sizes],
        in_specs=[by_rows] * 3 + [fixed((3, shard, features)), fixed((16, features)), smem],
        out_specs=[by_rows] * 2
        + [pl.BlockSpec((4, part, features), lambda i: (0, i, 0))]
        + [fixed(size) for size in sizes],
        compiler_params=pltpu.CompilerParams(vmem_limit_bytes=60 * 1024 * 1024),
    )(cotangent, layer_out, grad_tokens, packed, sums, depth_weights)
    return (*outs[:8], outs[8].T, *outs[9:13], outs[13].reshape(-1), outs[14], outs[15].reshape(-1))


def per_device(*arrays):
    rows, features = arrays[0].shape
    shard, width = arrays[4].shape
    dp = lax.axis_size("dp")
    fits = (
        shard % 16 == 0
        and dp % 4 == 0
        and lax.axis_size("tensor") == 4
        and arrays[3].shape[0] == 2
        and arrays[8].shape[1] == features
        and 4 * width == features
        and shard * dp == features
    )
    return fused_device(*arrays) if fits else plain_device(*arrays)


def solution(mesh):
    in_specs = (
        P(("dp", "tensor"), None),
        P(None, ("dp", "tensor"), None),
        P(("dp", "tensor"), None),
        P("dp", None),
        P("dp", "tensor"),
        P("dp", "tensor"),
        P("dp", "tensor"),
        P("tensor", "dp"),
        P("dp", "tensor"),
        P("tensor", "dp"),
        P(),
        P(),
        P(),
        P(),
        P(),
        P(),
        P(),
    )
    out_specs = (
        P(("dp", "tensor"), None),
        P(("dp", "tensor"), None),
        P(None, ("dp", "tensor"), None),
        P("dp", "tensor"),
        P("dp", "tensor"),
        P("dp", "tensor"),
        P("tensor", "dp"),
        P("dp", "tensor"),
        P("tensor", "dp"),
        P(),
        P(),
        P(),
        P(),
        P(),
        P(),
        P(),
    )
    return jax.shard_map(
        per_device, mesh=mesh, in_specs=in_specs, out_specs=out_specs, check_vma=False
    )
```

```python
import functools
import math

import jax
import jax.numpy as jnp
import numpy as np
from jax import lax
from jax.experimental import pallas as pl
from jax.experimental.pallas import tpu as pltpu
from jax.sharding import PartitionSpec as P

HEAD_DIM = 64
PIECE = 256


EPSILON = 1e-05
NEGATIVE = -1e30


def layer_norm(values, gain, shift):
    centre = values - jnp.mean(values, axis=-1, keepdims=True)
    spread = jnp.mean(centre * centre, axis=-1, keepdims=True)
    return centre * lax.rsqrt(spread + EPSILON) * gain + shift


def tables(seq_length, head_size):
    half_dim = head_size // 2
    frequency = jnp.exp(
        -jnp.log(10000.0) * jnp.arange(half_dim, dtype=jnp.float32) * 2.0 / head_size
    )
    angles = jnp.arange(seq_length, dtype=jnp.float32)[:, None] * frequency[None, :]
    return (jnp.cos(angles), jnp.sin(angles))


def rotate(values, cosine_table, sine_table):
    half_dim = values.shape[-1] // 2
    front_half = values[..., :half_dim]
    back_half = values[..., half_dim:]
    cosines = cosine_table[:, None, :]
    sine_rows = sine_table[:, None, :]
    return jnp.concatenate(
        [
            front_half * cosines - back_half * sine_rows,
            back_half * cosines + front_half * sine_rows,
        ],
        axis=-1,
    )


def allowed_mask(starts, seq_length, piece_size):
    position = jnp.arange(seq_length, dtype=jnp.int32)
    inside = (position[None, None, :] >= starts[:, :, None]) & (
        position[None, None, :] < starts[:, :, None] + piece_size
    )
    jointly = jnp.any(inside[:, :, :, None] & inside[:, :, None, :], axis=1)
    return jointly | (position[None, :, None] >= position[None, None, :])


def gelu_tanh(values):
    return jax.nn.gelu(values, approximate=True)


def right_transposed(matrix, weight):
    return lax.dot_general(
        matrix, weight, (((1,), (1,)), ((), ())), preferred_element_type=jnp.float32
    )


def left_transposed(matrix, other):
    return lax.dot_general(
        matrix, other, (((0,), (0,)), ((), ())), preferred_element_type=jnp.float32
    )


def attend_forward(query, key_rows, value_rows, allowed, score_scale):

    def one_sequence(entries):
        query_seq, key_seq, value_seq, allowed_seq = entries
        scores = (
            jnp.einsum("qhd,khd->hqk", query_seq, key_seq, preferred_element_type=jnp.float32)
            * score_scale
        )
        scores = jnp.where(allowed_seq[None], scores, NEGATIVE)
        highest = jnp.max(scores, axis=-1, keepdims=True)
        powers = jnp.exp(scores - highest)
        row_total = jnp.sum(powers, axis=-1, keepdims=True)
        attention = (powers / row_total).astype(jnp.bfloat16)
        mixed_rows = jnp.einsum(
            "hqk,khd->qhd", attention, value_seq, preferred_element_type=jnp.float32
        )
        return (mixed_rows.astype(jnp.bfloat16), highest + jnp.log(row_total))

    return lax.map(one_sequence, (query, key_rows, value_rows, allowed))


def attend_backward(query, key_rows, value_rows, grad_mixed, log_totals, allowed, score_scale):

    def one_sequence(entries):
        query_seq, key_seq, value_seq, grad_seq, log_seq, allowed_seq = entries
        scores = (
            jnp.einsum("qhd,khd->hqk", query_seq, key_seq, preferred_element_type=jnp.float32)
            * score_scale
        )
        scores = jnp.where(allowed_seq[None], scores, NEGATIVE)
        attention = jnp.exp(scores - log_seq)
        grad_value = jnp.einsum(
            "hqk,qhd->khd",
            attention.astype(jnp.bfloat16),
            grad_seq,
            preferred_element_type=jnp.float32,
        )
        grad_attention = jnp.einsum(
            "qhd,khd->hqk", grad_seq, value_seq, preferred_element_type=jnp.float32
        )
        row_delta = jnp.sum(attention * grad_attention, axis=-1, keepdims=True)
        grad_scores = (attention * (grad_attention - row_delta)).astype(jnp.bfloat16)
        grad_query = (
            jnp.einsum("hqk,khd->qhd", grad_scores, key_seq, preferred_element_type=jnp.float32)
            * score_scale
        )
        grad_key = (
            jnp.einsum("hqk,qhd->khd", grad_scores, query_seq, preferred_element_type=jnp.float32)
            * score_scale
        )
        return (grad_query, grad_key, grad_value.astype(jnp.bfloat16))

    return lax.map(one_sequence, (query, key_rows, value_rows, grad_mixed, log_totals, allowed))


def plain_device(
    tokens,
    stack,
    cotangent,
    starts,
    w_query,
    w_key,
    w_value,
    w_output,
    w_in,
    w_out,
    gain_one,
    shift_one,
    gain_two,
    shift_two,
    bias_in,
    bias_out,
    depth_weights,
):
    rows_here = tokens.shape[0]
    features = tokens.shape[1]
    groups = lax.axis_size("tensor")
    position = lax.axis_index("tensor")
    seq_count = starts.shape[0]
    seq_length = rows_here * groups // seq_count
    score_scale = 1.0 / math.sqrt(HEAD_DIM)
    local_heads = w_query.shape[1] // HEAD_DIM
    hidden = w_in.shape[1]
    cosine_table, sine_table = tables(seq_length, HEAD_DIM)
    allowed = allowed_mask(starts, seq_length, PIECE)

    def to_heads(matrix):
        return matrix.reshape(seq_count, seq_length, local_heads, HEAD_DIM)

    def from_heads(blocks):
        return blocks.reshape(seq_count * seq_length, local_heads * HEAD_DIM)

    def share_rows(local_rows):
        return lax.all_gather(local_rows, "tensor", axis=0, tiled=True)

    def share_grad(local_rows):
        return lax.all_gather(local_rows, "tensor", axis=0, tiled=True)

    def merge_rows(source, weight):
        return lax.psum_scatter(
            jnp.dot(source, weight, preferred_element_type=jnp.float32),
            "tensor",
            scatter_dimension=0,
            tiled=True,
        )

    def return_rows(pairs):
        running = jnp.zeros((lax.axis_size("tensor") * rows_here, features), jnp.float32)
        for source, weight in pairs:
            running = running + right_transposed(source, weight)
        return lax.psum_scatter(running, "tensor", scatter_dimension=0, tiled=True)

    query_w, key_w, value_w, output_w = (
        lax.all_gather(w_query, "dp", axis=0, tiled=True),
        lax.all_gather(w_key, "dp", axis=0, tiled=True),
        lax.all_gather(w_value, "dp", axis=0, tiled=True),
        lax.all_gather(w_output, "dp", axis=1, tiled=True),
    )
    inner_w, outer_w = (
        lax.all_gather(w_in, "dp", axis=0, tiled=True),
        lax.all_gather(w_out, "dp", axis=1, tiled=True),
    )
    token_rows = tokens.astype(jnp.float32)
    normed_one = layer_norm(token_rows, gain_one, shift_one).astype(jnp.bfloat16)
    normed_all = share_rows(normed_one)
    query = rotate(
        to_heads(jnp.dot(normed_all, query_w, preferred_element_type=jnp.float32)),
        cosine_table,
        sine_table,
    ).astype(jnp.bfloat16)
    key_rows = rotate(
        to_heads(jnp.dot(normed_all, key_w, preferred_element_type=jnp.float32)),
        cosine_table,
        sine_table,
    ).astype(jnp.bfloat16)
    value_rows = to_heads(jnp.dot(normed_all, value_w, preferred_element_type=jnp.float32)).astype(
        jnp.bfloat16
    )
    mixed_heads, log_totals = attend_forward(query, key_rows, value_rows, allowed, score_scale)
    mixed_flat = from_heads(mixed_heads)
    middle = token_rows + merge_rows(mixed_flat, output_w)
    normed_two = layer_norm(middle, gain_two, shift_two).astype(jnp.bfloat16)
    second_all = share_rows(normed_two)
    bias_slice = lax.dynamic_slice_in_dim(bias_in, position * hidden, hidden)
    pre_act = jnp.dot(second_all, inner_w, preferred_element_type=jnp.float32) + bias_slice
    activated = gelu_tanh(pre_act).astype(jnp.bfloat16)
    block_out = middle + merge_rows(activated, outer_w) + bias_out
    averaged = depth_weights[4] * block_out
    for layer_index in range(4):
        averaged = averaged + depth_weights[layer_index] * stack[layer_index].astype(jnp.float32)
    layer_out = averaged.astype(jnp.bfloat16)
    grad_rows = cotangent.astype(jnp.float32)
    grad_stack = jnp.stack([depth_weights[layer_index] * grad_rows for layer_index in range(4)])
    depth_terms = jnp.stack(
        [jnp.sum(stack[layer_index].astype(jnp.float32) * grad_rows) for layer_index in range(4)]
        + [jnp.sum(block_out * grad_rows)]
    )
    grad_block = depth_weights[4] * grad_rows
    grad_bias_out = jnp.sum(grad_block, axis=0)
    grad_sent = share_grad(grad_block.astype(jnp.bfloat16))
    grad_outer = left_transposed(activated, grad_sent)
    grad_act = right_transposed(grad_sent, outer_w)
    grad_pre = jax.vjp(gelu_tanh, pre_act)[1](grad_act)[0].astype(jnp.bfloat16)
    grad_bias_slice = jnp.sum(grad_pre.astype(jnp.float32), axis=0)
    bias_full = lax.dynamic_update_slice_in_dim(
        jnp.zeros((bias_in.shape[0],), jnp.float32), grad_bias_slice, position * hidden, 0
    )
    grad_inner = left_transposed(second_all, grad_pre)
    grad_norm_two = return_rows(((grad_pre, inner_w),))
    layer_two = jax.vjp(layer_norm, middle, gain_two, shift_two)[1](grad_norm_two)
    grad_middle = grad_block + layer_two[0]
    grad_attn_sent = share_grad(grad_middle.astype(jnp.bfloat16))
    grad_output_w = left_transposed(mixed_flat, grad_attn_sent)
    grad_mixed = right_transposed(grad_attn_sent, output_w).astype(jnp.bfloat16)
    grad_query, grad_key, grad_value = attend_backward(
        query, key_rows, value_rows, to_heads(grad_mixed), log_totals, allowed, score_scale
    )
    grad_query = from_heads(rotate(grad_query, cosine_table, -sine_table)).astype(jnp.bfloat16)
    grad_key = from_heads(rotate(grad_key, cosine_table, -sine_table)).astype(jnp.bfloat16)
    grad_value = from_heads(grad_value)
    grad_query_w = left_transposed(normed_all, grad_query)
    grad_key_w = left_transposed(normed_all, grad_key)
    grad_value_w = left_transposed(normed_all, grad_value)
    grad_norm_one = return_rows(((grad_query, query_w), (grad_key, key_w), (grad_value, value_w)))
    layer_one = jax.vjp(layer_norm, token_rows, gain_one, shift_one)[1](grad_norm_one)
    grad_tokens = grad_middle + layer_one[0]
    grad_w_query, grad_w_key, grad_w_value, grad_w_output, grad_w_in, grad_w_out = (
        lax.psum_scatter(grad_query_w, "dp", scatter_dimension=0, tiled=True),
        lax.psum_scatter(grad_key_w, "dp", scatter_dimension=0, tiled=True),
        lax.psum_scatter(grad_value_w, "dp", scatter_dimension=0, tiled=True),
        lax.psum_scatter(grad_output_w, "dp", scatter_dimension=1, tiled=True),
        lax.psum_scatter(grad_inner, "dp", scatter_dimension=0, tiled=True),
        lax.psum_scatter(grad_outer, "dp", scatter_dimension=1, tiled=True),
    )
    summed = lax.psum(
        (
            layer_one[1],
            layer_one[2],
            layer_two[1],
            layer_two[2],
            bias_full,
            grad_bias_out,
            depth_terms,
        ),
        ("dp", "tensor"),
    )
    return (
        layer_out,
        grad_tokens,
        grad_stack,
        grad_w_query,
        grad_w_key,
        grad_w_value,
        grad_w_output,
        grad_w_in,
        grad_w_out,
        summed[0],
        summed[1],
        summed[2],
        summed[3],
        summed[4],
        summed[5],
        summed[6],
    )


BF = jnp.bfloat16
F32 = jnp.float32
MESH = pl.DeviceIdType.MESH
BLOCK = 256
EXPONENT_SCALE = math.log2(math.e) / math.sqrt(HEAD_DIM)


PLAN = (
    (
        ("A", 0, 0, 128),
        ("A", 0, 128, 128),
        ("A", 0, 256, 128),
        ("A", 0, 384, 128),
        ("A", 0, 512, 128),
        ("B", 0, 640, 128),
        ("A", 1, 0, 256),
        ("A", 1, 256, 256),
        ("B", 1, 512, 128),
        ("B", 1, 640, 128),
        ("A", 2, 0, 256),
        ("B", 2, 256, 128),
        ("A", 2, 384, 128),
        ("B", 2, 512, 128),
        ("B", 2, 640, 128),
    ),
    (
        ("A", 2, 0, 256),
        ("B", 2, 256, 128),
        ("A", 2, 384, 256),
        ("B", 2, 640, 128),
        ("B", 1, 0, 128),
        ("A", 1, 128, 128),
        ("B", 1, 256, 128),
        ("A", 1, 384, 256),
        ("B", 1, 640, 128),
        ("A", 0, 0, 128),
        ("A", 0, 128, 128),
        ("A", 0, 256, 128),
        ("A", 0, 384, 128),
        ("A", 0, 512, 128),
        ("B", 0, 640, 128),
    ),
    {
        "norm": ((1, 0, 0), (1, 5, 0), (1, 8, 0), (1, 9, 0),),
        "mask0": ((1, 1, 0), (1, 11, 0), (1, 13, 0), (1, 14, 0),),
        "mask2": ((1, 2, 0),),
        "mask3": ((1, 0, 1),),
        "stack2": ((1, 3, 0),),
        "stack3": ((1, 1, 1),),
        "proj0.0": ((1, 4, 0), (1, 0, 2), (1, 2, 1), (1, 5, 1), (1, 1, 2), (1, 3, 1), (1, 4, 1), (1, 0, 3), (1, 6, 0), (1, 2, 2), (1, 5, 2), (1, 1, 3), (1, 7, 0), (1, 3, 2), (1, 6, 1), (1, 2, 3), (1, 8, 1), (1, 5, 3), (1, 4, 2),),
        "att0.0": ((1, 7, 1),),
        "att0.1": ((1, 3, 3),),
        "att0.2": ((1, 9, 1),),
        "att0.3": ((1, 6, 2),),
        "att2.0": ((1, 8, 2),),
        "att2.2": ((1, 4, 3), (1, 10, 0),),
        "att3.0": ((1, 9, 2),),
        "att3.2": ((1, 11, 1),),
        "att3.3": ((1, 7, 2), (1, 8, 3),),
        "att5.0": ((1, 10, 1),),
        "att5.2": ((1, 6, 3), (1, 12, 0),),
        "r.other": ((1, 9, 3),),
        "r.low": ((1, 13, 1),),
        "ln2": ((1, 11, 2),),
        "in0": ((1, 10, 2), (1, 14, 1),),
        "in1": ((1, 12, 1), (1, 7, 3),),
        "in3": ((1, 11, 3), (1, 13, 2),),
        "dc2": ((1, 14, 2),),
        "dc3": ((1, 12, 2),),
        "bh0": ((1, 13, 3), (1, 10, 3), (0, 1, 0), (0, 0, 0), (1, 14, 3),),
        "bh1": ((1, 12, 3), (0, 3, 0),),
        "bh2": ((0, 1, 1),),
        "bh3": ((0, 2, 0),),
        "lnb2": ((0, 0, 1), (0, 3, 1),),
        "db3": ((0, 1, 2),),
        "go": ((0, 4, 0), (0, 5, 0),),
        "dwo": ((0, 0, 2),),
        "ab0.0": ((0, 1, 3), (0, 2, 1),),
        "ab0.1": ((0, 3, 2),),
        "ab0.2": ((0, 7, 0),),
        "ab1.0": ((0, 4, 1),),
        "ab1.1": ((0, 3, 3), (0, 0, 3), (0, 5, 1),),
        "ab1.3": ((0, 6, 0),),
        "ab2.0": ((0, 2, 2),),
        "ab2.3": ((0, 4, 2),),
        "da0": ((0, 5, 2), (0, 8, 0),),
        "ab3.0": ((0, 9, 0),),
        "ab3.1": ((0, 4, 3), (0, 6, 1),),
        "ab3.2": ((0, 2, 3), (0, 7, 1),),
        "ab3.3": ((0, 10, 0),),
        "ab4.0": ((0, 5, 3),),
        "ab4.2": ((0, 8, 1),),
        "ab4.3": ((0, 14, 0),),
        "ab5.0": ((0, 6, 2), (0, 11, 0),),
        "ab5.3": ((0, 7, 2),),
        "da2": ((0, 6, 3),),
        "da3": ((0, 8, 2),),
        "bp0": ((0, 9, 1), (0, 12, 0),),
        "bp1": ((0, 10, 1), (0, 14, 1),),
        "lnb1": ((0, 7, 3), (0, 8, 3), (0, 9, 2), (0, 11, 1), (0, 13, 0),),
        "vs0": ((0, 10, 2), (0, 12, 1), (0, 14, 2),),
        "vs1": ((0, 9, 3), (0, 11, 2), (0, 13, 1),),
        "out1": ((0, 10, 3), (0, 12, 2), (0, 14, 3),),
        "fin": ((0, 11, 3), (0, 13, 2),),
        "vs2": ((0, 12, 3),),
        "end": ((0, 13, 3),),
    },
)


def dot(left, right, left_axis, right_axis):
    return lax.dot_general(
        left, right, (((left_axis,), (right_axis,)), ((), ())), preferred_element_type=F32
    )


def norm_parts(values):
    centre = values - jnp.mean(values, axis=-1, keepdims=True)
    inverse = lax.rsqrt(jnp.mean(centre * centre, axis=-1, keepdims=True) + EPSILON)
    return centre * inverse, inverse


def norm_back(grad, gain, unit, inverse):
    scaled = grad * gain
    first = jnp.mean(scaled, axis=-1, keepdims=True)
    second = jnp.mean(scaled * unit, axis=-1, keepdims=True)
    return inverse * (scaled - first - unit * second)


def gelu_pair(values):
    root = math.sqrt(2.0 / math.pi)
    square = values * values
    bend = jnp.tanh(root * values * (1.0 + 0.044715 * square))
    half = 0.5 * (1.0 + bend)
    slope = half + 0.5 * root * values * (1.0 - bend * bend) * (1.0 + 3 * 0.044715 * square)
    return values * half, slope


def column_sum(values):
    return jnp.sum(values, axis=0, keepdims=True)


def rotary_tables(length):
    half = HEAD_DIM // 2
    frequency = np.exp(-np.log(10000.0) * np.arange(half) * 2.0 / HEAD_DIM)
    angles = np.arange(length)[:, None] * frequency[None, :]
    return np.cos(angles).astype(np.float32), np.sin(angles).astype(np.float32)


def fused_body(
    nz,
    rows,
    features,
    shard,
    plan,
    tokens_hbm,
    cotangent_hbm,
    stack,
    w_query,
    w_key,
    w_value,
    w_output,
    w_in,
    w_out,
    gain_one,
    shift_one,
    gain_two,
    shift_two,
    bias_in,
    bias_out,
    depth,
    starts,
    cosine_t,
    sine_t,
    layer_hbm,
    grad_tokens_hbm,
    grad_packed,
    grad_vectors,
    G,
    D,
    RY,
    RX,
    RZ,
    A,
    C,
    GM,
    K,
    V,
    KT,
    QT,
    OT,
    LS,
    MB,
    Z,
    GP,
    GOT,
    GT,
    WO,
    R32,
    AVG,
    SR,
    SB,
    XG,
    VS,
    VR,
    VZ,
    GKA,
    GVA,
    tokens,
    cotangent,
    cosine,
    sine,
    BI,
    grad_tokens,
    local_sem,
    ag_send,
    ag_recv,
    rs_send,
    rs_recv,
    sib_send,
    sib_recv,
    vec_send,
    vec_recv,
):
    length = 2 * rows
    heads = 3
    width = heads * HEAD_DIM
    gathers, reduces, schedule = plan
    dp = lax.axis_index("dp")
    t = lax.axis_index("tensor")
    z = dp // 2
    x = lax.rem(dp, 2)
    low = lax.rem(t, 2)
    pair = t // 2
    other = 1 - low
    sib = (dp, t + 1 - 2 * low)
    ypeer = (dp, lax.rem(t + 2, 4))
    xpeer = (dp + 1 - 2 * x, t)

    def zpeer(j):
        return (lax.rem(z + j, nz) * 2 + x, t)

    def remote(src, dst, send, recv, peer):
        return pltpu.make_async_remote_copy(
            src_ref=src, dst_ref=dst, send_sem=send, recv_sem=recv,
            device_id=peer, device_id_type=MESH,
        )

    everything = slice(None)

    def gather_copies(f, stage):
        kind, k, first, count = gathers[f]
        cols = pl.ds(first, count)
        axis = ("zxy" if kind == "A" else "yzx")[stage]
        if axis == "z":
            slot = 0 if kind == "A" else everything
            mine = G.at[k, slot, z, x, :, cols]
            sent, taken = [], []
            for j in range(nz - 1):
                sems = (ag_send.at[f, j], ag_recv.at[f, j], zpeer(j + 1))
                sent.append(lambda mine=mine, sems=sems: remote(mine, mine, *sems))
                from_z = lax.rem(z + nz - 1 - j, nz)
                taken.append(
                    lambda mine=mine, sems=sems, from_z=from_z: remote(
                        mine, G.at[k, slot, from_z, x, :, cols], *sems
                    )
                )
            return sent, taken
        if axis == "x":
            slot = 0 if kind == "A" else everything
            ref = G.at[k, slot, :, x, :, cols]
            copy = lambda: remote(ref, ref, ag_send.at[f, nz - 1], ag_recv.at[f, nz - 1], xpeer)
            return [copy], [copy]
        sems = (ag_send.at[f, nz], ag_recv.at[f, nz], ypeer)
        if kind == "A":
            copy = lambda: remote(G.at[k, 0, :, :, :, cols], G.at[k, 1, :, :, :, cols], *sems)
        else:
            copy = lambda: remote(G.at[k, 0, z, x, :, cols], G.at[k, 1, z, x, :, cols], *sems)
        return [copy], [copy]

    def gather_step(f, stage):
        if stage == 4:
            for past in range(3):
                for copy in gather_copies(f, past)[0]:
                    copy().wait_send()
            return
        awaited = {1: 0, 2: 1, 3: 2, 5: 1}.get(stage)
        if awaited is not None:
            for copy in gather_copies(f, awaited)[1]:
                copy().wait_recv()
        started = {0: 0, 1: 1, 2: 2, 6: 2}.get(stage)
        if started is not None:
            for copy in gather_copies(f, started)[0]:
                copy().start()

    def reduce_copies(f, stage):
        kind, k, first, count = reduces[f]
        cols = pl.ds(first, count)
        axis = ("yxz" if kind == "A" else "xzy")[stage]

        def sems(n):
            return rs_send.at[f, n], rs_recv.at[f, n]

        if axis == "z":
            slot = 0 if kind == "A" else everything
            land = 0 if kind == "A" else everything
            return [
                lambda j=j: remote(
                    D.at[k, slot, lax.rem(z + j + 1, nz), x, :, cols],
                    RZ.at[k, j, land, :, cols], *sems(j), zpeer(j + 1),
                )
                for j in range(nz - 1)
            ]
        if axis == "x":
            if kind == "A":
                return [
                    lambda: remote(
                        D.at[k, 0, :, 1 - x, :, cols], RX.at[k, :, :, cols], *sems(nz - 1), xpeer
                    )
                ]
            return [
                lambda: remote(
                    D.at[k, :, :, 1 - x, :, cols], RY.at[k, :, :, :, cols], *sems(nz - 1), xpeer
                )
            ]
        if kind == "A":
            return [
                lambda side=side, n=n: remote(
                    D.at[k, 1, :, side, :, cols], RY.at[k, side, :, :, cols], *sems(nz + n), ypeer
                )
                for n, side in enumerate((1 - x, x))
            ]
        return [lambda: remote(D.at[k, 1, z, x, :, cols], RX.at[k, 0, :, cols], *sems(nz), ypeer)]

    def reduce_step(f, stage):
        kind, k, first, count = reduces[f]
        cols = pl.ds(first, count)
        if stage == 4:
            for past in range(3):
                for copy in reduce_copies(f, past):
                    copy().wait_send()
            return
        before = reduce_copies(f, stage - 1) if stage else []
        after = reduce_copies(f, stage) if stage < 3 else []

        def add(target, source):
            target[...] = (target[...].astype(F32) + source[...].astype(F32)).astype(BF)

        if kind == "A" and stage == 1:
            before[0]().wait_recv()
            add(D.at[k, 0, :, 1 - x, :, cols], RY.at[k, 1 - x, :, :, cols])
            after[0]().start()
            before[1]().wait_recv()
            add(D.at[k, 0, :, x, :, cols], RY.at[k, x, :, :, cols])
            return
        for copy in before:
            copy().wait_recv()
        if kind == "A" and stage == 2:
            add(D.at[k, 0, :, x, :, cols], RX.at[k, :, :, cols])
        elif kind == "B" and stage == 1:
            add(D.at[k, :, :, x, :, cols], RY.at[k, :, :, :, cols])
        elif kind == "B" and stage == 2:
            total = D[k, :, z, x, :, cols].astype(F32)
            for j in range(nz - 1):
                total = total + RZ[k, j, :, :, cols].astype(F32)
            D[k, 1, z, x, :, cols] = total[1].astype(BF)
            grad_packed[k, :, cols] = total[0]
        elif kind == "A" and stage == 3:
            total = D[k, 0, z, x, :, cols].astype(F32)
            for j in range(nz - 1):
                total = total + RZ[k, j, 0, :, cols].astype(F32)
            grad_packed[k, :, cols] = total
        elif kind == "B" and stage == 3:
            grad_packed[k, :, cols] = grad_packed[k, :, cols] + RX[k, 0, :, cols].astype(F32)
        for copy in after:
            copy().start()

    def drain(k):
        for f in range(len(gathers)):
            if gathers[f][1] == k:
                gather_step(f, 4)

    def tick(name):
        for gather, flow, stage in schedule.get(name, ()):
            if gather:
                gather_step(flow, stage)
            else:
                reduce_step(flow, stage)

    def tick_at(prefix, index, count, suffix=""):
        for i in range(count):
            name = prefix + str(i) + suffix
            if schedule.get(name):

                @pl.when(index == i)
                def _(name=name):
                    tick(name)

    def sib_copy(n, src, dst):
        return remote(src, dst, sib_send.at[n], sib_recv.at[n], sib)

    send_a = sib_copy(0, A.at[low], A.at[low])
    take_a = sib_copy(0, A.at[low], A.at[other])
    send_gm = sib_copy(1, GM.at[low], GM.at[low])
    take_gm = sib_copy(1, GM.at[low], GM.at[other])
    half_rows = rows // 2
    part_r = [
        sib_copy(n, SB.at[pl.ds(i * half_rows, half_rows)], XG.at[pl.ds(i * half_rows, half_rows)])
        for i, n in enumerate((2, 8))
    ]
    send_c = sib_copy(3, C.at[low], C.at[low])
    take_c = sib_copy(3, C.at[low], C.at[other])
    part_g = sib_copy(4, SB, XG)
    send_gl = sib_copy(5, GM.at[low], GM.at[low])
    take_gl = sib_copy(5, GM.at[low], GM.at[other])
    part_b = sib_copy(6, SB, XG)
    part_a = sib_copy(7, SB, XG)

    loads = [
        pltpu.make_async_copy(tokens_hbm, tokens, local_sem.at[0]),
        pltpu.make_async_copy(cotangent_hbm, cotangent, local_sem.at[1]),
        pltpu.make_async_copy(stack, Z, local_sem.at[2]),
    ]
    for load in loads:
        load.start()
    barrier = pltpu.get_barrier_semaphore()
    partners = [sib, ypeer, xpeer] + [zpeer(j + 1) for j in range(nz - 1)]
    for peer in partners:
        pl.semaphore_signal(barrier, inc=1, device_id=peer, device_id_type=MESH)
    G[0, 0, z, x] = jnp.concatenate(
        [w_query[...], w_key[...], w_value[...], w_output[...].T], axis=1
    )
    G[1, 0, z, x] = w_in[...]
    G[2, 0, z, x] = w_out[...]
    pl.semaphore_wait(barrier, len(partners))
    tick("norm")

    gain_one, shift_one, gain_two, shift_two, bias_out = (
        ref[...].reshape(1, features)
        for ref in (gain_one, shift_one, gain_two, shift_two, bias_out)
    )
    piece = 128
    pieces = rows // piece

    def chunk(i):
        return pl.ds(i * piece if isinstance(i, int) else pl.multiple_of(i * piece, piece), piece)

    def over_pieces(step, carry):
        for i in range(pieces):
            carry = step(i, carry)
        return carry

    loads[0].wait()
    loads[1].wait()

    def first_norm(i, carry):
        unit, _ = norm_parts(tokens[chunk(i), :].astype(F32))
        A[low, chunk(i), :] = (unit * gain_one + shift_one).astype(BF)
        GM[low, chunk(i), :] = (depth[4] * cotangent[chunk(i), :].astype(F32)).astype(BF)
        return carry

    lax.fori_loop(0, pieces, first_norm, 0)
    send_a.start()
    send_gm.start()
    for n in range(4):
        BI[n : n + 1, :] = bias_in[:, n * features : (n + 1) * features]
    cosine[...] = jnp.concatenate([cosine_t[...]] * 4, axis=0).T
    sine[...] = jnp.concatenate([-sine_t[...], sine_t[...]] * 2, axis=0).T

    s0, s1 = starts[pair, 0], starts[pair, 1]
    blocks = length // BLOCK
    for block in range(blocks):
        tick("mask" + str(block))
        key = block * BLOCK + lax.broadcasted_iota(jnp.int32, (2 * BLOCK, BLOCK), 0)
        query = block * BLOCK + lax.broadcasted_iota(jnp.int32, (2 * BLOCK, BLOCK), 1)
        fine = key <= query
        for s in (s0, s1):
            fine = fine | ((key >= s) & (key < s + PIECE) & (query >= s) & (query < s + PIECE))
        MB[block] = jnp.where(fine, 0.0, NEGATIVE)
    VS[...] = jnp.zeros_like(VS)
    for s in range(2):
        for h in range(heads):
            V[heads * s + h, :, HEAD_DIM:] = jnp.where(
                lax.broadcasted_iota(jnp.int32, (length, HEAD_DIM), 1) == 0, 1.0, 0.0
            ).astype(BF)

    loads[2].wait()

    def earlier(i, sums):
        tick_at("stack", i, pieces)
        grad = cotangent[chunk(i), :].astype(F32)
        mean = jnp.zeros((piece, features), F32)
        new = [sums[0] + column_sum(grad)]
        for k in range(4):
            layer = Z[k, chunk(i), :].astype(F32)
            mean = mean + depth[k] * layer
            new.append(sums[k + 1] + column_sum(layer * grad))
        AVG[chunk(i), :] = mean
        return tuple(new)

    zero_row = jnp.zeros((1, features), F32)
    sums = lax.fori_loop(0, pieces, earlier, (zero_row,) * 5)
    VS[4:5, :] = depth[4] * sums[0]
    for k in range(4):
        VS[5 + k : 6 + k, :] = sums[k + 1]

    take_a.wait_recv()

    def whole(ref, *index):
        value = ref[index]
        return value.reshape(value.shape[-4] * value.shape[-3] * value.shape[-2], value.shape[-1])

    lane = lax.broadcasted_iota(jnp.int32, (rows, 128), 1)
    front = lax.rem(lane, HEAD_DIM) < HEAD_DIM // 2

    def project(slot):
        for half in range(2):
            tick_at("proj", slot, 2, "." + str(half))
            weight = whole(G, 0, slot, everything, everything, everything, slice(0, 640))
            span = slice(half * rows, (half + 1) * rows)
            result = dot(A[half], weight, 1, 0)
            turned = []
            for tile in range(3):
                part = result[:, tile * 128 : (tile + 1) * 128]
                partner = jnp.where(front, pltpu.roll(part, 96, 1), pltpu.roll(part, 32, 1))
                turned.append((part * cosine[span, :] + partner * sine[span, :]).astype(BF))
            for h in range(heads):
                n = heads * slot + h
                at = h * HEAD_DIM
                QT[n, :, span] = turned[at // 128][:, at % 128 : at % 128 + HEAD_DIM].T
                at = width + h * HEAD_DIM
                key = turned[at // 128][:, at % 128 : at % 128 + HEAD_DIM]
                K[n, span, :] = key
                KT[n, :, span] = key.T
                at = 2 * width + h * HEAD_DIM
                V[n, span, :HEAD_DIM] = result[:, at : at + HEAD_DIM].astype(BF)

    def span_of(block):
        lo = block * BLOCK
        return lo, min(lo + 2 * BLOCK, length)

    def attend(n, carry):
        @pl.when(lax.rem(n, heads) == 0)
        def _():
            project(n // heads)

        def scores(block):
            lo, top = span_of(block)
            return dot(K[n, 0:top, :], QT[n, :, lo : lo + BLOCK], 1, 0)

        ahead = scores(0)
        for block in range(blocks):
            tick_at("att", n, 2 * heads, "." + str(block))
            lo, top = span_of(block)
            half, at = lo // rows, lo % rows
            score = ahead * EXPONENT_SCALE
            if block + 1 < blocks:
                ahead = scores(block + 1)
            tail = score[lo:] + MB[block, 0 : top - lo, :]
            score = jnp.concatenate([score[:lo], tail], axis=0) if lo else tail
            highest = jnp.max(score, axis=0, keepdims=True)
            power = jnp.exp2(score - highest).astype(BF)
            mixed = dot(V[n, 0:top, :], power, 0, 0)
            total = mixed[HEAD_DIM : HEAD_DIM + 1, :]
            OT[half, n, :, at : at + BLOCK] = (mixed[:HEAD_DIM, :] / total).astype(BF)
            LS[pl.ds(n, 1), lo : lo + BLOCK] = highest + jnp.log2(total)
        return carry

    lax.fori_loop(0, 2 * heads, attend, 0)
    tick("wo")
    for slot in range(2):
        flipped = whole(G, 0, slot, everything, everything, everything, slice(512, 768)).T
        WO[slot * width : (slot + 1) * width, :] = flipped[64:256, :]

    def mixed_rows(half):
        return OT[half].reshape(2 * width, rows)

    tick("r.other")
    for i in range(2):
        span = slice(i * half_rows, (i + 1) * half_rows)
        left = OT[other, :, :, span].reshape(2 * width, half_rows)
        SB[span, :] = dot(left, WO[...], 0, 0).astype(BF)
        part_r[i].start()
    tick("r.low")
    R32[...] = dot(mixed_rows(low), WO[...], 0, 0)
    for copy in part_r:
        copy.wait_recv()
    tick("ln2")

    def second_norm(i, carry):
        middle = tokens[chunk(i), :].astype(F32) + R32[chunk(i), :] + XG[chunk(i), :].astype(F32)
        R32[chunk(i), :] = middle
        unit, _ = norm_parts(middle)
        C[low, chunk(i), :] = (unit * gain_two + shift_two).astype(BF)
        return carry

    over_pieces(second_norm, 0)
    send_c.start()
    def hidden_bias(slot):
        return BI[pl.ds(lax.rem(t + 2 * slot, 4), 1), :]

    def inner(i, carry):
        tick_at("in", i, 4)

        @pl.when(i == 2)
        def _():
            take_c.wait_recv()

        half, slot = lax.rem(low + i // 2, 2), lax.rem(i, 2)
        pre = dot(C[half], whole(G, 1, slot), 1, 0) + hidden_bias(slot)
        act, slope = gelu_pair(pre)
        Z[2 * slot + half] = act.astype(BF)
        GP[2 * slot + half] = slope.astype(BF)
        return carry

    lax.fori_loop(0, 4, inner, 0)
    take_gm.wait_recv()

    def outer_products(name, k, left, right):
        half_cols = features // 2

        def one(i, carry):
            tick_at(name, i, 4)
            slot, part = 1 - i // 2, lax.rem(i, 2)
            cols = pl.ds(pl.multiple_of(part * half_cols, 128), half_cols)
            value = dot(
                left[:, :, cols].reshape(length, half_cols),
                right[pl.ds(2 * slot, 2)].reshape(length, features),
                0,
                0,
            )
            D[k, slot, pl.ds(part * (nz // 2), nz // 2)] = value.astype(BF).reshape(
                nz // 2, 2, shard, features
            )
            return carry

        lax.fori_loop(0, 4, one, 0)

    outer_products("dc", 2, GM, Z)

    def back(i, carry):
        half = lax.rem(other + i, 2)

        def one(slot, total):
            tick_at("bh", 2 * i + slot, 4)
            grad = dot(GM[half], whole(G, 2, slot), 1, 0)
            total = total + column_sum(grad * Z[2 * slot + half].astype(F32))
            grad = (grad * GP[2 * slot + half].astype(F32)).astype(BF)
            GP[2 * slot + half] = grad
            row = pl.ds(9 + lax.rem(t + 2 * slot, 4), 1)
            VS[row, :] = VS[row, :] + column_sum(grad.astype(F32))
            return total

        carry = lax.fori_loop(0, 2, one, carry)
        tick_at("bi", i, 2)
        grad_tokens[...] = dot(GP[half], whole(G, 1, 0), 1, 1) + dot(
            GP[2 + half], whole(G, 1, 1), 1, 1
        )

        @pl.when(i == 0)
        def _():
            for copy in part_r:
                copy.wait_send()
            SB[...] = grad_tokens[...].astype(BF)
            part_g.start()

        return carry

    drain(0)
    VS[13:14, :] = lax.fori_loop(0, 2, back, zero_row) / depth[4]
    part_g.wait_recv()
    send_gm.wait_send()
    tick("lnb2")

    def second_back(i, carry):
        middle = R32[chunk(i), :]
        unit, inverse = norm_parts(middle)
        grad = grad_tokens[chunk(i), :] + XG[chunk(i), :].astype(F32)
        coming = cotangent[chunk(i), :].astype(F32)
        whole_grad = depth[4] * coming + norm_back(grad, gain_two, unit, inverse)
        grad_tokens[chunk(i), :] = whole_grad
        GM[low, chunk(i), :] = whole_grad.astype(BF)
        return (
            carry[0] + column_sum(grad * unit),
            carry[1] + column_sum(grad),
            carry[2] + column_sum(coming * (middle + bias_out)),
        )

    sums = lax.fori_loop(0, pieces, second_back, (zero_row,) * 3)
    VS[2:3, :] = sums[0]
    VS[3:4, :] = sums[1]
    send_gl.start()
    VS[13:14, :] = VS[13:14, :] + sums[2]
    outer_products("db", 1, C, GP)

    drain(1)
    take_gl.wait_recv()
    tick("go")

    def grad_mixed(half, carry):
        GOT[half] = dot(WO[...], GM[half], 1, 1).astype(BF).reshape(2 * heads, HEAD_DIM, rows)
        return carry

    lax.fori_loop(0, 2, grad_mixed, 0)
    tick("dwo")
    for slot in range(2):
        value = sum(
            dot(OT[half, heads * slot : heads * slot + heads].reshape(width, rows), GM[half], 1, 0)
            for half in range(2)
        )
        D[0, slot, :, :, :, 3 * width :] = value.T.astype(BF).reshape(nz, 2, shard, width)

    def unturn(value, span):
        front_half, back_half = value[: HEAD_DIM // 2], value[HEAD_DIM // 2 :]
        cosines, sines = cosine_t[:, span], sine_t[:, span]
        return jnp.concatenate(
            [front_half * cosines + back_half * sines, back_half * cosines - front_half * sines],
            axis=0,
        )

    scale = 1.0 / math.sqrt(HEAD_DIM)

    def attend_back(i, carry):
        slot, h = 1 - i // heads, lax.rem(i, heads)
        n = heads * slot + h

        def place(which):
            return pl.ds(pl.multiple_of(which * width + h * HEAD_DIM, HEAD_DIM), HEAD_DIM)

        def products(block):
            lo, top = span_of(block)
            half, at = lo // rows, lo % rows
            grad_t = GOT[half, n, :, at : at + BLOCK]
            return (
                dot(K[n, 0:top, :], QT[n, :, lo : lo + BLOCK], 1, 0),
                dot(V[n, 0:top, :HEAD_DIM], grad_t, 1, 0),
            )

        for step in range(blocks):
            tick_at("ab", i, 2 * heads, "." + str(step))
            block = blocks - 1 - step
            lo, top = span_of(block)
            half, at = lo // rows, lo % rows
            here = slice(at, at + BLOCK)
            score, grad_power = products(block)
            grad_t = GOT[half, n, :, here]
            delta = jnp.sum(
                OT[half, n, :, here].astype(F32) * grad_t.astype(F32), axis=0, keepdims=True
            )
            score = score * EXPONENT_SCALE - LS[pl.ds(n, 1), lo : lo + BLOCK]
            tail = score[lo:] + MB[block, 0 : top - lo, :]
            score = jnp.concatenate([score[:lo], tail], axis=0) if lo else tail
            power = jnp.exp2(score)
            grad_score = (power * (grad_power - delta)).astype(BF)
            grad_value = dot(grad_t, power.astype(BF), 1, 1)
            grad_key = dot(QT[n, :, lo : lo + BLOCK], grad_score, 1, 1)
            if step:
                GVA[:, 0:top] += grad_value
                GKA[:, 0:top] += grad_key
            else:
                GVA[...] = grad_value
                GKA[...] = grad_key
            grad_query = dot(KT[n, :, 0:top], grad_score, 1, 0) * scale
            GT[slot, half, place(0), here] = unturn(grad_query, slice(lo, lo + BLOCK)).astype(BF)
        for half in range(2):
            span = slice(half * rows, (half + 1) * rows)
            GT[slot, half, place(1), :] = unturn(GKA[:, span] * scale, span).astype(BF)
            GT[slot, half, place(2), :] = GVA[:, span].astype(BF)

        @pl.when(h == heads - 1)
        def _():
            for part in range(2):
                tick_at("da", 2 * (1 - slot) + part, 4)
                half_cols = features // 2
                cols = slice(part * half_cols, (part + 1) * half_cols)
                value = dot(A[0, :, cols], GT[slot, 0], 0, 1) + dot(
                    A[1, :, cols], GT[slot, 1], 0, 1
                )
                first = part * (nz // 2)
                D[0, slot, first : first + nz // 2, :, :, : 3 * width] = value.astype(BF).reshape(
                    nz // 2, 2, shard, 3 * width
                )

        return carry

    lax.fori_loop(0, 2 * heads, attend_back, 0)

    def back_project(half):
        return sum(dot(GT[s, half], whole(G, 0, s)[:, : 3 * width], 0, 1) for s in range(2))

    part_g.wait_send()

    def back_projects(i, carry):
        tick_at("bp", i, 2)
        SR[...] = back_project(lax.rem(other + i, 2))

        @pl.when(i == 0)
        def _():
            SB[...] = SR[...].astype(BF)
            part_a.start()

        return carry

    lax.fori_loop(0, 2, back_projects, 0)
    part_a.wait_recv()
    tick("lnb1")

    def first_back(i, carry):
        unit, inverse = norm_parts(tokens[chunk(i), :].astype(F32))
        grad = SR[chunk(i), :] + XG[chunk(i), :].astype(F32)
        grad_tokens[chunk(i), :] = grad_tokens[chunk(i), :] + norm_back(grad, gain_one, unit, inverse)
        return (carry[0] + column_sum(grad * unit), carry[1] + column_sum(grad))

    sums = over_pieces(first_back, (zero_row, zero_row))
    store_tokens = pltpu.make_async_copy(grad_tokens, grad_tokens_hbm, local_sem.at[3])
    store_tokens.start()
    VS[0:1, :] = sums[0]
    VS[1:2, :] = sums[1]

    def vector_round(n, src, peer):
        copy = remote(src, VR.at[n], vec_send.at[n], vec_recv.at[n], peer)
        copy.start()
        return copy

    round_s = vector_round(0, VS, sib)
    tick("vs0")
    round_s.wait_recv()
    VZ[nz] = VS[...] + VR[0]
    round_y = vector_round(1, VZ.at[nz], ypeer)
    tick("vs1")

    part_a.wait_send()

    def outer(half):
        return dot(Z[half], whole(G, 2, 0), 1, 1) + dot(Z[2 + half], whole(G, 2, 1), 1, 1)

    def outers(i, carry):
        tick_at("out", i, 2)
        SR[...] = outer(lax.rem(other + i, 2))

        @pl.when(i == 0)
        def _():
            SB[...] = SR[...].astype(BF)
            part_b.start()

        return carry

    lax.fori_loop(0, 1, outers, 0)
    round_y.wait_recv()
    VZ[nz + 1] = VZ[nz] + VR[1]
    round_x = vector_round(2, VZ.at[nz + 1], xpeer)
    lax.fori_loop(1, 2, outers, 0)
    part_b.wait_recv()
    round_x.wait_recv()
    VZ[z] = VZ[nz + 1] + VR[2]
    rounds_z = [
        remote(VZ.at[z], VZ.at[z], vec_send.at[3 + j], vec_recv.at[3 + j], zpeer(j + 1))
        for j in range(nz - 1)
    ]
    for c in rounds_z:
        c.start()
    tick("fin")

    def finish_block(i, carry):
        value = R32[chunk(i), :] + SR[chunk(i), :] + XG[chunk(i), :].astype(F32) + bias_out
        tokens[chunk(i), :] = (AVG[chunk(i), :] + depth[4] * value).astype(BF)
        return carry

    lax.fori_loop(0, pieces, finish_block, 0)
    store_layer = pltpu.make_async_copy(tokens, layer_hbm, local_sem.at[4])
    store_layer.start()
    tick("vs2")
    for j in range(nz - 1):
        remote(
            VZ.at[z], VZ.at[lax.rem(z + nz - 1 - j, nz)],
            vec_send.at[3 + j], vec_recv.at[3 + j], zpeer(j + 1),
        ).wait_recv()
    total = VZ[0]
    for j in range(1, nz):
        total = total + VZ[j]
    grad_vectors[...] = total
    drain(2)
    tick("end")
    for f in range(len(reduces)):
        reduce_step(f, 4)
    store_tokens.wait()
    store_layer.wait()
    for c in [send_a, send_c, send_gl, part_b, round_s, round_y, round_x] + rounds_z:
        c.wait_send()


def spread_body(width, cotangent, average, tokens, packed, sums, depth, *outs):
    layer_out, grad_tokens, stack, wq, wk, wv, wo, wi, wu = outs[:9]
    gain_one, shift_one, gain_two, shift_two, bias_in, bias_out, grad_depth = outs[9:]
    layer_out[...] = average[...]
    grad_tokens[...] = tokens[...]
    for k in range(4):
        stack[k] = depth[k] * cotangent[...].astype(F32)

    @pl.when(pl.program_id(0) == 0)
    def _():
        for n, ref in enumerate((wq, wk, wv)):
            ref[...] = packed[0, :, n * width : (n + 1) * width]
        wo[...] = packed[0, :, 3 * width :].T
        wi[...] = packed[1]
        wu[...] = packed[2]
        for n, ref in enumerate((gain_one, shift_one, gain_two, shift_two, bias_out)):
            ref[...] = sums[n, :]
        bias_in[...] = jnp.concatenate([sums[9 + n : 10 + n, :] for n in range(4)], axis=1)
        lane = lax.broadcasted_iota(jnp.int32, (1, 5), 1)
        total = jnp.zeros((1, 5), F32)
        for n, row in enumerate((5, 6, 7, 8, 13)):
            total = jnp.where(lane == n, jnp.sum(sums[row : row + 1, :]), total)
        grad_depth[...] = total


def fused_device(
    tokens,
    stack,
    cotangent,
    starts,
    w_query,
    w_key,
    w_value,
    w_output,
    w_in,
    w_out,
    gain_one,
    shift_one,
    gain_two,
    shift_two,
    bias_in,
    bias_out,
    depth_weights,
):
    rows, features = tokens.shape
    shard = w_query.shape[0]
    nz = lax.axis_size("dp") // 2
    length = 2 * rows
    width = w_query.shape[1]
    heads = width // HEAD_DIM
    cos_np, sin_np = rotary_tables(length)
    gathers, reduces, schedule = PLAN
    shape = jax.ShapeDtypeStruct
    vmem = pl.BlockSpec(memory_space=pltpu.VMEM)
    smem = pl.BlockSpec(memory_space=pltpu.SMEM)
    hbm = pl.BlockSpec(memory_space=pl.ANY)
    dma = pltpu.SemaphoreType.DMA
    scratch = [
        pltpu.VMEM((3, 2, nz, 2, shard, features), BF),
        pltpu.VMEM((3, 2, nz, 2, shard, features), BF),
        pltpu.VMEM((3, 2, nz, shard, features), BF),
        pltpu.VMEM((3, nz, shard, features), BF),
        pltpu.VMEM((3, nz - 1, 2, shard, features), BF),
        pltpu.VMEM((2, rows, features), BF),
        pltpu.VMEM((2, rows, features), BF),
        pltpu.VMEM((2, rows, features), BF),
        pltpu.VMEM((2 * heads, length, HEAD_DIM), BF),
        pltpu.VMEM((2 * heads, length, 2 * HEAD_DIM), BF),
        pltpu.VMEM((2 * heads, HEAD_DIM, length), BF),
        pltpu.VMEM((2 * heads, HEAD_DIM, length), BF),
        pltpu.VMEM((2, 2 * heads, HEAD_DIM, rows), BF),
        pltpu.VMEM((8, length), F32),
        pltpu.VMEM((length // BLOCK, 2 * BLOCK, BLOCK), F32),
        pltpu.VMEM((4, rows, features), BF),
        pltpu.VMEM((4, rows, features), BF),
        pltpu.VMEM((2, 2 * heads, HEAD_DIM, rows), BF),
        pltpu.VMEM((2, 2, 3 * width, rows), BF),
        pltpu.VMEM((2 * width, features), BF),
        pltpu.VMEM((rows, features), F32),
        pltpu.VMEM((rows, features), F32),
        pltpu.VMEM((rows, features), F32),
        pltpu.VMEM((rows, features), BF),
        pltpu.VMEM((rows, features), BF),
        pltpu.VMEM((16, features), F32),
        pltpu.VMEM((3, 16, features), F32),
        pltpu.VMEM((nz + 2, 16, features), F32),
        pltpu.VMEM((HEAD_DIM, length), F32),
        pltpu.VMEM((HEAD_DIM, length), F32),
        pltpu.VMEM((rows, features), BF),
        pltpu.VMEM((rows, features), BF),
        pltpu.VMEM((length, 2 * HEAD_DIM), F32),
        pltpu.VMEM((length, 2 * HEAD_DIM), F32),
        pltpu.VMEM((4, features), F32),
        pltpu.VMEM((rows, features), F32),
        dma((5,)),
        dma((len(gathers), nz + 1)),
        dma((len(gathers), nz + 1)),
        dma((len(reduces), nz + 2)),
        dma((len(reduces), nz + 2)),
        dma((9,)),
        dma((9,)),
        dma((nz + 2,)),
        dma((nz + 2,)),
    ]

    layer_out, grad_tokens, packed, sums = pl.pallas_call(
        functools.partial(fused_body, nz, rows, features, shard, PLAN),
        out_shape=[
            shape((rows, features), BF),
            shape((rows, features), F32),
            shape((3, shard, features), F32),
            shape((16, features), F32),
        ],
        in_specs=[hbm] * 3 + [vmem] * 12 + [smem] * 2 + [vmem] * 2,
        out_specs=[hbm] * 2 + [vmem] * 2,
        scratch_shapes=scratch,
        compiler_params=pltpu.CompilerParams(
            collective_id=0, has_side_effects=True, vmem_limit_bytes=64 * 1024 * 1024
        ),
    )(
        tokens,
        cotangent,
        stack,
        w_query,
        w_key,
        w_value,
        w_output,
        w_in,
        w_out.T,
        gain_one,
        shift_one,
        gain_two,
        shift_two,
        bias_in.reshape(1, -1),
        bias_out,
        depth_weights,
        starts,
        jnp.asarray(cos_np.T.copy()),
        jnp.asarray(sin_np.T.copy()),
    )

    steps = 2
    part = rows // steps
    sizes = (
        [(shard, width)] * 3
        + [(width, shard), (shard, features), (shard, features)]
        + [(features,)] * 4
        + [(1, 4 * features), (features,), (1, 5)]
    )

    def fixed(size):
        return pl.BlockSpec(size, lambda i: (0,) * len(size))

    by_rows = pl.BlockSpec((part, features), lambda i: (i, 0))
    outs = pl.pallas_call(
        functools.partial(spread_body, width),
        grid=(steps,),
        out_shape=[
            shape((rows, features), BF),
            shape((rows, features), F32),
            shape((4, rows, features), F32),
        ]
        + [shape(size, F32) for size in sizes],
        in_specs=[by_rows] * 3 + [fixed((3, shard, features)), fixed((16, features)), smem],
        out_specs=[by_rows] * 2
        + [pl.BlockSpec((4, part, features), lambda i: (0, i, 0))]
        + [fixed(size) for size in sizes],
        compiler_params=pltpu.CompilerParams(vmem_limit_bytes=60 * 1024 * 1024),
    )(cotangent, layer_out, grad_tokens, packed, sums, depth_weights)
    return (*outs[:8], outs[8].T, *outs[9:13], outs[13].reshape(-1), outs[14], outs[15].reshape(-1))


def per_device(*arrays):
    rows, features = arrays[0].shape
    shard, width = arrays[4].shape
    dp = lax.axis_size("dp")
    fits = (
        shard % 16 == 0
        and dp % 4 == 0
        and lax.axis_size("tensor") == 4
        and arrays[3].shape[0] == 2
        and arrays[8].shape[1] == features
        and 4 * width == features
        and shard * dp == features
    )
    return fused_device(*arrays) if fits else plain_device(*arrays)


def solution(mesh):
    in_specs = (
        P(("dp", "tensor"), None),
        P(None, ("dp", "tensor"), None),
        P(("dp", "tensor"), None),
        P("dp", None),
        P("dp", "tensor"),
        P("dp", "tensor"),
        P("dp", "tensor"),
        P("tensor", "dp"),
        P("dp", "tensor"),
        P("tensor", "dp"),
        P(),
        P(),
        P(),
        P(),
        P(),
        P(),
        P(),
    )
    out_specs = (
        P(("dp", "tensor"), None),
        P(("dp", "tensor"), None),
        P(None, ("dp", "tensor"), None),
        P("dp", "tensor"),
        P("dp", "tensor"),
        P("dp", "tensor"),
        P("tensor", "dp"),
        P("dp", "tensor"),
        P("tensor", "dp"),
        P(),
        P(),
        P(),
        P(),
        P(),
        P(),
        P(),
    )
    return jax.shard_map(
        per_device, mesh=mesh, in_specs=in_specs, out_specs=out_specs, check_vma=False
    )
```

```python
import functools
import math

import jax
import jax.numpy as jnp
import numpy as np
from jax import lax
from jax.experimental import pallas as pl
from jax.experimental.pallas import tpu as pltpu
from jax.sharding import PartitionSpec as P

HEAD_DIM = 64
PIECE = 256


EPSILON = 1e-05
NEGATIVE = -1e30


def layer_norm(values, gain, shift):
    centre = values - jnp.mean(values, axis=-1, keepdims=True)
    spread = jnp.mean(centre * centre, axis=-1, keepdims=True)
    return centre * lax.rsqrt(spread + EPSILON) * gain + shift


def tables(seq_length, head_size):
    half_dim = head_size // 2
    frequency = jnp.exp(
        -jnp.log(10000.0) * jnp.arange(half_dim, dtype=jnp.float32) * 2.0 / head_size
    )
    angles = jnp.arange(seq_length, dtype=jnp.float32)[:, None] * frequency[None, :]
    return (jnp.cos(angles), jnp.sin(angles))


def rotate(values, cosine_table, sine_table):
    half_dim = values.shape[-1] // 2
    front_half = values[..., :half_dim]
    back_half = values[..., half_dim:]
    cosines = cosine_table[:, None, :]
    sine_rows = sine_table[:, None, :]
    return jnp.concatenate(
        [
            front_half * cosines - back_half * sine_rows,
            back_half * cosines + front_half * sine_rows,
        ],
        axis=-1,
    )


def allowed_mask(starts, seq_length, piece_size):
    position = jnp.arange(seq_length, dtype=jnp.int32)
    inside = (position[None, None, :] >= starts[:, :, None]) & (
        position[None, None, :] < starts[:, :, None] + piece_size
    )
    jointly = jnp.any(inside[:, :, :, None] & inside[:, :, None, :], axis=1)
    return jointly | (position[None, :, None] >= position[None, None, :])


def gelu_tanh(values):
    return jax.nn.gelu(values, approximate=True)


def right_transposed(matrix, weight):
    return lax.dot_general(
        matrix, weight, (((1,), (1,)), ((), ())), preferred_element_type=jnp.float32
    )


def left_transposed(matrix, other):
    return lax.dot_general(
        matrix, other, (((0,), (0,)), ((), ())), preferred_element_type=jnp.float32
    )


def attend_forward(query, key_rows, value_rows, allowed, score_scale):

    def one_sequence(entries):
        query_seq, key_seq, value_seq, allowed_seq = entries
        scores = (
            jnp.einsum("qhd,khd->hqk", query_seq, key_seq, preferred_element_type=jnp.float32)
            * score_scale
        )
        scores = jnp.where(allowed_seq[None], scores, NEGATIVE)
        highest = jnp.max(scores, axis=-1, keepdims=True)
        powers = jnp.exp(scores - highest)
        row_total = jnp.sum(powers, axis=-1, keepdims=True)
        attention = (powers / row_total).astype(jnp.bfloat16)
        mixed_rows = jnp.einsum(
            "hqk,khd->qhd", attention, value_seq, preferred_element_type=jnp.float32
        )
        return (mixed_rows.astype(jnp.bfloat16), highest + jnp.log(row_total))

    return lax.map(one_sequence, (query, key_rows, value_rows, allowed))


def attend_backward(query, key_rows, value_rows, grad_mixed, log_totals, allowed, score_scale):

    def one_sequence(entries):
        query_seq, key_seq, value_seq, grad_seq, log_seq, allowed_seq = entries
        scores = (
            jnp.einsum("qhd,khd->hqk", query_seq, key_seq, preferred_element_type=jnp.float32)
            * score_scale
        )
        scores = jnp.where(allowed_seq[None], scores, NEGATIVE)
        attention = jnp.exp(scores - log_seq)
        grad_value = jnp.einsum(
            "hqk,qhd->khd",
            attention.astype(jnp.bfloat16),
            grad_seq,
            preferred_element_type=jnp.float32,
        )
        grad_attention = jnp.einsum(
            "qhd,khd->hqk", grad_seq, value_seq, preferred_element_type=jnp.float32
        )
        row_delta = jnp.sum(attention * grad_attention, axis=-1, keepdims=True)
        grad_scores = (attention * (grad_attention - row_delta)).astype(jnp.bfloat16)
        grad_query = (
            jnp.einsum("hqk,khd->qhd", grad_scores, key_seq, preferred_element_type=jnp.float32)
            * score_scale
        )
        grad_key = (
            jnp.einsum("hqk,qhd->khd", grad_scores, query_seq, preferred_element_type=jnp.float32)
            * score_scale
        )
        return (grad_query, grad_key, grad_value.astype(jnp.bfloat16))

    return lax.map(one_sequence, (query, key_rows, value_rows, grad_mixed, log_totals, allowed))


def plain_device(
    tokens,
    stack,
    cotangent,
    starts,
    w_query,
    w_key,
    w_value,
    w_output,
    w_in,
    w_out,
    gain_one,
    shift_one,
    gain_two,
    shift_two,
    bias_in,
    bias_out,
    depth_weights,
):
    rows_here = tokens.shape[0]
    features = tokens.shape[1]
    groups = lax.axis_size("tensor")
    position = lax.axis_index("tensor")
    seq_count = starts.shape[0]
    seq_length = rows_here * groups // seq_count
    score_scale = 1.0 / math.sqrt(HEAD_DIM)
    local_heads = w_query.shape[1] // HEAD_DIM
    hidden = w_in.shape[1]
    cosine_table, sine_table = tables(seq_length, HEAD_DIM)
    allowed = allowed_mask(starts, seq_length, PIECE)

    def to_heads(matrix):
        return matrix.reshape(seq_count, seq_length, local_heads, HEAD_DIM)

    def from_heads(blocks):
        return blocks.reshape(seq_count * seq_length, local_heads * HEAD_DIM)

    def share_rows(local_rows):
        return lax.all_gather(local_rows, "tensor", axis=0, tiled=True)

    def share_grad(local_rows):
        return lax.all_gather(local_rows, "tensor", axis=0, tiled=True)

    def merge_rows(source, weight):
        return lax.psum_scatter(
            jnp.dot(source, weight, preferred_element_type=jnp.float32),
            "tensor",
            scatter_dimension=0,
            tiled=True,
        )

    def return_rows(pairs):
        running = jnp.zeros((lax.axis_size("tensor") * rows_here, features), jnp.float32)
        for source, weight in pairs:
            running = running + right_transposed(source, weight)
        return lax.psum_scatter(running, "tensor", scatter_dimension=0, tiled=True)

    query_w, key_w, value_w, output_w = (
        lax.all_gather(w_query, "dp", axis=0, tiled=True),
        lax.all_gather(w_key, "dp", axis=0, tiled=True),
        lax.all_gather(w_value, "dp", axis=0, tiled=True),
        lax.all_gather(w_output, "dp", axis=1, tiled=True),
    )
    inner_w, outer_w = (
        lax.all_gather(w_in, "dp", axis=0, tiled=True),
        lax.all_gather(w_out, "dp", axis=1, tiled=True),
    )
    token_rows = tokens.astype(jnp.float32)
    normed_one = layer_norm(token_rows, gain_one, shift_one).astype(jnp.bfloat16)
    normed_all = share_rows(normed_one)
    query = rotate(
        to_heads(jnp.dot(normed_all, query_w, preferred_element_type=jnp.float32)),
        cosine_table,
        sine_table,
    ).astype(jnp.bfloat16)
    key_rows = rotate(
        to_heads(jnp.dot(normed_all, key_w, preferred_element_type=jnp.float32)),
        cosine_table,
        sine_table,
    ).astype(jnp.bfloat16)
    value_rows = to_heads(jnp.dot(normed_all, value_w, preferred_element_type=jnp.float32)).astype(
        jnp.bfloat16
    )
    mixed_heads, log_totals = attend_forward(query, key_rows, value_rows, allowed, score_scale)
    mixed_flat = from_heads(mixed_heads)
    middle = token_rows + merge_rows(mixed_flat, output_w)
    normed_two = layer_norm(middle, gain_two, shift_two).astype(jnp.bfloat16)
    second_all = share_rows(normed_two)
    bias_slice = lax.dynamic_slice_in_dim(bias_in, position * hidden, hidden)
    pre_act = jnp.dot(second_all, inner_w, preferred_element_type=jnp.float32) + bias_slice
    activated = gelu_tanh(pre_act).astype(jnp.bfloat16)
    block_out = middle + merge_rows(activated, outer_w) + bias_out
    averaged = depth_weights[4] * block_out
    for layer_index in range(4):
        averaged = averaged + depth_weights[layer_index] * stack[layer_index].astype(jnp.float32)
    layer_out = averaged.astype(jnp.bfloat16)
    grad_rows = cotangent.astype(jnp.float32)
    grad_stack = jnp.stack([depth_weights[layer_index] * grad_rows for layer_index in range(4)])
    depth_terms = jnp.stack(
        [jnp.sum(stack[layer_index].astype(jnp.float32) * grad_rows) for layer_index in range(4)]
        + [jnp.sum(block_out * grad_rows)]
    )
    grad_block = depth_weights[4] * grad_rows
    grad_bias_out = jnp.sum(grad_block, axis=0)
    grad_sent = share_grad(grad_block.astype(jnp.bfloat16))
    grad_outer = left_transposed(activated, grad_sent)
    grad_act = right_transposed(grad_sent, outer_w)
    grad_pre = jax.vjp(gelu_tanh, pre_act)[1](grad_act)[0].astype(jnp.bfloat16)
    grad_bias_slice = jnp.sum(grad_pre.astype(jnp.float32), axis=0)
    bias_full = lax.dynamic_update_slice_in_dim(
        jnp.zeros((bias_in.shape[0],), jnp.float32), grad_bias_slice, position * hidden, 0
    )
    grad_inner = left_transposed(second_all, grad_pre)
    grad_norm_two = return_rows(((grad_pre, inner_w),))
    layer_two = jax.vjp(layer_norm, middle, gain_two, shift_two)[1](grad_norm_two)
    grad_middle = grad_block + layer_two[0]
    grad_attn_sent = share_grad(grad_middle.astype(jnp.bfloat16))
    grad_output_w = left_transposed(mixed_flat, grad_attn_sent)
    grad_mixed = right_transposed(grad_attn_sent, output_w).astype(jnp.bfloat16)
    grad_query, grad_key, grad_value = attend_backward(
        query, key_rows, value_rows, to_heads(grad_mixed), log_totals, allowed, score_scale
    )
    grad_query = from_heads(rotate(grad_query, cosine_table, -sine_table)).astype(jnp.bfloat16)
    grad_key = from_heads(rotate(grad_key, cosine_table, -sine_table)).astype(jnp.bfloat16)
    grad_value = from_heads(grad_value)
    grad_query_w = left_transposed(normed_all, grad_query)
    grad_key_w = left_transposed(normed_all, grad_key)
    grad_value_w = left_transposed(normed_all, grad_value)
    grad_norm_one = return_rows(((grad_query, query_w), (grad_key, key_w), (grad_value, value_w)))
    layer_one = jax.vjp(layer_norm, token_rows, gain_one, shift_one)[1](grad_norm_one)
    grad_tokens = grad_middle + layer_one[0]
    grad_w_query, grad_w_key, grad_w_value, grad_w_output, grad_w_in, grad_w_out = (
        lax.psum_scatter(grad_query_w, "dp", scatter_dimension=0, tiled=True),
        lax.psum_scatter(grad_key_w, "dp", scatter_dimension=0, tiled=True),
        lax.psum_scatter(grad_value_w, "dp", scatter_dimension=0, tiled=True),
        lax.psum_scatter(grad_output_w, "dp", scatter_dimension=1, tiled=True),
        lax.psum_scatter(grad_inner, "dp", scatter_dimension=0, tiled=True),
        lax.psum_scatter(grad_outer, "dp", scatter_dimension=1, tiled=True),
    )
    summed = lax.psum(
        (
            layer_one[1],
            layer_one[2],
            layer_two[1],
            layer_two[2],
            bias_full,
            grad_bias_out,
            depth_terms,
        ),
        ("dp", "tensor"),
    )
    return (
        layer_out,
        grad_tokens,
        grad_stack,
        grad_w_query,
        grad_w_key,
        grad_w_value,
        grad_w_output,
        grad_w_in,
        grad_w_out,
        summed[0],
        summed[1],
        summed[2],
        summed[3],
        summed[4],
        summed[5],
        summed[6],
    )


BF = jnp.bfloat16
F32 = jnp.float32
MESH = pl.DeviceIdType.MESH
BLOCK = 256
EXPONENT_SCALE = math.log2(math.e) / math.sqrt(HEAD_DIM)


PLAN = (
    (
        ("A", 0, 0, 128),
        ("A", 0, 128, 128),
        ("A", 0, 256, 128),
        ("A", 0, 384, 128),
        ("A", 0, 512, 128),
        ("B", 0, 640, 128),
        ("A", 1, 0, 256),
        ("A", 1, 256, 256),
        ("B", 1, 512, 128),
        ("B", 1, 640, 128),
        ("A", 2, 0, 256),
        ("B", 2, 256, 128),
        ("A", 2, 384, 128),
        ("B", 2, 512, 128),
        ("B", 2, 640, 128),
    ),
    (
        ("A", 2, 0, 256),
        ("B", 2, 256, 128),
        ("A", 2, 384, 256),
        ("B", 2, 640, 128),
        ("B", 1, 0, 128),
        ("A", 1, 128, 128),
        ("B", 1, 256, 128),
        ("A", 1, 384, 256),
        ("B", 1, 640, 128),
        ("A", 0, 0, 128),
        ("A", 0, 128, 128),
        ("A", 0, 256, 128),
        ("A", 0, 384, 128),
        ("A", 0, 512, 128),
        ("B", 0, 640, 128),
    ),
    {
        "norm": ((1, 0, 0), (1, 5, 0), (1, 8, 0), (1, 9, 0),),
        "mask0": ((1, 1, 0), (1, 11, 0), (1, 13, 0), (1, 14, 0),),
        "mask2": ((1, 2, 0),),
        "mask3": ((1, 0, 1),),
        "stack2": ((1, 3, 0),),
        "stack3": ((1, 1, 1),),
        "proj0.0": ((1, 4, 0), (1, 0, 2), (1, 2, 1), (1, 5, 1), (1, 1, 2), (1, 3, 1), (1, 4, 1), (1, 0, 3), (1, 6, 0), (1, 2, 2), (1, 5, 2), (1, 1, 3), (1, 7, 0), (1, 3, 2), (1, 6, 1), (1, 2, 3), (1, 8, 1), (1, 5, 3), (1, 4, 2),),
        "att0.0": ((1, 7, 1),),
        "att0.1": ((1, 3, 3),),
        "att0.2": ((1, 9, 1),),
        "att0.3": ((1, 6, 2),),
        "att2.0": ((1, 8, 2),),
        "att2.2": ((1, 4, 3), (1, 10, 0),),
        "att3.0": ((1, 9, 2),),
        "att3.2": ((1, 11, 1),),
        "att3.3": ((1, 7, 2), (1, 8, 3),),
        "att5.0": ((1, 10, 1),),
        "att5.2": ((1, 6, 3), (1, 12, 0),),
        "r.other": ((1, 9, 3),),
        "r.low": ((1, 13, 1),),
        "ln2": ((1, 11, 2),),
        "in0": ((1, 10, 2), (1, 14, 1),),
        "in1": ((1, 12, 1), (1, 7, 3),),
        "in3": ((1, 11, 3), (1, 13, 2),),
        "dc2": ((1, 14, 2),),
        "dc3": ((1, 12, 2),),
        "bh0": ((1, 13, 3), (1, 10, 3), (0, 1, 0), (0, 0, 0), (1, 14, 3),),
        "bh1": ((1, 12, 3), (0, 3, 0),),
        "bh2": ((0, 1, 1),),
        "bh3": ((0, 2, 0),),
        "lnb2": ((0, 0, 1), (0, 3, 1),),
        "db3": ((0, 1, 2),),
        "go": ((0, 4, 0), (0, 5, 0),),
        "dwo": ((0, 0, 2),),
        "ab0.0": ((0, 1, 3), (0, 2, 1),),
        "ab0.1": ((0, 3, 2),),
        "ab0.2": ((0, 7, 0),),
        "ab1.0": ((0, 4, 1),),
        "ab1.1": ((0, 3, 3), (0, 0, 3), (0, 5, 1),),
        "ab1.3": ((0, 6, 0),),
        "ab2.0": ((0, 2, 2),),
        "ab2.3": ((0, 4, 2),),
        "da0": ((0, 5, 2), (0, 8, 0),),
        "ab3.0": ((0, 9, 0),),
        "ab3.1": ((0, 4, 3), (0, 6, 1),),
        "ab3.2": ((0, 2, 3), (0, 7, 1),),
        "ab3.3": ((0, 10, 0),),
        "ab4.0": ((0, 5, 3),),
        "ab4.2": ((0, 8, 1),),
        "ab4.3": ((0, 14, 0),),
        "ab5.0": ((0, 6, 2), (0, 11, 0),),
        "ab5.3": ((0, 7, 2),),
        "da2": ((0, 6, 3),),
        "da3": ((0, 8, 2),),
        "bp0": ((0, 9, 1), (0, 12, 0),),
        "bp1": ((0, 10, 1), (0, 14, 1),),
        "lnb1": ((0, 7, 3), (0, 8, 3), (0, 9, 2), (0, 11, 1), (0, 13, 0),),
        "vs0": ((0, 10, 2), (0, 12, 1), (0, 14, 2),),
        "vs1": ((0, 9, 3), (0, 11, 2), (0, 13, 1),),
        "out1": ((0, 10, 3), (0, 12, 2), (0, 14, 3),),
        "fin": ((0, 11, 3), (0, 13, 2),),
        "vs2": ((0, 12, 3),),
        "end": ((0, 13, 3),),
    },
)


def dot(left, right, left_axis, right_axis):
    return lax.dot_general(
        left, right, (((left_axis,), (right_axis,)), ((), ())), preferred_element_type=F32
    )


def norm_parts(values):
    centre = values - jnp.mean(values, axis=-1, keepdims=True)
    inverse = lax.rsqrt(jnp.mean(centre * centre, axis=-1, keepdims=True) + EPSILON)
    return centre * inverse, inverse


def norm_back(grad, gain, unit, inverse):
    scaled = grad * gain
    first = jnp.mean(scaled, axis=-1, keepdims=True)
    second = jnp.mean(scaled * unit, axis=-1, keepdims=True)
    return inverse * (scaled - first - unit * second)


def gelu_pair(values):
    root = math.sqrt(2.0 / math.pi)
    square = values * values
    bend = jnp.tanh(root * values * (1.0 + 0.044715 * square))
    half = 0.5 * (1.0 + bend)
    slope = half + 0.5 * root * values * (1.0 - bend * bend) * (1.0 + 3 * 0.044715 * square)
    return values * half, slope


def column_sum(values):
    return jnp.sum(values, axis=0, keepdims=True)


def rotary_tables(length):
    half = HEAD_DIM // 2
    frequency = np.exp(-np.log(10000.0) * np.arange(half) * 2.0 / HEAD_DIM)
    angles = np.arange(length)[:, None] * frequency[None, :]
    return np.cos(angles).astype(np.float32), np.sin(angles).astype(np.float32)


def fused_body(
    nz,
    rows,
    features,
    shard,
    plan,
    tokens_hbm,
    cotangent_hbm,
    stack,
    w_query,
    w_key,
    w_value,
    w_output,
    w_in,
    w_out,
    gain_one,
    shift_one,
    gain_two,
    shift_two,
    bias_in,
    bias_out,
    depth,
    starts,
    cosine_t,
    sine_t,
    layer_hbm,
    grad_tokens_hbm,
    grad_packed,
    grad_vectors,
    G,
    D,
    RY,
    RX,
    RZ,
    A,
    C,
    GM,
    K,
    V,
    KT,
    QT,
    OT,
    LS,
    MB,
    Z,
    GP,
    GOT,
    GT,
    WO,
    R32,
    AVG,
    SR,
    SB,
    XG,
    VS,
    V8,
    VI,
    VP,
    VO,
    VL,
    VM,
    GKA,
    GVA,
    tokens,
    cotangent,
    cosine,
    sine,
    BI,
    grad_tokens,
    local_sem,
    ag_send,
    ag_recv,
    rs_send,
    rs_recv,
    sib_send,
    sib_recv,
    vec_send,
    vec_recv,
    late_send,
    late_recv,
):
    length = 2 * rows
    heads = 3
    width = heads * HEAD_DIM
    gathers, reduces, schedule = plan
    dp = lax.axis_index("dp")
    t = lax.axis_index("tensor")
    z = dp // 2
    x = lax.rem(dp, 2)
    low = lax.rem(t, 2)
    pair = t // 2
    other = 1 - low
    sib = (dp, t + 1 - 2 * low)
    ypeer = (dp, lax.rem(t + 2, 4))
    xpeer = (dp + 1 - 2 * x, t)

    def zpeer(j):
        return (lax.rem(z + j, nz) * 2 + x, t)

    def near_place(j):
        side = x + (1 - 2 * x) * (j // 4)
        upper = pair + (1 - 2 * pair) * ((j // 2) % 2)
        lower = low + (1 - 2 * low) * (j % 2)
        return side, 2 * upper + lower

    def near(j):
        side, place = near_place(j)
        return 2 * z + side, place

    def near_slot(j):
        side, place = near_place(j)
        return 4 * side + place

    def remote(src, dst, send, recv, peer):
        return pltpu.make_async_remote_copy(
            src_ref=src, dst_ref=dst, send_sem=send, recv_sem=recv,
            device_id=peer, device_id_type=MESH,
        )

    everything = slice(None)

    def gather_copies(f, stage):
        kind, k, first, count = gathers[f]
        cols = pl.ds(first, count)
        axis = ("zxy" if kind == "A" else "yzx")[stage]
        if axis == "z":
            slot = 0 if kind == "A" else everything
            mine = G.at[k, slot, z, x, :, cols]
            sent, taken = [], []
            for j in range(nz - 1):
                sems = (ag_send.at[f, j], ag_recv.at[f, j], zpeer(j + 1))
                sent.append(lambda mine=mine, sems=sems: remote(mine, mine, *sems))
                from_z = lax.rem(z + nz - 1 - j, nz)
                taken.append(
                    lambda mine=mine, sems=sems, from_z=from_z: remote(
                        mine, G.at[k, slot, from_z, x, :, cols], *sems
                    )
                )
            return sent, taken
        if axis == "x":
            slot = 0 if kind == "A" else everything
            ref = G.at[k, slot, :, x, :, cols]
            copy = lambda: remote(ref, ref, ag_send.at[f, nz - 1], ag_recv.at[f, nz - 1], xpeer)
            return [copy], [copy]
        sems = (ag_send.at[f, nz], ag_recv.at[f, nz], ypeer)
        if kind == "A":
            copy = lambda: remote(G.at[k, 0, :, :, :, cols], G.at[k, 1, :, :, :, cols], *sems)
        else:
            copy = lambda: remote(G.at[k, 0, z, x, :, cols], G.at[k, 1, z, x, :, cols], *sems)
        return [copy], [copy]

    def gather_step(f, stage):
        if stage == 4:
            for past in range(3):
                for copy in gather_copies(f, past)[0]:
                    copy().wait_send()
            return
        awaited = {1: 0, 2: 1, 3: 2, 5: 1}.get(stage)
        if awaited is not None:
            for copy in gather_copies(f, awaited)[1]:
                copy().wait_recv()
        started = {0: 0, 1: 1, 2: 2, 6: 2}.get(stage)
        if started is not None:
            for copy in gather_copies(f, started)[0]:
                copy().start()

    def reduce_copies(f, stage):
        kind, k, first, count = reduces[f]
        cols = pl.ds(first, count)
        axis = ("yxz" if kind == "A" else "xzy")[stage]

        def sems(n):
            return rs_send.at[f, n], rs_recv.at[f, n]

        if axis == "z":
            slot = 0 if kind == "A" else everything
            land = 0 if kind == "A" else everything
            return [
                lambda j=j: remote(
                    D.at[k, slot, lax.rem(z + j + 1, nz), x, :, cols],
                    RZ.at[k, j, land, :, cols], *sems(j), zpeer(j + 1),
                )
                for j in range(nz - 1)
            ]
        if axis == "x":
            if kind == "A":
                return [
                    lambda: remote(
                        D.at[k, 0, :, 1 - x, :, cols], RX.at[k, :, :, cols], *sems(nz - 1), xpeer
                    )
                ]
            return [
                lambda: remote(
                    D.at[k, :, :, 1 - x, :, cols], RY.at[k, :, :, :, cols], *sems(nz - 1), xpeer
                )
            ]
        if kind == "A":
            return [
                lambda side=side, n=n: remote(
                    D.at[k, 1, :, side, :, cols], RY.at[k, side, :, :, cols], *sems(nz + n), ypeer
                )
                for n, side in enumerate((1 - x, x))
            ]
        return [lambda: remote(D.at[k, 1, z, x, :, cols], RX.at[k, 0, :, cols], *sems(nz), ypeer)]

    def reduce_step(f, stage):
        kind, k, first, count = reduces[f]
        cols = pl.ds(first, count)
        if stage == 4:
            for past in range(3):
                for copy in reduce_copies(f, past):
                    copy().wait_send()
            return
        before = reduce_copies(f, stage - 1) if stage else []
        after = reduce_copies(f, stage) if stage < 3 else []

        def add(target, source):
            target[...] = (target[...].astype(F32) + source[...].astype(F32)).astype(BF)

        if kind == "A" and stage == 1:
            before[0]().wait_recv()
            add(D.at[k, 0, :, 1 - x, :, cols], RY.at[k, 1 - x, :, :, cols])
            after[0]().start()
            before[1]().wait_recv()
            add(D.at[k, 0, :, x, :, cols], RY.at[k, x, :, :, cols])
            return
        for copy in before:
            copy().wait_recv()
        if kind == "A" and stage == 2:
            add(D.at[k, 0, :, x, :, cols], RX.at[k, :, :, cols])
        elif kind == "B" and stage == 1:
            add(D.at[k, :, :, x, :, cols], RY.at[k, :, :, :, cols])
        elif kind == "B" and stage == 2:
            total = D[k, :, z, x, :, cols].astype(F32)
            for j in range(nz - 1):
                total = total + RZ[k, j, :, :, cols].astype(F32)
            D[k, 1, z, x, :, cols] = total[1].astype(BF)
            grad_packed[k, :, cols] = total[0]
        elif kind == "A" and stage == 3:
            total = D[k, 0, z, x, :, cols].astype(F32)
            for j in range(nz - 1):
                total = total + RZ[k, j, 0, :, cols].astype(F32)
            grad_packed[k, :, cols] = total
        elif kind == "B" and stage == 3:
            grad_packed[k, :, cols] = grad_packed[k, :, cols] + RX[k, 0, :, cols].astype(F32)
        for copy in after:
            copy().start()

    def drain(k):
        for f in range(len(gathers)):
            if gathers[f][1] == k:
                gather_step(f, 4)

    def tick(name):
        for gather, flow, stage in schedule.get(name, ()):
            if gather:
                gather_step(flow, stage)
            else:
                reduce_step(flow, stage)

    def tick_at(prefix, index, count, suffix=""):
        for i in range(count):
            name = prefix + str(i) + suffix
            if schedule.get(name):

                @pl.when(index == i)
                def _(name=name):
                    tick(name)

    def sib_copy(n, src, dst):
        return remote(src, dst, sib_send.at[n], sib_recv.at[n], sib)

    send_a = sib_copy(0, A.at[low], A.at[low])
    take_a = sib_copy(0, A.at[low], A.at[other])
    send_gm = sib_copy(1, GM.at[low], GM.at[low])
    take_gm = sib_copy(1, GM.at[low], GM.at[other])
    half_rows = rows // 2
    part_r = [
        sib_copy(n, SB.at[pl.ds(i * half_rows, half_rows)], XG.at[pl.ds(i * half_rows, half_rows)])
        for i, n in enumerate((2, 8))
    ]
    send_c = sib_copy(3, C.at[low], C.at[low])
    take_c = sib_copy(3, C.at[low], C.at[other])
    part_g = sib_copy(4, SB, XG)
    send_gl = sib_copy(5, GM.at[low], GM.at[low])
    take_gl = sib_copy(5, GM.at[low], GM.at[other])
    part_b = sib_copy(6, SB, XG)
    part_a = sib_copy(7, SB, XG)

    loads = [
        pltpu.make_async_copy(tokens_hbm, tokens, local_sem.at[0]),
        pltpu.make_async_copy(cotangent_hbm, cotangent, local_sem.at[1]),
        pltpu.make_async_copy(stack, Z, local_sem.at[2]),
    ]
    for load in loads:
        load.start()
    barrier = pltpu.get_barrier_semaphore()
    partners = [near(j) for j in range(1, 8)] + [zpeer(j + 1) for j in range(nz - 1)]
    for peer in partners:
        pl.semaphore_signal(barrier, inc=1, device_id=peer, device_id_type=MESH)
    G[0, 0, z, x] = jnp.concatenate(
        [w_query[...], w_key[...], w_value[...], w_output[...].T], axis=1
    )
    G[1, 0, z, x] = w_in[...]
    G[2, 0, z, x] = w_out[...]
    pl.semaphore_wait(barrier, len(partners))
    tick("norm")

    gain_one, shift_one, gain_two, shift_two, bias_out = (
        ref[...].reshape(1, features)
        for ref in (gain_one, shift_one, gain_two, shift_two, bias_out)
    )
    piece = 128
    pieces = rows // piece

    def chunk(i):
        return pl.ds(i * piece if isinstance(i, int) else pl.multiple_of(i * piece, piece), piece)

    def over_pieces(step, carry):
        for i in range(pieces):
            carry = step(i, carry)
        return carry

    loads[0].wait()
    loads[1].wait()

    def first_norm(i, carry):
        unit, _ = norm_parts(tokens[chunk(i), :].astype(F32))
        A[low, chunk(i), :] = (unit * gain_one + shift_one).astype(BF)
        GM[low, chunk(i), :] = (depth[4] * cotangent[chunk(i), :].astype(F32)).astype(BF)
        return carry

    lax.fori_loop(0, pieces, first_norm, 0)
    send_a.start()
    send_gm.start()
    for n in range(4):
        BI[n : n + 1, :] = bias_in[:, n * features : (n + 1) * features]
    cosine[...] = jnp.concatenate([cosine_t[...]] * 4, axis=0).T
    sine[...] = jnp.concatenate([-sine_t[...], sine_t[...]] * 2, axis=0).T

    s0, s1 = starts[pair, 0], starts[pair, 1]
    blocks = length // BLOCK
    for block in range(blocks):
        tick("mask" + str(block))
        key = block * BLOCK + lax.broadcasted_iota(jnp.int32, (2 * BLOCK, BLOCK), 0)
        query = block * BLOCK + lax.broadcasted_iota(jnp.int32, (2 * BLOCK, BLOCK), 1)
        fine = key <= query
        for s in (s0, s1):
            fine = fine | ((key >= s) & (key < s + PIECE) & (query >= s) & (query < s + PIECE))
        MB[block] = jnp.where(fine, 0.0, NEGATIVE)
    VS[...] = jnp.zeros_like(VS)
    for s in range(2):
        for h in range(heads):
            V[heads * s + h, :, HEAD_DIM:] = jnp.where(
                lax.broadcasted_iota(jnp.int32, (length, HEAD_DIM), 1) == 0, 1.0, 0.0
            ).astype(BF)

    loads[2].wait()

    def earlier(i, sums):
        tick_at("stack", i, pieces)
        grad = cotangent[chunk(i), :].astype(F32)
        mean = jnp.zeros((piece, features), F32)
        new = [sums[0] + column_sum(grad)]
        for k in range(4):
            layer = Z[k, chunk(i), :].astype(F32)
            mean = mean + depth[k] * layer
            new.append(sums[k + 1] + column_sum(layer * grad))
        AVG[chunk(i), :] = mean
        return tuple(new)

    zero_row = jnp.zeros((1, features), F32)
    sums = lax.fori_loop(0, pieces, earlier, (zero_row,) * 5)
    VS[4:5, :] = depth[4] * sums[0]
    for k in range(4):
        VS[5 + k : 6 + k, :] = sums[k + 1]

    take_a.wait_recv()

    def whole(ref, *index):
        value = ref[index]
        return value.reshape(value.shape[-4] * value.shape[-3] * value.shape[-2], value.shape[-1])

    lane = lax.broadcasted_iota(jnp.int32, (rows, 128), 1)
    front = lax.rem(lane, HEAD_DIM) < HEAD_DIM // 2

    def project(slot):
        for half in range(2):
            tick_at("proj", slot, 2, "." + str(half))
            weight = whole(G, 0, slot, everything, everything, everything, slice(0, 640))
            span = slice(half * rows, (half + 1) * rows)
            result = dot(A[half], weight, 1, 0)
            turned = []
            for tile in range(3):
                part = result[:, tile * 128 : (tile + 1) * 128]
                partner = jnp.where(front, pltpu.roll(part, 96, 1), pltpu.roll(part, 32, 1))
                turned.append((part * cosine[span, :] + partner * sine[span, :]).astype(BF))
            for h in range(heads):
                n = heads * slot + h
                at = h * HEAD_DIM
                QT[n, :, span] = turned[at // 128][:, at % 128 : at % 128 + HEAD_DIM].T
                at = width + h * HEAD_DIM
                key = turned[at // 128][:, at % 128 : at % 128 + HEAD_DIM]
                K[n, span, :] = key
                KT[n, :, span] = key.T
                at = 2 * width + h * HEAD_DIM
                V[n, span, :HEAD_DIM] = result[:, at : at + HEAD_DIM].astype(BF)

    def span_of(block):
        lo = block * BLOCK
        return lo, min(lo + 2 * BLOCK, length)

    def attend(n, carry):
        @pl.when(lax.rem(n, heads) == 0)
        def _():
            project(n // heads)

        def scores(block):
            lo, top = span_of(block)
            return dot(K[n, 0:top, :], QT[n, :, lo : lo + BLOCK], 1, 0)

        ahead = scores(0)
        for block in range(blocks):
            tick_at("att", n, 2 * heads, "." + str(block))
            lo, top = span_of(block)
            half, at = lo // rows, lo % rows
            score = ahead * EXPONENT_SCALE
            if block + 1 < blocks:
                ahead = scores(block + 1)
            tail = score[lo:] + MB[block, 0 : top - lo, :]
            score = jnp.concatenate([score[:lo], tail], axis=0) if lo else tail
            highest = jnp.max(score, axis=0, keepdims=True)
            power = jnp.exp2(score - highest).astype(BF)
            mixed = dot(V[n, 0:top, :], power, 0, 0)
            total = mixed[HEAD_DIM : HEAD_DIM + 1, :]
            OT[half, n, :, at : at + BLOCK] = (mixed[:HEAD_DIM, :] / total).astype(BF)
            LS[pl.ds(n, 1), lo : lo + BLOCK] = highest + jnp.log2(total)
        return carry

    lax.fori_loop(0, 2 * heads, attend, 0)
    tick("wo")
    for slot in range(2):
        flipped = whole(G, 0, slot, everything, everything, everything, slice(512, 768)).T
        WO[slot * width : (slot + 1) * width, :] = flipped[64:256, :]

    def mixed_rows(half):
        return OT[half].reshape(2 * width, rows)

    tick("r.other")
    for i in range(2):
        span = slice(i * half_rows, (i + 1) * half_rows)
        left = OT[other, :, :, span].reshape(2 * width, half_rows)
        SB[span, :] = dot(left, WO[...], 0, 0).astype(BF)
        part_r[i].start()
    tick("r.low")
    R32[...] = dot(mixed_rows(low), WO[...], 0, 0)
    for copy in part_r:
        copy.wait_recv()
    tick("ln2")

    def second_norm(i, carry):
        middle = tokens[chunk(i), :].astype(F32) + R32[chunk(i), :] + XG[chunk(i), :].astype(F32)
        R32[chunk(i), :] = middle
        unit, _ = norm_parts(middle)
        C[low, chunk(i), :] = (unit * gain_two + shift_two).astype(BF)
        return carry

    over_pieces(second_norm, 0)
    send_c.start()
    def hidden_bias(slot):
        return BI[pl.ds(lax.rem(t + 2 * slot, 4), 1), :]

    def inner(i, carry):
        tick_at("in", i, 4)

        @pl.when(i == 2)
        def _():
            take_c.wait_recv()

        half, slot = lax.rem(low + i // 2, 2), lax.rem(i, 2)
        pre = dot(C[half], whole(G, 1, slot), 1, 0) + hidden_bias(slot)
        act, slope = gelu_pair(pre)
        Z[2 * slot + half] = act.astype(BF)
        GP[2 * slot + half] = slope.astype(BF)
        return carry

    lax.fori_loop(0, 4, inner, 0)
    take_gm.wait_recv()

    def outer_products(name, k, left, right):
        half_cols = features // 2

        def one(i, carry):
            tick_at(name, i, 4)
            slot, part = 1 - i // 2, lax.rem(i, 2)
            cols = pl.ds(pl.multiple_of(part * half_cols, 128), half_cols)
            value = dot(
                left[:, :, cols].reshape(length, half_cols),
                right[pl.ds(2 * slot, 2)].reshape(length, features),
                0,
                0,
            )
            D[k, slot, pl.ds(part * (nz // 2), nz // 2)] = value.astype(BF).reshape(
                nz // 2, 2, shard, features
            )
            return carry

        lax.fori_loop(0, 4, one, 0)

    outer_products("dc", 2, GM, Z)

    def back(i, carry):
        half = lax.rem(other + i, 2)

        def one(slot, total):
            tick_at("bh", 2 * i + slot, 4)
            grad = dot(GM[half], whole(G, 2, slot), 1, 0)
            total = total + column_sum(grad * Z[2 * slot + half].astype(F32))
            grad = (grad * GP[2 * slot + half].astype(F32)).astype(BF)
            GP[2 * slot + half] = grad
            row = pl.ds(9 + lax.rem(t + 2 * slot, 4), 1)
            VS[row, :] = VS[row, :] + column_sum(grad.astype(F32))
            return total

        carry = lax.fori_loop(0, 2, one, carry)
        tick_at("bi", i, 2)
        grad_tokens[...] = dot(GP[half], whole(G, 1, 0), 1, 1) + dot(
            GP[2 + half], whole(G, 1, 1), 1, 1
        )

        @pl.when(i == 0)
        def _():
            for copy in part_r:
                copy.wait_send()
            SB[...] = grad_tokens[...].astype(BF)
            part_g.start()

        return carry

    drain(0)
    VS[13:14, :] = lax.fori_loop(0, 2, back, zero_row) / depth[4]
    part_g.wait_recv()
    send_gm.wait_send()
    tick("lnb2")

    def second_back(i, carry):
        middle = R32[chunk(i), :]
        unit, inverse = norm_parts(middle)
        grad = grad_tokens[chunk(i), :] + XG[chunk(i), :].astype(F32)
        coming = cotangent[chunk(i), :].astype(F32)
        whole_grad = depth[4] * coming + norm_back(grad, gain_two, unit, inverse)
        grad_tokens[chunk(i), :] = whole_grad
        GM[low, chunk(i), :] = whole_grad.astype(BF)
        return (
            carry[0] + column_sum(grad * unit),
            carry[1] + column_sum(grad),
            carry[2] + column_sum(coming * (middle + bias_out)),
        )

    sums = lax.fori_loop(0, pieces, second_back, (zero_row,) * 3)
    VS[2:3, :] = sums[0]
    VS[3:4, :] = sums[1]
    send_gl.start()
    VS[13:14, :] = VS[13:14, :] + sums[2]

    def vector_step(step):
        mine = near_slot(0)

        def hop(kind, j):
            if kind == 1:
                source, target, peer, sem = VP.at[z], VP.at[z], zpeer(j), 6 + j
            else:
                source = V8.at[near_slot(j)] if kind == 0 else VO.at[mine]
                target = VI.at[mine] if kind == 0 else VO.at[mine]
                peer, sem = near(j), j - 1 + (nz + 6) * (kind // 2)
            return remote(source, target, vec_send.at[sem], vec_recv.at[sem], peer)

        def taken(kind, j):
            if kind == 1:
                target, sem = VP.at[lax.rem(z + nz - j, nz)], 6 + j
            else:
                target = (VI if kind == 0 else VO).at[near_slot(j)]
                sem = j - 1 + (nz + 6) * (kind // 2)
            peer = zpeer(j) if kind == 1 else near(j)
            remote(V8.at[0], target, vec_send.at[sem], vec_recv.at[sem], peer).wait_recv()

        def ends(kind):
            return range(1, nz if kind == 1 else 8)

        if step == 0:
            for n in range(8):
                V8[n] = VS[2 * n : 2 * n + 2, :]
            VI[mine] = V8[mine]
        elif step < 4:
            for j in ends(step - 1):
                taken(step - 1, j)
            if step == 1:
                total = VI[0]
                for n in range(1, 8):
                    total = total + VI[n]
                VP[z] = total
            elif step == 2:
                total = VP[0]
                for n in range(1, nz):
                    total = total + VP[n]
                VO[mine] = total
            else:
                for n in range(8):
                    grad_vectors[2 * n : 2 * n + 2, :] = VO[n]
        else:
            for kind in range(3):
                for j in ends(kind):
                    hop(kind, j).wait_send()
        if step < 3:
            for j in ends(step):
                hop(step, j).start()

    vector_step(0)
    outer_products("db", 1, C, GP)

    drain(1)
    take_gl.wait_recv()
    tick("go")

    def grad_mixed(half, carry):
        GOT[half] = dot(WO[...], GM[half], 1, 1).astype(BF).reshape(2 * heads, HEAD_DIM, rows)
        return carry

    lax.fori_loop(0, 2, grad_mixed, 0)
    tick("dwo")
    for slot in range(2):
        value = sum(
            dot(OT[half, heads * slot : heads * slot + heads].reshape(width, rows), GM[half], 1, 0)
            for half in range(2)
        )
        D[0, slot, :, :, :, 3 * width :] = value.T.astype(BF).reshape(nz, 2, shard, width)

    def unturn(value, span):
        front_half, back_half = value[: HEAD_DIM // 2], value[HEAD_DIM // 2 :]
        cosines, sines = cosine_t[:, span], sine_t[:, span]
        return jnp.concatenate(
            [front_half * cosines + back_half * sines, back_half * cosines - front_half * sines],
            axis=0,
        )

    scale = 1.0 / math.sqrt(HEAD_DIM)

    def attend_back(i, carry):
        slot, h = 1 - i // heads, lax.rem(i, heads)
        n = heads * slot + h

        def place(which):
            return pl.ds(pl.multiple_of(which * width + h * HEAD_DIM, HEAD_DIM), HEAD_DIM)

        def products(block):
            lo, top = span_of(block)
            half, at = lo // rows, lo % rows
            grad_t = GOT[half, n, :, at : at + BLOCK]
            return (
                dot(K[n, 0:top, :], QT[n, :, lo : lo + BLOCK], 1, 0),
                dot(V[n, 0:top, :HEAD_DIM], grad_t, 1, 0),
            )

        for step in range(blocks):
            tick_at("ab", i, 2 * heads, "." + str(step))
            if step == 3:
                pl.when(i == 1)(functools.partial(vector_step, 1))
                pl.when(i == 4)(functools.partial(vector_step, 2))
            block = blocks - 1 - step
            lo, top = span_of(block)
            half, at = lo // rows, lo % rows
            here = slice(at, at + BLOCK)
            score, grad_power = products(block)
            grad_t = GOT[half, n, :, here]
            delta = jnp.sum(
                OT[half, n, :, here].astype(F32) * grad_t.astype(F32), axis=0, keepdims=True
            )
            score = score * EXPONENT_SCALE - LS[pl.ds(n, 1), lo : lo + BLOCK]
            tail = score[lo:] + MB[block, 0 : top - lo, :]
            score = jnp.concatenate([score[:lo], tail], axis=0) if lo else tail
            power = jnp.exp2(score)
            grad_score = (power * (grad_power - delta)).astype(BF)
            grad_value = dot(grad_t, power.astype(BF), 1, 1)
            grad_key = dot(QT[n, :, lo : lo + BLOCK], grad_score, 1, 1)
            if step:
                GVA[:, 0:top] += grad_value
                GKA[:, 0:top] += grad_key
            else:
                GVA[...] = grad_value
                GKA[...] = grad_key
            grad_query = dot(KT[n, :, 0:top], grad_score, 1, 0) * scale
            GT[slot, half, place(0), here] = unturn(grad_query, slice(lo, lo + BLOCK)).astype(BF)
        for half in range(2):
            span = slice(half * rows, (half + 1) * rows)
            GT[slot, half, place(1), :] = unturn(GKA[:, span] * scale, span).astype(BF)
            GT[slot, half, place(2), :] = GVA[:, span].astype(BF)

        @pl.when(h == heads - 1)
        def _():
            for part in range(2):
                tick_at("da", 2 * (1 - slot) + part, 4)
                half_cols = features // 2
                cols = slice(part * half_cols, (part + 1) * half_cols)
                value = dot(A[0, :, cols], GT[slot, 0], 0, 1) + dot(
                    A[1, :, cols], GT[slot, 1], 0, 1
                )
                first = part * (nz // 2)
                D[0, slot, first : first + nz // 2, :, :, : 3 * width] = value.astype(BF).reshape(
                    nz // 2, 2, shard, 3 * width
                )

        return carry

    lax.fori_loop(0, 2 * heads, attend_back, 0)

    def back_project(half):
        return sum(dot(GT[s, half], whole(G, 0, s)[:, : 3 * width], 0, 1) for s in range(2))

    part_g.wait_send()

    def back_projects(i, carry):
        tick_at("bp", i, 2)
        SR[...] = back_project(lax.rem(other + i, 2))

        @pl.when(i == 0)
        def _():
            SB[...] = SR[...].astype(BF)
            part_a.start()

        return carry

    lax.fori_loop(0, 2, back_projects, 0)
    part_a.wait_recv()
    tick("lnb1")

    def first_back(i, carry):
        unit, inverse = norm_parts(tokens[chunk(i), :].astype(F32))
        grad = SR[chunk(i), :] + XG[chunk(i), :].astype(F32)
        grad_tokens[chunk(i), :] = grad_tokens[chunk(i), :] + norm_back(grad, gain_one, unit, inverse)
        return (carry[0] + column_sum(grad * unit), carry[1] + column_sum(grad))

    sums = over_pieces(first_back, (zero_row, zero_row))
    store_tokens = pltpu.make_async_copy(grad_tokens, grad_tokens_hbm, local_sem.at[3])
    store_tokens.start()
    VL[near_slot(0), 0:1, :] = sums[0]
    VL[near_slot(0), 1:2, :] = sums[1]
    late = [
        remote(
            VL.at[near_slot(0)], VL.at[near_slot(0)],
            late_send.at[j - 1], late_recv.at[j - 1], near(j),
        )
        for j in range(1, 8)
    ]
    for c in late:
        c.start()

    def late_taken(j):
        return remote(
            VL.at[near_slot(0)], VL.at[near_slot(j)],
            late_send.at[j - 1], late_recv.at[j - 1], near(j),
        )

    tick("vs0")
    tick("vs1")

    part_a.wait_send()

    def outer(half):
        return dot(Z[half], whole(G, 2, 0), 1, 1) + dot(Z[2 + half], whole(G, 2, 1), 1, 1)

    def outers(i, carry):
        tick_at("out", i, 2)
        SR[...] = outer(lax.rem(other + i, 2))

        @pl.when(i == 0)
        def _():
            SB[...] = SR[...].astype(BF)
            late_taken(1).wait_recv()
            part_b.start()

        return carry

    lax.fori_loop(0, 1, outers, 0)
    lax.fori_loop(1, 2, outers, 0)
    part_b.wait_recv()
    for j in range(2, 8):
        late_taken(j).wait_recv()
    eight = VL[0]
    for n in range(1, 8):
        eight = eight + VL[n]
    VM[z] = eight
    last = [
        remote(VM.at[z], VM.at[z], late_send.at[7 + j], late_recv.at[7 + j], zpeer(j + 1))
        for j in range(nz - 1)
    ]
    for c in last:
        c.start()
    tick("fin")

    def finish_block(i, carry):
        value = R32[chunk(i), :] + SR[chunk(i), :] + XG[chunk(i), :].astype(F32) + bias_out
        tokens[chunk(i), :] = (AVG[chunk(i), :] + depth[4] * value).astype(BF)
        return carry

    lax.fori_loop(0, pieces, finish_block, 0)
    store_layer = pltpu.make_async_copy(tokens, layer_hbm, local_sem.at[4])
    store_layer.start()
    tick("vs2")
    drain(2)
    tick("end")
    for j in range(nz - 1):
        remote(
            VM.at[z], VM.at[lax.rem(z + nz - 1 - j, nz)],
            late_send.at[7 + j], late_recv.at[7 + j], zpeer(j + 1),
        ).wait_recv()
    first_sums = VM[0]
    for j in range(1, nz):
        first_sums = first_sums + VM[j]
    vector_step(3)
    grad_vectors[0:2, :] = first_sums
    for f in range(len(reduces)):
        reduce_step(f, 4)
    store_tokens.wait()
    store_layer.wait()
    vector_step(4)
    for c in [send_a, send_c, send_gl, part_b] + late + last:
        c.wait_send()


def spread_body(width, cotangent, average, tokens, packed, sums, depth, *outs):
    layer_out, grad_tokens, stack, wq, wk, wv, wo, wi, wu = outs[:9]
    gain_one, shift_one, gain_two, shift_two, bias_in, bias_out, grad_depth = outs[9:]
    layer_out[...] = average[...]
    grad_tokens[...] = tokens[...]
    for k in range(4):
        stack[k] = depth[k] * cotangent[...].astype(F32)

    @pl.when(pl.program_id(0) == 0)
    def _():
        for n, ref in enumerate((wq, wk, wv)):
            ref[...] = packed[0, :, n * width : (n + 1) * width]
        wo[...] = packed[0, :, 3 * width :].T
        wi[...] = packed[1]
        wu[...] = packed[2]
        for n, ref in enumerate((gain_one, shift_one, gain_two, shift_two, bias_out)):
            ref[...] = sums[n, :]
        bias_in[...] = jnp.concatenate([sums[9 + n : 10 + n, :] for n in range(4)], axis=1)
        lane = lax.broadcasted_iota(jnp.int32, (1, 5), 1)
        total = jnp.zeros((1, 5), F32)
        for n, row in enumerate((5, 6, 7, 8, 13)):
            total = jnp.where(lane == n, jnp.sum(sums[row : row + 1, :]), total)
        grad_depth[...] = total


def fused_device(
    tokens,
    stack,
    cotangent,
    starts,
    w_query,
    w_key,
    w_value,
    w_output,
    w_in,
    w_out,
    gain_one,
    shift_one,
    gain_two,
    shift_two,
    bias_in,
    bias_out,
    depth_weights,
):
    rows, features = tokens.shape
    shard = w_query.shape[0]
    nz = lax.axis_size("dp") // 2
    length = 2 * rows
    width = w_query.shape[1]
    heads = width // HEAD_DIM
    cos_np, sin_np = rotary_tables(length)
    gathers, reduces, schedule = PLAN
    shape = jax.ShapeDtypeStruct
    vmem = pl.BlockSpec(memory_space=pltpu.VMEM)
    smem = pl.BlockSpec(memory_space=pltpu.SMEM)
    hbm = pl.BlockSpec(memory_space=pl.ANY)
    dma = pltpu.SemaphoreType.DMA
    scratch = [
        pltpu.VMEM((3, 2, nz, 2, shard, features), BF),
        pltpu.VMEM((3, 2, nz, 2, shard, features), BF),
        pltpu.VMEM((3, 2, nz, shard, features), BF),
        pltpu.VMEM((3, nz, shard, features), BF),
        pltpu.VMEM((3, nz - 1, 2, shard, features), BF),
        pltpu.VMEM((2, rows, features), BF),
        pltpu.VMEM((2, rows, features), BF),
        pltpu.VMEM((2, rows, features), BF),
        pltpu.VMEM((2 * heads, length, HEAD_DIM), BF),
        pltpu.VMEM((2 * heads, length, 2 * HEAD_DIM), BF),
        pltpu.VMEM((2 * heads, HEAD_DIM, length), BF),
        pltpu.VMEM((2 * heads, HEAD_DIM, length), BF),
        pltpu.VMEM((2, 2 * heads, HEAD_DIM, rows), BF),
        pltpu.VMEM((8, length), F32),
        pltpu.VMEM((length // BLOCK, 2 * BLOCK, BLOCK), F32),
        pltpu.VMEM((4, rows, features), BF),
        pltpu.VMEM((4, rows, features), BF),
        pltpu.VMEM((2, 2 * heads, HEAD_DIM, rows), BF),
        pltpu.VMEM((2, 2, 3 * width, rows), BF),
        pltpu.VMEM((2 * width, features), BF),
        pltpu.VMEM((rows, features), F32),
        pltpu.VMEM((rows, features), F32),
        pltpu.VMEM((rows, features), F32),
        pltpu.VMEM((rows, features), BF),
        pltpu.VMEM((rows, features), BF),
        pltpu.VMEM((16, features), F32),
        pltpu.VMEM((8, 2, features), F32),
        pltpu.VMEM((8, 2, features), F32),
        pltpu.VMEM((nz, 2, features), F32),
        pltpu.VMEM((8, 2, features), F32),
        pltpu.VMEM((8, 2, features), F32),
        pltpu.VMEM((nz, 2, features), F32),
        pltpu.VMEM((HEAD_DIM, length), F32),
        pltpu.VMEM((HEAD_DIM, length), F32),
        pltpu.VMEM((rows, features), BF),
        pltpu.VMEM((rows, features), BF),
        pltpu.VMEM((length, 2 * HEAD_DIM), F32),
        pltpu.VMEM((length, 2 * HEAD_DIM), F32),
        pltpu.VMEM((4, features), F32),
        pltpu.VMEM((rows, features), F32),
        dma((5,)),
        dma((len(gathers), nz + 1)),
        dma((len(gathers), nz + 1)),
        dma((len(reduces), nz + 2)),
        dma((len(reduces), nz + 2)),
        dma((9,)),
        dma((9,)),
        dma((nz + 13,)),
        dma((nz + 13,)),
        dma((nz + 6,)),
        dma((nz + 6,)),
    ]

    layer_out, grad_tokens, packed, sums = pl.pallas_call(
        functools.partial(fused_body, nz, rows, features, shard, PLAN),
        out_shape=[
            shape((rows, features), BF),
            shape((rows, features), F32),
            shape((3, shard, features), F32),
            shape((16, features), F32),
        ],
        in_specs=[hbm] * 3 + [vmem] * 12 + [smem] * 2 + [vmem] * 2,
        out_specs=[hbm] * 2 + [vmem] * 2,
        scratch_shapes=scratch,
        compiler_params=pltpu.CompilerParams(
            collective_id=0, has_side_effects=True, vmem_limit_bytes=64 * 1024 * 1024
        ),
    )(
        tokens,
        cotangent,
        stack,
        w_query,
        w_key,
        w_value,
        w_output,
        w_in,
        w_out.T,
        gain_one,
        shift_one,
        gain_two,
        shift_two,
        bias_in.reshape(1, -1),
        bias_out,
        depth_weights,
        starts,
        jnp.asarray(cos_np.T.copy()),
        jnp.asarray(sin_np.T.copy()),
    )

    steps = 2
    part = rows // steps
    sizes = (
        [(shard, width)] * 3
        + [(width, shard), (shard, features), (shard, features)]
        + [(features,)] * 4
        + [(1, 4 * features), (features,), (1, 5)]
    )

    def fixed(size):
        return pl.BlockSpec(size, lambda i: (0,) * len(size))

    by_rows = pl.BlockSpec((part, features), lambda i: (i, 0))
    outs = pl.pallas_call(
        functools.partial(spread_body, width),
        grid=(steps,),
        out_shape=[
            shape((rows, features), BF),
            shape((rows, features), F32),
            shape((4, rows, features), F32),
        ]
        + [shape(size, F32) for size in sizes],
        in_specs=[by_rows] * 3 + [fixed((3, shard, features)), fixed((16, features)), smem],
        out_specs=[by_rows] * 2
        + [pl.BlockSpec((4, part, features), lambda i: (0, i, 0))]
        + [fixed(size) for size in sizes],
        compiler_params=pltpu.CompilerParams(vmem_limit_bytes=60 * 1024 * 1024),
    )(cotangent, layer_out, grad_tokens, packed, sums, depth_weights)
    return (*outs[:8], outs[8].T, *outs[9:13], outs[13].reshape(-1), outs[14], outs[15].reshape(-1))


def per_device(*arrays):
    rows, features = arrays[0].shape
    shard, width = arrays[4].shape
    dp = lax.axis_size("dp")
    fits = (
        shard % 16 == 0
        and dp % 4 == 0
        and lax.axis_size("tensor") == 4
        and arrays[3].shape[0] == 2
        and arrays[8].shape[1] == features
        and 4 * width == features
        and shard * dp == features
    )
    return fused_device(*arrays) if fits else plain_device(*arrays)


def solution(mesh):
    in_specs = (
        P(("dp", "tensor"), None),
        P(None, ("dp", "tensor"), None),
        P(("dp", "tensor"), None),
        P("dp", None),
        P("dp", "tensor"),
        P("dp", "tensor"),
        P("dp", "tensor"),
        P("tensor", "dp"),
        P("dp", "tensor"),
        P("tensor", "dp"),
        P(),
        P(),
        P(),
        P(),
        P(),
        P(),
        P(),
    )
    out_specs = (
        P(("dp", "tensor"), None),
        P(("dp", "tensor"), None),
        P(None, ("dp", "tensor"), None),
        P("dp", "tensor"),
        P("dp", "tensor"),
        P("dp", "tensor"),
        P("tensor", "dp"),
        P("dp", "tensor"),
        P("tensor", "dp"),
        P(),
        P(),
        P(),
        P(),
        P(),
        P(),
        P(),
    )
    return jax.shard_map(
        per_device, mesh=mesh, in_specs=in_specs, out_specs=out_specs, check_vma=False
    )
```

```python
import functools
import math

import jax
import jax.numpy as jnp
import numpy as np
from jax import lax
from jax.experimental import pallas as pl
from jax.experimental.pallas import tpu as pltpu
from jax.sharding import PartitionSpec as P

HEAD_DIM = 64
PIECE = 256


EPSILON = 1e-05
NEGATIVE = -1e30


def layer_norm(values, gain, shift):
    centre = values - jnp.mean(values, axis=-1, keepdims=True)
    spread = jnp.mean(centre * centre, axis=-1, keepdims=True)
    return centre * lax.rsqrt(spread + EPSILON) * gain + shift


def tables(seq_length, head_size):
    half_dim = head_size // 2
    frequency = jnp.exp(
        -jnp.log(10000.0) * jnp.arange(half_dim, dtype=jnp.float32) * 2.0 / head_size
    )
    angles = jnp.arange(seq_length, dtype=jnp.float32)[:, None] * frequency[None, :]
    return (jnp.cos(angles), jnp.sin(angles))


def rotate(values, cosine_table, sine_table):
    half_dim = values.shape[-1] // 2
    front_half = values[..., :half_dim]
    back_half = values[..., half_dim:]
    cosines = cosine_table[:, None, :]
    sine_rows = sine_table[:, None, :]
    return jnp.concatenate(
        [
            front_half * cosines - back_half * sine_rows,
            back_half * cosines + front_half * sine_rows,
        ],
        axis=-1,
    )


def allowed_mask(starts, seq_length, piece_size):
    position = jnp.arange(seq_length, dtype=jnp.int32)
    inside = (position[None, None, :] >= starts[:, :, None]) & (
        position[None, None, :] < starts[:, :, None] + piece_size
    )
    jointly = jnp.any(inside[:, :, :, None] & inside[:, :, None, :], axis=1)
    return jointly | (position[None, :, None] >= position[None, None, :])


def gelu_tanh(values):
    return jax.nn.gelu(values, approximate=True)


def right_transposed(matrix, weight):
    return lax.dot_general(
        matrix, weight, (((1,), (1,)), ((), ())), preferred_element_type=jnp.float32
    )


def left_transposed(matrix, other):
    return lax.dot_general(
        matrix, other, (((0,), (0,)), ((), ())), preferred_element_type=jnp.float32
    )


def attend_forward(query, key_rows, value_rows, allowed, score_scale):

    def one_sequence(entries):
        query_seq, key_seq, value_seq, allowed_seq = entries
        scores = (
            jnp.einsum("qhd,khd->hqk", query_seq, key_seq, preferred_element_type=jnp.float32)
            * score_scale
        )
        scores = jnp.where(allowed_seq[None], scores, NEGATIVE)
        highest = jnp.max(scores, axis=-1, keepdims=True)
        powers = jnp.exp(scores - highest)
        row_total = jnp.sum(powers, axis=-1, keepdims=True)
        attention = (powers / row_total).astype(jnp.bfloat16)
        mixed_rows = jnp.einsum(
            "hqk,khd->qhd", attention, value_seq, preferred_element_type=jnp.float32
        )
        return (mixed_rows.astype(jnp.bfloat16), highest + jnp.log(row_total))

    return lax.map(one_sequence, (query, key_rows, value_rows, allowed))


def attend_backward(query, key_rows, value_rows, grad_mixed, log_totals, allowed, score_scale):

    def one_sequence(entries):
        query_seq, key_seq, value_seq, grad_seq, log_seq, allowed_seq = entries
        scores = (
            jnp.einsum("qhd,khd->hqk", query_seq, key_seq, preferred_element_type=jnp.float32)
            * score_scale
        )
        scores = jnp.where(allowed_seq[None], scores, NEGATIVE)
        attention = jnp.exp(scores - log_seq)
        grad_value = jnp.einsum(
            "hqk,qhd->khd",
            attention.astype(jnp.bfloat16),
            grad_seq,
            preferred_element_type=jnp.float32,
        )
        grad_attention = jnp.einsum(
            "qhd,khd->hqk", grad_seq, value_seq, preferred_element_type=jnp.float32
        )
        row_delta = jnp.sum(attention * grad_attention, axis=-1, keepdims=True)
        grad_scores = (attention * (grad_attention - row_delta)).astype(jnp.bfloat16)
        grad_query = (
            jnp.einsum("hqk,khd->qhd", grad_scores, key_seq, preferred_element_type=jnp.float32)
            * score_scale
        )
        grad_key = (
            jnp.einsum("hqk,qhd->khd", grad_scores, query_seq, preferred_element_type=jnp.float32)
            * score_scale
        )
        return (grad_query, grad_key, grad_value.astype(jnp.bfloat16))

    return lax.map(one_sequence, (query, key_rows, value_rows, grad_mixed, log_totals, allowed))


def plain_device(
    tokens,
    stack,
    cotangent,
    starts,
    w_query,
    w_key,
    w_value,
    w_output,
    w_in,
    w_out,
    gain_one,
    shift_one,
    gain_two,
    shift_two,
    bias_in,
    bias_out,
    depth_weights,
):
    rows_here = tokens.shape[0]
    features = tokens.shape[1]
    groups = lax.axis_size("tensor")
    position = lax.axis_index("tensor")
    seq_count = starts.shape[0]
    seq_length = rows_here * groups // seq_count
    score_scale = 1.0 / math.sqrt(HEAD_DIM)
    local_heads = w_query.shape[1] // HEAD_DIM
    hidden = w_in.shape[1]
    cosine_table, sine_table = tables(seq_length, HEAD_DIM)
    allowed = allowed_mask(starts, seq_length, PIECE)

    def to_heads(matrix):
        return matrix.reshape(seq_count, seq_length, local_heads, HEAD_DIM)

    def from_heads(blocks):
        return blocks.reshape(seq_count * seq_length, local_heads * HEAD_DIM)

    def share_rows(local_rows):
        return lax.all_gather(local_rows, "tensor", axis=0, tiled=True)

    def share_grad(local_rows):
        return lax.all_gather(local_rows, "tensor", axis=0, tiled=True)

    def merge_rows(source, weight):
        return lax.psum_scatter(
            jnp.dot(source, weight, preferred_element_type=jnp.float32),
            "tensor",
            scatter_dimension=0,
            tiled=True,
        )

    def return_rows(pairs):
        running = jnp.zeros((lax.axis_size("tensor") * rows_here, features), jnp.float32)
        for source, weight in pairs:
            running = running + right_transposed(source, weight)
        return lax.psum_scatter(running, "tensor", scatter_dimension=0, tiled=True)

    query_w, key_w, value_w, output_w = (
        lax.all_gather(w_query, "dp", axis=0, tiled=True),
        lax.all_gather(w_key, "dp", axis=0, tiled=True),
        lax.all_gather(w_value, "dp", axis=0, tiled=True),
        lax.all_gather(w_output, "dp", axis=1, tiled=True),
    )
    inner_w, outer_w = (
        lax.all_gather(w_in, "dp", axis=0, tiled=True),
        lax.all_gather(w_out, "dp", axis=1, tiled=True),
    )
    token_rows = tokens.astype(jnp.float32)
    normed_one = layer_norm(token_rows, gain_one, shift_one).astype(jnp.bfloat16)
    normed_all = share_rows(normed_one)
    query = rotate(
        to_heads(jnp.dot(normed_all, query_w, preferred_element_type=jnp.float32)),
        cosine_table,
        sine_table,
    ).astype(jnp.bfloat16)
    key_rows = rotate(
        to_heads(jnp.dot(normed_all, key_w, preferred_element_type=jnp.float32)),
        cosine_table,
        sine_table,
    ).astype(jnp.bfloat16)
    value_rows = to_heads(jnp.dot(normed_all, value_w, preferred_element_type=jnp.float32)).astype(
        jnp.bfloat16
    )
    mixed_heads, log_totals = attend_forward(query, key_rows, value_rows, allowed, score_scale)
    mixed_flat = from_heads(mixed_heads)
    middle = token_rows + merge_rows(mixed_flat, output_w)
    normed_two = layer_norm(middle, gain_two, shift_two).astype(jnp.bfloat16)
    second_all = share_rows(normed_two)
    bias_slice = lax.dynamic_slice_in_dim(bias_in, position * hidden, hidden)
    pre_act = jnp.dot(second_all, inner_w, preferred_element_type=jnp.float32) + bias_slice
    activated = gelu_tanh(pre_act).astype(jnp.bfloat16)
    block_out = middle + merge_rows(activated, outer_w) + bias_out
    averaged = depth_weights[4] * block_out
    for layer_index in range(4):
        averaged = averaged + depth_weights[layer_index] * stack[layer_index].astype(jnp.float32)
    layer_out = averaged.astype(jnp.bfloat16)
    grad_rows = cotangent.astype(jnp.float32)
    grad_stack = jnp.stack([depth_weights[layer_index] * grad_rows for layer_index in range(4)])
    depth_terms = jnp.stack(
        [jnp.sum(stack[layer_index].astype(jnp.float32) * grad_rows) for layer_index in range(4)]
        + [jnp.sum(block_out * grad_rows)]
    )
    grad_block = depth_weights[4] * grad_rows
    grad_bias_out = jnp.sum(grad_block, axis=0)
    grad_sent = share_grad(grad_block.astype(jnp.bfloat16))
    grad_outer = left_transposed(activated, grad_sent)
    grad_act = right_transposed(grad_sent, outer_w)
    grad_pre = jax.vjp(gelu_tanh, pre_act)[1](grad_act)[0].astype(jnp.bfloat16)
    grad_bias_slice = jnp.sum(grad_pre.astype(jnp.float32), axis=0)
    bias_full = lax.dynamic_update_slice_in_dim(
        jnp.zeros((bias_in.shape[0],), jnp.float32), grad_bias_slice, position * hidden, 0
    )
    grad_inner = left_transposed(second_all, grad_pre)
    grad_norm_two = return_rows(((grad_pre, inner_w),))
    layer_two = jax.vjp(layer_norm, middle, gain_two, shift_two)[1](grad_norm_two)
    grad_middle = grad_block + layer_two[0]
    grad_attn_sent = share_grad(grad_middle.astype(jnp.bfloat16))
    grad_output_w = left_transposed(mixed_flat, grad_attn_sent)
    grad_mixed = right_transposed(grad_attn_sent, output_w).astype(jnp.bfloat16)
    grad_query, grad_key, grad_value = attend_backward(
        query, key_rows, value_rows, to_heads(grad_mixed), log_totals, allowed, score_scale
    )
    grad_query = from_heads(rotate(grad_query, cosine_table, -sine_table)).astype(jnp.bfloat16)
    grad_key = from_heads(rotate(grad_key, cosine_table, -sine_table)).astype(jnp.bfloat16)
    grad_value = from_heads(grad_value)
    grad_query_w = left_transposed(normed_all, grad_query)
    grad_key_w = left_transposed(normed_all, grad_key)
    grad_value_w = left_transposed(normed_all, grad_value)
    grad_norm_one = return_rows(((grad_query, query_w), (grad_key, key_w), (grad_value, value_w)))
    layer_one = jax.vjp(layer_norm, token_rows, gain_one, shift_one)[1](grad_norm_one)
    grad_tokens = grad_middle + layer_one[0]
    grad_w_query, grad_w_key, grad_w_value, grad_w_output, grad_w_in, grad_w_out = (
        lax.psum_scatter(grad_query_w, "dp", scatter_dimension=0, tiled=True),
        lax.psum_scatter(grad_key_w, "dp", scatter_dimension=0, tiled=True),
        lax.psum_scatter(grad_value_w, "dp", scatter_dimension=0, tiled=True),
        lax.psum_scatter(grad_output_w, "dp", scatter_dimension=1, tiled=True),
        lax.psum_scatter(grad_inner, "dp", scatter_dimension=0, tiled=True),
        lax.psum_scatter(grad_outer, "dp", scatter_dimension=1, tiled=True),
    )
    summed = lax.psum(
        (
            layer_one[1],
            layer_one[2],
            layer_two[1],
            layer_two[2],
            bias_full,
            grad_bias_out,
            depth_terms,
        ),
        ("dp", "tensor"),
    )
    return (
        layer_out,
        grad_tokens,
        grad_stack,
        grad_w_query,
        grad_w_key,
        grad_w_value,
        grad_w_output,
        grad_w_in,
        grad_w_out,
        summed[0],
        summed[1],
        summed[2],
        summed[3],
        summed[4],
        summed[5],
        summed[6],
    )


BF = jnp.bfloat16
F32 = jnp.float32
MESH = pl.DeviceIdType.MESH
BLOCK = 256
EXPONENT_SCALE = math.log2(math.e) / math.sqrt(HEAD_DIM)


PLAN = (
    (
        ("A", 0, 0, 128),
        ("A", 0, 128, 128),
        ("A", 0, 256, 128),
        ("A", 0, 384, 128),
        ("A", 0, 512, 128),
        ("B", 0, 640, 128),
        ("A", 1, 0, 128),
        ("B", 1, 128, 128),
        ("A", 1, 256, 128),
        ("A", 1, 384, 256),
        ("B", 1, 640, 128),
        ("A", 2, 0, 128),
        ("B", 2, 128, 128),
        ("A", 2, 256, 128),
        ("A", 2, 384, 128),
        ("B", 2, 512, 128),
        ("B", 2, 640, 128),
    ),
    (
        ("A", 2, 0, 128),
        ("B", 2, 128, 256),
        ("A", 2, 384, 128),
        ("A", 2, 512, 256),
        ("B", 1, 0, 128),
        ("B", 1, 128, 128),
        ("B", 1, 256, 128),
        ("A", 1, 384, 128),
        ("A", 1, 512, 256),
        ("A", 0, 0, 256),
        ("A", 0, 256, 128),
        ("A", 0, 384, 128),
        ("A", 0, 512, 128),
        ("B", 0, 640, 128),
    ),
    {
        "norm": ((1, 0, 0), (1, 5, 0), (1, 7, 0), (1, 10, 0),),
        "mask0": ((1, 1, 0), (1, 12, 0), (1, 15, 0), (1, 16, 0),),
        "mask2": ((1, 2, 0),),
        "mask3": ((1, 0, 1),),
        "stack2": ((1, 3, 0),),
        "stack3": ((1, 1, 1),),
        "proj0.0": ((1, 4, 0), (1, 0, 2), (1, 2, 1), (1, 5, 1), (1, 1, 2), (1, 3, 1), (1, 4, 1), (1, 0, 3), (1, 6, 0), (1, 2, 2), (1, 7, 1), (1, 5, 2), (1, 1, 3), (1, 3, 2), (1, 6, 1), (1, 8, 0), (1, 2, 3), (1, 9, 0), (1, 5, 3), (1, 4, 2),),
        "proj0.1": ((1, 7, 2),),
        "att0.1": ((1, 3, 3),),
        "att0.2": ((1, 10, 1),),
        "att0.3": ((1, 6, 2), (1, 8, 1),),
        "att2.0": ((1, 9, 1),),
        "att2.2": ((1, 4, 3), (1, 7, 3), (1, 11, 0),),
        "proj1.1": ((1, 8, 2), (1, 12, 1),),
        "att3.0": ((1, 10, 2), (1, 6, 3),),
        "att4.1": ((1, 9, 2), (1, 13, 0),),
        "att4.3": ((1, 11, 1),),
        "att5.2": ((1, 8, 3), (1, 14, 0),),
        "wo": ((1, 12, 2),),
        "r.other": ((1, 10, 3),),
        "r.low": ((1, 15, 1),),
        "in0": ((1, 11, 2), (1, 13, 1), (1, 16, 1),),
        "in1": ((1, 9, 3), (1, 12, 3), (1, 14, 1),),
        "in3": ((1, 15, 2),),
        "dc0": ((1, 13, 2),),
        "dc1": ((1, 11, 3),),
        "dc3": ((1, 14, 2), (1, 16, 2),),
        "bh0": ((1, 15, 3), (1, 13, 3), (0, 1, 0), (0, 0, 0), (1, 16, 3),),
        "bh1": ((1, 14, 3),),
        "bi0": ((0, 2, 0),),
        "bh3": ((0, 0, 1), (0, 3, 0),),
        "lnb2": ((0, 1, 1), (0, 2, 1),),
        "go": ((0, 4, 0), (0, 7, 0),),
        "ab0.0": ((0, 0, 2),),
        "ab0.1": ((0, 3, 1), (0, 8, 0),),
        "ab0.2": ((0, 2, 2),),
        "ab1.0": ((0, 4, 1),),
        "ab1.1": ((0, 0, 3), (0, 5, 0),),
        "ab2.0": ((0, 2, 3),),
        "ab2.1": ((0, 3, 2),),
        "ab2.2": ((0, 6, 0),),
        "ab2.3": ((0, 1, 2),),
        "da0": ((0, 4, 2),),
        "da1": ((0, 5, 1),),
        "ab3.0": ((0, 9, 0), (0, 7, 1),),
        "ab3.1": ((0, 1, 3),),
        "ab3.2": ((0, 4, 3),),
        "ab3.3": ((0, 3, 3), (0, 8, 1), (0, 6, 1),),
        "ab4.3": ((0, 13, 0),),
        "ab5.0": ((0, 5, 2), (0, 7, 2), (0, 10, 0),),
        "ab5.3": ((0, 8, 2),),
        "da2": ((0, 5, 3),),
        "da3": ((0, 6, 2), (0, 11, 0),),
        "bp0": ((0, 7, 3), (0, 9, 1),),
        "bp1": ((0, 13, 1),),
        "lnb1": ((0, 6, 3), (0, 8, 3), (0, 10, 1), (0, 12, 0),),
        "vs0": ((0, 9, 2), (0, 11, 1), (0, 13, 2),),
        "vs1": ((0, 10, 2), (0, 12, 1), (0, 13, 3),),
        "out1": ((0, 11, 2),),
        "fin": ((0, 9, 3), (0, 10, 3), (0, 12, 2),),
        "end": ((0, 11, 3), (0, 12, 3),),
    },
)


def dot(left, right, left_axis, right_axis):
    return lax.dot_general(
        left, right, (((left_axis,), (right_axis,)), ((), ())), preferred_element_type=F32
    )


def norm_parts(values):
    centre = values - jnp.mean(values, axis=-1, keepdims=True)
    inverse = lax.rsqrt(jnp.mean(centre * centre, axis=-1, keepdims=True) + EPSILON)
    return centre * inverse, inverse


def norm_back(grad, gain, unit, inverse):
    scaled = grad * gain
    first = jnp.mean(scaled, axis=-1, keepdims=True)
    second = jnp.mean(scaled * unit, axis=-1, keepdims=True)
    return inverse * (scaled - first - unit * second)


def gelu_pair(values):
    root = math.sqrt(2.0 / math.pi)
    square = values * values
    bend = jnp.tanh(root * values * (1.0 + 0.044715 * square))
    half = 0.5 * (1.0 + bend)
    slope = half + 0.5 * root * values * (1.0 - bend * bend) * (1.0 + 3 * 0.044715 * square)
    return values * half, slope


def column_sum(values):
    return jnp.sum(values, axis=0, keepdims=True)


def rotary_tables(length):
    half = HEAD_DIM // 2
    frequency = np.exp(-np.log(10000.0) * np.arange(half) * 2.0 / HEAD_DIM)
    angles = np.arange(length)[:, None] * frequency[None, :]
    return np.cos(angles).astype(np.float32), np.sin(angles).astype(np.float32)


def fused_body(
    nz,
    rows,
    features,
    shard,
    plan,
    tokens_hbm,
    cotangent_hbm,
    stack,
    w_query,
    w_key,
    w_value,
    w_output,
    w_in,
    w_out,
    gain_one,
    shift_one,
    gain_two,
    shift_two,
    bias_in,
    bias_out,
    depth,
    starts,
    cosine_t,
    sine_t,
    layer_hbm,
    grad_tokens_hbm,
    grad_packed,
    grad_vectors,
    G,
    D,
    RY,
    RX,
    RZ,
    A,
    C,
    GM,
    K,
    V,
    KT,
    QT,
    OT,
    LS,
    MB,
    Z,
    GP,
    GOT,
    GT,
    WO,
    R32,
    AVG,
    SR,
    SB,
    XG,
    VS,
    V8,
    VI,
    VP,
    VO,
    VL,
    VM,
    GKA,
    GVA,
    tokens,
    cotangent,
    cosine,
    sine,
    BI,
    grad_tokens,
    local_sem,
    ag_send,
    ag_recv,
    rs_send,
    rs_recv,
    sib_send,
    sib_recv,
    vec_send,
    vec_recv,
    late_send,
    late_recv,
):
    length = 2 * rows
    heads = 3
    width = heads * HEAD_DIM
    gathers, reduces, schedule = plan
    dp = lax.axis_index("dp")
    t = lax.axis_index("tensor")
    z = dp // 2
    x = lax.rem(dp, 2)
    low = lax.rem(t, 2)
    pair = t // 2
    other = 1 - low
    sib = (dp, t + 1 - 2 * low)
    ypeer = (dp, lax.rem(t + 2, 4))
    xpeer = (dp + 1 - 2 * x, t)

    def zpeer(j):
        return (lax.rem(z + j, nz) * 2 + x, t)

    def near_place(j):
        side = x + (1 - 2 * x) * (j // 4)
        upper = pair + (1 - 2 * pair) * ((j // 2) % 2)
        lower = low + (1 - 2 * low) * (j % 2)
        return side, 2 * upper + lower

    def near(j):
        side, place = near_place(j)
        return 2 * z + side, place

    def near_slot(j):
        side, place = near_place(j)
        return 4 * side + place

    def remote(src, dst, send, recv, peer):
        return pltpu.make_async_remote_copy(
            src_ref=src, dst_ref=dst, send_sem=send, recv_sem=recv,
            device_id=peer, device_id_type=MESH,
        )

    everything = slice(None)

    def gather_copies(f, stage):
        kind, k, first, count = gathers[f]
        cols = pl.ds(first, count)
        axis = ("zxy" if kind == "A" else "yzx")[stage]
        if axis == "z":
            slot = 0 if kind == "A" else everything
            mine = G.at[k, slot, z, x, :, cols]
            sent, taken = [], []
            for j in range(nz - 1):
                sems = (ag_send.at[f, j], ag_recv.at[f, j], zpeer(j + 1))
                sent.append(lambda mine=mine, sems=sems: remote(mine, mine, *sems))
                from_z = lax.rem(z + nz - 1 - j, nz)
                taken.append(
                    lambda mine=mine, sems=sems, from_z=from_z: remote(
                        mine, G.at[k, slot, from_z, x, :, cols], *sems
                    )
                )
            return sent, taken
        if axis == "x":
            slot = 0 if kind == "A" else everything
            ref = G.at[k, slot, :, x, :, cols]
            copy = lambda: remote(ref, ref, ag_send.at[f, nz - 1], ag_recv.at[f, nz - 1], xpeer)
            return [copy], [copy]
        sems = (ag_send.at[f, nz], ag_recv.at[f, nz], ypeer)
        if kind == "A":
            copy = lambda: remote(G.at[k, 0, :, :, :, cols], G.at[k, 1, :, :, :, cols], *sems)
        else:
            copy = lambda: remote(G.at[k, 0, z, x, :, cols], G.at[k, 1, z, x, :, cols], *sems)
        return [copy], [copy]

    def gather_step(f, stage):
        if stage == 4:
            for past in range(3):
                for copy in gather_copies(f, past)[0]:
                    copy().wait_send()
            return
        awaited = {1: 0, 2: 1, 3: 2, 5: 1}.get(stage)
        if awaited is not None:
            for copy in gather_copies(f, awaited)[1]:
                copy().wait_recv()
        started = {0: 0, 1: 1, 2: 2, 6: 2}.get(stage)
        if started is not None:
            for copy in gather_copies(f, started)[0]:
                copy().start()

    def reduce_copies(f, stage):
        kind, k, first, count = reduces[f]
        cols = pl.ds(first, count)
        axis = ("yxz" if kind == "A" else "xzy")[stage]

        def sems(n):
            return rs_send.at[f, n], rs_recv.at[f, n]

        if axis == "z":
            slot = 0 if kind == "A" else everything
            land = 0 if kind == "A" else everything
            return [
                lambda j=j: remote(
                    D.at[k, slot, lax.rem(z + j + 1, nz), x, :, cols],
                    RZ.at[k, j, land, :, cols], *sems(j), zpeer(j + 1),
                )
                for j in range(nz - 1)
            ]
        if axis == "x":
            if kind == "A":
                return [
                    lambda: remote(
                        D.at[k, 0, :, 1 - x, :, cols], RX.at[k, :, :, cols], *sems(nz - 1), xpeer
                    )
                ]
            return [
                lambda: remote(
                    D.at[k, :, :, 1 - x, :, cols], RY.at[k, :, :, :, cols], *sems(nz - 1), xpeer
                )
            ]
        if kind == "A":
            return [
                lambda side=side, n=n: remote(
                    D.at[k, 1, :, side, :, cols], RY.at[k, side, :, :, cols], *sems(nz + n), ypeer
                )
                for n, side in enumerate((1 - x, x))
            ]
        return [lambda: remote(D.at[k, 1, z, x, :, cols], RX.at[k, 0, :, cols], *sems(nz), ypeer)]

    def reduce_step(f, stage):
        kind, k, first, count = reduces[f]
        cols = pl.ds(first, count)
        if stage == 4:
            for past in range(3):
                for copy in reduce_copies(f, past):
                    copy().wait_send()
            return
        before = reduce_copies(f, stage - 1) if stage else []
        after = reduce_copies(f, stage) if stage < 3 else []

        def add(target, source):
            target[...] = (target[...].astype(F32) + source[...].astype(F32)).astype(BF)

        if kind == "A" and stage == 1:
            before[0]().wait_recv()
            add(D.at[k, 0, :, 1 - x, :, cols], RY.at[k, 1 - x, :, :, cols])
            after[0]().start()
            before[1]().wait_recv()
            add(D.at[k, 0, :, x, :, cols], RY.at[k, x, :, :, cols])
            return
        for copy in before:
            copy().wait_recv()
        if kind == "A" and stage == 2:
            add(D.at[k, 0, :, x, :, cols], RX.at[k, :, :, cols])
        elif kind == "B" and stage == 1:
            add(D.at[k, :, :, x, :, cols], RY.at[k, :, :, :, cols])
        elif kind == "B" and stage == 2:
            total = D[k, :, z, x, :, cols].astype(F32)
            for j in range(nz - 1):
                total = total + RZ[k, j, :, :, cols].astype(F32)
            D[k, 1, z, x, :, cols] = total[1].astype(BF)
            grad_packed[k, :, cols] = total[0]
        elif kind == "A" and stage == 3:
            total = D[k, 0, z, x, :, cols].astype(F32)
            for j in range(nz - 1):
                total = total + RZ[k, j, 0, :, cols].astype(F32)
            grad_packed[k, :, cols] = total
        elif kind == "B" and stage == 3:
            grad_packed[k, :, cols] = grad_packed[k, :, cols] + RX[k, 0, :, cols].astype(F32)
        for copy in after:
            copy().start()

    def drain(k):
        for f in range(len(gathers)):
            if gathers[f][1] == k:
                gather_step(f, 4)

    def tick(name):
        for gather, flow, stage in schedule.get(name, ()):
            if gather:
                gather_step(flow, stage)
            else:
                reduce_step(flow, stage)

    def tick_at(prefix, index, count, suffix=""):
        for i in range(count):
            name = prefix + str(i) + suffix
            if schedule.get(name):

                @pl.when(index == i)
                def _(name=name):
                    tick(name)

    def sib_copy(n, src, dst):
        return remote(src, dst, sib_send.at[n], sib_recv.at[n], sib)

    send_a = sib_copy(0, A.at[low], A.at[low])
    take_a = sib_copy(0, A.at[low], A.at[other])
    send_gm = sib_copy(1, GM.at[low], GM.at[low])
    take_gm = sib_copy(1, GM.at[low], GM.at[other])
    half_rows = rows // 2
    part_r = [
        sib_copy(n, SB.at[pl.ds(i * half_rows, half_rows)], XG.at[pl.ds(i * half_rows, half_rows)])
        for i, n in enumerate((2, 8))
    ]
    send_c = sib_copy(3, C.at[low], C.at[low])
    take_c = sib_copy(3, C.at[low], C.at[other])
    part_g = sib_copy(4, SB, XG)
    send_gl = sib_copy(5, GM.at[low], GM.at[low])
    take_gl = sib_copy(5, GM.at[low], GM.at[other])
    part_b = sib_copy(6, SB, XG)
    part_a = sib_copy(7, SB, XG)

    loads = [
        pltpu.make_async_copy(tokens_hbm, tokens, local_sem.at[0]),
        pltpu.make_async_copy(cotangent_hbm, cotangent, local_sem.at[1]),
        pltpu.make_async_copy(stack, Z, local_sem.at[2]),
    ]
    for load in loads:
        load.start()
    barrier = pltpu.get_barrier_semaphore()
    partners = [near(j) for j in range(1, 8)] + [zpeer(j + 1) for j in range(nz - 1)]
    for peer in partners:
        pl.semaphore_signal(barrier, inc=1, device_id=peer, device_id_type=MESH)
    G[0, 0, z, x] = jnp.concatenate(
        [w_query[...], w_key[...], w_value[...], w_output[...].T], axis=1
    )
    G[1, 0, z, x] = w_in[...]
    G[2, 0, z, x] = w_out[...]
    pl.semaphore_wait(barrier, len(partners))
    tick("norm")

    gain_one, shift_one, gain_two, shift_two, bias_out = (
        ref[...].reshape(1, features)
        for ref in (gain_one, shift_one, gain_two, shift_two, bias_out)
    )
    piece = 128
    pieces = rows // piece

    def chunk(i):
        return pl.ds(i * piece if isinstance(i, int) else pl.multiple_of(i * piece, piece), piece)

    def over_pieces(step, carry):
        for i in range(pieces):
            carry = step(i, carry)
        return carry

    loads[0].wait()
    loads[1].wait()

    def first_norm(i, carry):
        unit, _ = norm_parts(tokens[chunk(i), :].astype(F32))
        A[low, chunk(i), :] = (unit * gain_one + shift_one).astype(BF)
        GM[low, chunk(i), :] = (depth[4] * cotangent[chunk(i), :].astype(F32)).astype(BF)
        return carry

    lax.fori_loop(0, pieces, first_norm, 0)
    send_a.start()
    send_gm.start()
    for n in range(4):
        BI[n : n + 1, :] = bias_in[:, n * features : (n + 1) * features]
    cosine[...] = jnp.concatenate([cosine_t[...]] * 4, axis=0).T
    sine[...] = jnp.concatenate([-sine_t[...], sine_t[...]] * 2, axis=0).T

    s0, s1 = starts[pair, 0], starts[pair, 1]
    blocks = length // BLOCK
    for block in range(blocks):
        tick("mask" + str(block))
        key = block * BLOCK + lax.broadcasted_iota(jnp.int32, (2 * BLOCK, BLOCK), 0)
        query = block * BLOCK + lax.broadcasted_iota(jnp.int32, (2 * BLOCK, BLOCK), 1)
        fine = key <= query
        for s in (s0, s1):
            fine = fine | ((key >= s) & (key < s + PIECE) & (query >= s) & (query < s + PIECE))
        MB[block] = jnp.where(fine, 0.0, NEGATIVE)
    VS[...] = jnp.zeros_like(VS)
    for s in range(2):
        for h in range(heads):
            V[heads * s + h, :, HEAD_DIM:] = jnp.where(
                lax.broadcasted_iota(jnp.int32, (length, HEAD_DIM), 1) == 0, 1.0, 0.0
            ).astype(BF)

    loads[2].wait()

    def earlier(i, sums):
        tick_at("stack", i, pieces)
        grad = cotangent[chunk(i), :].astype(F32)
        mean = jnp.zeros((piece, features), F32)
        new = [sums[0] + column_sum(grad)]
        for k in range(4):
            layer = Z[k, chunk(i), :].astype(F32)
            mean = mean + depth[k] * layer
            new.append(sums[k + 1] + column_sum(layer * grad))
        AVG[chunk(i), :] = mean
        return tuple(new)

    zero_row = jnp.zeros((1, features), F32)
    sums = lax.fori_loop(0, pieces, earlier, (zero_row,) * 5)
    VS[4:5, :] = depth[4] * sums[0]
    for k in range(4):
        VS[5 + k : 6 + k, :] = sums[k + 1]

    take_a.wait_recv()

    def whole(ref, *index):
        value = ref[index]
        return value.reshape(value.shape[-4] * value.shape[-3] * value.shape[-2], value.shape[-1])

    lane = lax.broadcasted_iota(jnp.int32, (rows, 128), 1)
    front = lax.rem(lane, HEAD_DIM) < HEAD_DIM // 2

    def project(slot):
        for half in range(2):
            tick_at("proj", slot, 2, "." + str(half))
            weight = whole(G, 0, slot, everything, everything, everything, slice(0, 640))
            span = slice(half * rows, (half + 1) * rows)
            result = dot(A[half], weight, 1, 0)
            turned = []
            for tile in range(3):
                part = result[:, tile * 128 : (tile + 1) * 128]
                partner = jnp.where(front, pltpu.roll(part, 96, 1), pltpu.roll(part, 32, 1))
                turned.append((part * cosine[span, :] + partner * sine[span, :]).astype(BF))
            for h in range(heads):
                n = heads * slot + h
                at = h * HEAD_DIM
                QT[n, :, span] = turned[at // 128][:, at % 128 : at % 128 + HEAD_DIM].T
                at = width + h * HEAD_DIM
                key = turned[at // 128][:, at % 128 : at % 128 + HEAD_DIM]
                K[n, span, :] = key
                KT[n, :, span] = key.T
                at = 2 * width + h * HEAD_DIM
                V[n, span, :HEAD_DIM] = result[:, at : at + HEAD_DIM].astype(BF)

    def span_of(block):
        lo = block * BLOCK
        return lo, min(lo + 2 * BLOCK, length)

    def attend(n, carry):
        @pl.when(lax.rem(n, heads) == 0)
        def _():
            project(n // heads)

        def scores(block):
            lo, top = span_of(block)
            return dot(K[n, 0:top, :], QT[n, :, lo : lo + BLOCK], 1, 0)

        ahead = scores(0)
        for block in range(blocks):
            tick_at("att", n, 2 * heads, "." + str(block))
            lo, top = span_of(block)
            half, at = lo // rows, lo % rows
            score = ahead * EXPONENT_SCALE
            if block + 1 < blocks:
                ahead = scores(block + 1)
            tail = score[lo:] + MB[block, 0 : top - lo, :]
            score = jnp.concatenate([score[:lo], tail], axis=0) if lo else tail
            highest = jnp.max(score, axis=0, keepdims=True)
            power = jnp.exp2(score - highest).astype(BF)
            mixed = dot(V[n, 0:top, :], power, 0, 0)
            total = mixed[HEAD_DIM : HEAD_DIM + 1, :]
            OT[half, n, :, at : at + BLOCK] = (mixed[:HEAD_DIM, :] / total).astype(BF)
            LS[pl.ds(n, 1), lo : lo + BLOCK] = highest + jnp.log2(total)
        return carry

    lax.fori_loop(0, 2 * heads, attend, 0)
    tick("wo")
    for slot in range(2):
        flipped = whole(G, 0, slot, everything, everything, everything, slice(512, 768)).T
        WO[slot * width : (slot + 1) * width, :] = flipped[64:256, :]

    def mixed_rows(half):
        return OT[half].reshape(2 * width, rows)

    tick("r.other")
    for i in range(2):
        span = slice(i * half_rows, (i + 1) * half_rows)
        left = OT[other, :, :, span].reshape(2 * width, half_rows)
        SB[span, :] = dot(left, WO[...], 0, 0).astype(BF)
        part_r[i].start()
    tick("r.low")
    R32[...] = dot(mixed_rows(low), WO[...], 0, 0)
    for copy in part_r:
        copy.wait_recv()
    tick("ln2")

    def second_norm(i, carry):
        middle = tokens[chunk(i), :].astype(F32) + R32[chunk(i), :] + XG[chunk(i), :].astype(F32)
        R32[chunk(i), :] = middle
        unit, _ = norm_parts(middle)
        C[low, chunk(i), :] = (unit * gain_two + shift_two).astype(BF)
        return carry

    over_pieces(second_norm, 0)
    send_c.start()
    def hidden_bias(slot):
        return BI[pl.ds(lax.rem(t + 2 * slot, 4), 1), :]

    def inner(i, carry):
        tick_at("in", i, 4)

        @pl.when(i == 2)
        def _():
            take_c.wait_recv()

        half, slot = lax.rem(low + i // 2, 2), lax.rem(i, 2)
        pre = dot(C[half], whole(G, 1, slot), 1, 0) + hidden_bias(slot)
        act, slope = gelu_pair(pre)
        Z[2 * slot + half] = act.astype(BF)
        GP[2 * slot + half] = slope.astype(BF)
        return carry

    lax.fori_loop(0, 4, inner, 0)
    take_gm.wait_recv()

    def outer_products(name, k, left, right):
        half_cols = features // 2

        def one(i, carry):
            tick_at(name, i, 4)
            slot, part = 1 - i // 2, lax.rem(i, 2)
            cols = pl.ds(pl.multiple_of(part * half_cols, 128), half_cols)
            value = dot(
                left[:, :, cols].reshape(length, half_cols),
                right[pl.ds(2 * slot, 2)].reshape(length, features),
                0,
                0,
            )
            D[k, slot, pl.ds(part * (nz // 2), nz // 2)] = value.astype(BF).reshape(
                nz // 2, 2, shard, features
            )
            return carry

        lax.fori_loop(0, 4, one, 0)

    outer_products("dc", 2, GM, Z)

    def back(i, carry):
        half = lax.rem(other + i, 2)

        def one(slot, total):
            tick_at("bh", 2 * i + slot, 4)
            grad = dot(GM[half], whole(G, 2, slot), 1, 0)
            total = total + column_sum(grad * Z[2 * slot + half].astype(F32))
            grad = (grad * GP[2 * slot + half].astype(F32)).astype(BF)
            GP[2 * slot + half] = grad
            row = pl.ds(9 + lax.rem(t + 2 * slot, 4), 1)
            VS[row, :] = VS[row, :] + column_sum(grad.astype(F32))
            return total

        carry = lax.fori_loop(0, 2, one, carry)
        tick_at("bi", i, 2)
        grad_tokens[...] = dot(GP[half], whole(G, 1, 0), 1, 1) + dot(
            GP[2 + half], whole(G, 1, 1), 1, 1
        )

        @pl.when(i == 0)
        def _():
            for copy in part_r:
                copy.wait_send()
            SB[...] = grad_tokens[...].astype(BF)
            part_g.start()

        return carry

    drain(0)
    VS[13:14, :] = lax.fori_loop(0, 2, back, zero_row) / depth[4]
    part_g.wait_recv()
    send_gm.wait_send()
    tick("lnb2")

    def second_back(i, carry):
        middle = R32[chunk(i), :]
        unit, inverse = norm_parts(middle)
        grad = grad_tokens[chunk(i), :] + XG[chunk(i), :].astype(F32)
        coming = cotangent[chunk(i), :].astype(F32)
        whole_grad = depth[4] * coming + norm_back(grad, gain_two, unit, inverse)
        grad_tokens[chunk(i), :] = whole_grad
        GM[low, chunk(i), :] = whole_grad.astype(BF)
        return (
            carry[0] + column_sum(grad * unit),
            carry[1] + column_sum(grad),
            carry[2] + column_sum(coming * (middle + bias_out)),
        )

    sums = lax.fori_loop(0, pieces, second_back, (zero_row,) * 3)
    VS[2:3, :] = sums[0]
    VS[3:4, :] = sums[1]
    send_gl.start()
    VS[13:14, :] = VS[13:14, :] + sums[2]

    def vector_step(step):
        mine = near_slot(0)

        def hop(kind, j):
            if kind == 1:
                source, target, peer, sem = VP.at[z], VP.at[z], zpeer(j), 6 + j
            else:
                source = V8.at[near_slot(j)] if kind == 0 else VO.at[mine]
                target = VI.at[mine] if kind == 0 else VO.at[mine]
                peer, sem = near(j), j - 1 + (nz + 6) * (kind // 2)
            return remote(source, target, vec_send.at[sem], vec_recv.at[sem], peer)

        def taken(kind, j):
            if kind == 1:
                target, sem = VP.at[lax.rem(z + nz - j, nz)], 6 + j
            else:
                target = (VI if kind == 0 else VO).at[near_slot(j)]
                sem = j - 1 + (nz + 6) * (kind // 2)
            peer = zpeer(j) if kind == 1 else near(j)
            remote(V8.at[0], target, vec_send.at[sem], vec_recv.at[sem], peer).wait_recv()

        def ends(kind):
            return range(1, nz if kind == 1 else 8)

        if step == 0:
            for n in range(8):
                V8[n] = VS[2 * n : 2 * n + 2, :]
            VI[mine] = V8[mine]
        elif step < 4:
            for j in ends(step - 1):
                taken(step - 1, j)
            if step == 1:
                total = VI[0]
                for n in range(1, 8):
                    total = total + VI[n]
                VP[z] = total
            elif step == 2:
                total = VP[0]
                for n in range(1, nz):
                    total = total + VP[n]
                VO[mine] = total
            else:
                for n in range(8):
                    grad_vectors[2 * n : 2 * n + 2, :] = VO[n]
        else:
            for kind in range(3):
                for j in ends(kind):
                    hop(kind, j).wait_send()
        if step < 3:
            for j in ends(step):
                hop(step, j).start()

    vector_step(0)
    outer_products("db", 1, C, GP)

    drain(1)
    take_gl.wait_recv()
    tick("go")

    def grad_mixed(half, carry):
        GOT[half] = dot(WO[...], GM[half], 1, 1).astype(BF).reshape(2 * heads, HEAD_DIM, rows)
        return carry

    lax.fori_loop(0, 2, grad_mixed, 0)
    tick("dwo")
    for slot in range(2):
        value = sum(
            dot(OT[half, heads * slot : heads * slot + heads].reshape(width, rows), GM[half], 1, 0)
            for half in range(2)
        )
        D[0, slot, :, :, :, 3 * width :] = value.T.astype(BF).reshape(nz, 2, shard, width)

    def unturn(value, span):
        front_half, back_half = value[: HEAD_DIM // 2], value[HEAD_DIM // 2 :]
        cosines, sines = cosine_t[:, span], sine_t[:, span]
        return jnp.concatenate(
            [front_half * cosines + back_half * sines, back_half * cosines - front_half * sines],
            axis=0,
        )

    scale = 1.0 / math.sqrt(HEAD_DIM)

    def attend_back(i, carry):
        slot, h = 1 - i // heads, lax.rem(i, heads)
        n = heads * slot + h

        def place(which):
            return pl.ds(pl.multiple_of(which * width + h * HEAD_DIM, HEAD_DIM), HEAD_DIM)

        def products(block):
            lo, top = span_of(block)
            half, at = lo // rows, lo % rows
            grad_t = GOT[half, n, :, at : at + BLOCK]
            return (
                dot(K[n, 0:top, :], QT[n, :, lo : lo + BLOCK], 1, 0),
                dot(V[n, 0:top, :HEAD_DIM], grad_t, 1, 0),
            )

        for step in range(blocks):
            tick_at("ab", i, 2 * heads, "." + str(step))
            if step == 3:
                pl.when(i == 1)(functools.partial(vector_step, 1))
                pl.when(i == 4)(functools.partial(vector_step, 2))
            block = blocks - 1 - step
            lo, top = span_of(block)
            half, at = lo // rows, lo % rows
            here = slice(at, at + BLOCK)
            score, grad_power = products(block)
            grad_t = GOT[half, n, :, here]
            delta = jnp.sum(
                OT[half, n, :, here].astype(F32) * grad_t.astype(F32), axis=0, keepdims=True
            )
            score = score * EXPONENT_SCALE - LS[pl.ds(n, 1), lo : lo + BLOCK]
            tail = score[lo:] + MB[block, 0 : top - lo, :]
            score = jnp.concatenate([score[:lo], tail], axis=0) if lo else tail
            power = jnp.exp2(score)
            grad_score = (power * (grad_power - delta)).astype(BF)
            grad_value = dot(grad_t, power.astype(BF), 1, 1)
            grad_key = dot(QT[n, :, lo : lo + BLOCK], grad_score, 1, 1)
            if step:
                GVA[:, 0:top] += grad_value
                GKA[:, 0:top] += grad_key
            else:
                GVA[...] = grad_value
                GKA[...] = grad_key
            grad_query = dot(KT[n, :, 0:top], grad_score, 1, 0) * scale
            GT[slot, half, place(0), here] = unturn(grad_query, slice(lo, lo + BLOCK)).astype(BF)
        for half in range(2):
            span = slice(half * rows, (half + 1) * rows)
            GT[slot, half, place(1), :] = unturn(GKA[:, span] * scale, span).astype(BF)
            GT[slot, half, place(2), :] = GVA[:, span].astype(BF)

        @pl.when(h == heads - 1)
        def _():
            for part in range(2):
                tick_at("da", 2 * (1 - slot) + part, 4)
                half_cols = features // 2
                cols = slice(part * half_cols, (part + 1) * half_cols)
                value = dot(A[0, :, cols], GT[slot, 0], 0, 1) + dot(
                    A[1, :, cols], GT[slot, 1], 0, 1
                )
                first = part * (nz // 2)
                D[0, slot, first : first + nz // 2, :, :, : 3 * width] = value.astype(BF).reshape(
                    nz // 2, 2, shard, 3 * width
                )

        return carry

    lax.fori_loop(0, 2 * heads, attend_back, 0)

    def back_project(half):
        return sum(dot(GT[s, half], whole(G, 0, s)[:, : 3 * width], 0, 1) for s in range(2))

    part_g.wait_send()

    def back_projects(i, carry):
        tick_at("bp", i, 2)
        SR[...] = back_project(lax.rem(other + i, 2))

        @pl.when(i == 0)
        def _():
            SB[...] = SR[...].astype(BF)
            part_a.start()

        return carry

    lax.fori_loop(0, 2, back_projects, 0)
    part_a.wait_recv()
    tick("lnb1")

    def first_back(i, carry):
        unit, inverse = norm_parts(tokens[chunk(i), :].astype(F32))
        grad = SR[chunk(i), :] + XG[chunk(i), :].astype(F32)
        grad_tokens[chunk(i), :] = grad_tokens[chunk(i), :] + norm_back(grad, gain_one, unit, inverse)
        return (carry[0] + column_sum(grad * unit), carry[1] + column_sum(grad))

    sums = over_pieces(first_back, (zero_row, zero_row))
    store_tokens = pltpu.make_async_copy(grad_tokens, grad_tokens_hbm, local_sem.at[3])
    store_tokens.start()
    VL[near_slot(0), 0:1, :] = sums[0]
    VL[near_slot(0), 1:2, :] = sums[1]
    late = [
        remote(
            VL.at[near_slot(0)], VL.at[near_slot(0)],
            late_send.at[j - 1], late_recv.at[j - 1], near(j),
        )
        for j in range(1, 8)
    ]
    for c in late:
        c.start()

    def late_taken(j):
        return remote(
            VL.at[near_slot(0)], VL.at[near_slot(j)],
            late_send.at[j - 1], late_recv.at[j - 1], near(j),
        )

    tick("vs0")
    tick("vs1")

    part_a.wait_send()

    def outer(half):
        return dot(Z[half], whole(G, 2, 0), 1, 1) + dot(Z[2 + half], whole(G, 2, 1), 1, 1)

    def outers(i, carry):
        tick_at("out", i, 2)
        SR[...] = outer(lax.rem(other + i, 2))

        @pl.when(i == 0)
        def _():
            SB[...] = SR[...].astype(BF)
            late_taken(1).wait_recv()
            part_b.start()

        return carry

    lax.fori_loop(0, 1, outers, 0)
    lax.fori_loop(1, 2, outers, 0)
    part_b.wait_recv()
    for j in range(2, 8):
        late_taken(j).wait_recv()
    eight = VL[0]
    for n in range(1, 8):
        eight = eight + VL[n]
    VM[z] = eight
    last = [
        remote(VM.at[z], VM.at[z], late_send.at[7 + j], late_recv.at[7 + j], zpeer(j + 1))
        for j in range(nz - 1)
    ]
    for c in last:
        c.start()
    tick("fin")

    def finish_block(i, carry):
        value = R32[chunk(i), :] + SR[chunk(i), :] + XG[chunk(i), :].astype(F32) + bias_out
        tokens[chunk(i), :] = (AVG[chunk(i), :] + depth[4] * value).astype(BF)
        return carry

    lax.fori_loop(0, pieces, finish_block, 0)
    store_layer = pltpu.make_async_copy(tokens, layer_hbm, local_sem.at[4])
    store_layer.start()
    tick("vs2")
    drain(2)
    tick("end")
    for j in range(nz - 1):
        remote(
            VM.at[z], VM.at[lax.rem(z + nz - 1 - j, nz)],
            late_send.at[7 + j], late_recv.at[7 + j], zpeer(j + 1),
        ).wait_recv()
    first_sums = VM[0]
    for j in range(1, nz):
        first_sums = first_sums + VM[j]
    vector_step(3)
    grad_vectors[0:2, :] = first_sums
    for f in range(len(reduces)):
        reduce_step(f, 4)
    store_tokens.wait()
    store_layer.wait()
    vector_step(4)
    for c in [send_a, send_c, send_gl, part_b] + late + last:
        c.wait_send()


def spread_body(width, cotangent, average, tokens, packed, sums, depth, *outs):
    layer_out, grad_tokens, stack, wq, wk, wv, wo, wi, wu = outs[:9]
    gain_one, shift_one, gain_two, shift_two, bias_in, bias_out, grad_depth = outs[9:]
    layer_out[...] = average[...]
    grad_tokens[...] = tokens[...]
    for k in range(4):
        stack[k] = depth[k] * cotangent[...].astype(F32)

    @pl.when(pl.program_id(0) == 0)
    def _():
        for n, ref in enumerate((wq, wk, wv)):
            ref[...] = packed[0, :, n * width : (n + 1) * width]
        wo[...] = packed[0, :, 3 * width :].T
        wi[...] = packed[1]
        wu[...] = packed[2]
        for n, ref in enumerate((gain_one, shift_one, gain_two, shift_two, bias_out)):
            ref[...] = sums[n, :]
        bias_in[...] = jnp.concatenate([sums[9 + n : 10 + n, :] for n in range(4)], axis=1)
        lane = lax.broadcasted_iota(jnp.int32, (1, 5), 1)
        total = jnp.zeros((1, 5), F32)
        for n, row in enumerate((5, 6, 7, 8, 13)):
            total = jnp.where(lane == n, jnp.sum(sums[row : row + 1, :]), total)
        grad_depth[...] = total


def fused_device(
    tokens,
    stack,
    cotangent,
    starts,
    w_query,
    w_key,
    w_value,
    w_output,
    w_in,
    w_out,
    gain_one,
    shift_one,
    gain_two,
    shift_two,
    bias_in,
    bias_out,
    depth_weights,
):
    rows, features = tokens.shape
    shard = w_query.shape[0]
    nz = lax.axis_size("dp") // 2
    length = 2 * rows
    width = w_query.shape[1]
    heads = width // HEAD_DIM
    cos_np, sin_np = rotary_tables(length)
    gathers, reduces, schedule = PLAN
    shape = jax.ShapeDtypeStruct
    vmem = pl.BlockSpec(memory_space=pltpu.VMEM)
    smem = pl.BlockSpec(memory_space=pltpu.SMEM)
    hbm = pl.BlockSpec(memory_space=pl.ANY)
    dma = pltpu.SemaphoreType.DMA
    scratch = [
        pltpu.VMEM((3, 2, nz, 2, shard, features), BF),
        pltpu.VMEM((3, 2, nz, 2, shard, features), BF),
        pltpu.VMEM((3, 2, nz, shard, features), BF),
        pltpu.VMEM((3, nz, shard, features), BF),
        pltpu.VMEM((3, nz - 1, 2, shard, features), BF),
        pltpu.VMEM((2, rows, features), BF),
        pltpu.VMEM((2, rows, features), BF),
        pltpu.VMEM((2, rows, features), BF),
        pltpu.VMEM((2 * heads, length, HEAD_DIM), BF),
        pltpu.VMEM((2 * heads, length, 2 * HEAD_DIM), BF),
        pltpu.VMEM((2 * heads, HEAD_DIM, length), BF),
        pltpu.VMEM((2 * heads, HEAD_DIM, length), BF),
        pltpu.VMEM((2, 2 * heads, HEAD_DIM, rows), BF),
        pltpu.VMEM((8, length), F32),
        pltpu.VMEM((length // BLOCK, 2 * BLOCK, BLOCK), F32),
        pltpu.VMEM((4, rows, features), BF),
        pltpu.VMEM((4, rows, features), BF),
        pltpu.VMEM((2, 2 * heads, HEAD_DIM, rows), BF),
        pltpu.VMEM((2, 2, 3 * width, rows), BF),
        pltpu.VMEM((2 * width, features), BF),
        pltpu.VMEM((rows, features), F32),
        pltpu.VMEM((rows, features), F32),
        pltpu.VMEM((rows, features), F32),
        pltpu.VMEM((rows, features), BF),
        pltpu.VMEM((rows, features), BF),
        pltpu.VMEM((16, features), F32),
        pltpu.VMEM((8, 2, features), F32),
        pltpu.VMEM((8, 2, features), F32),
        pltpu.VMEM((nz, 2, features), F32),
        pltpu.VMEM((8, 2, features), F32),
        pltpu.VMEM((8, 2, features), F32),
        pltpu.VMEM((nz, 2, features), F32),
        pltpu.VMEM((HEAD_DIM, length), F32),
        pltpu.VMEM((HEAD_DIM, length), F32),
        pltpu.VMEM((rows, features), BF),
        pltpu.VMEM((rows, features), BF),
        pltpu.VMEM((length, 2 * HEAD_DIM), F32),
        pltpu.VMEM((length, 2 * HEAD_DIM), F32),
        pltpu.VMEM((4, features), F32),
        pltpu.VMEM((rows, features), F32),
        dma((5,)),
        dma((len(gathers), nz + 1)),
        dma((len(gathers), nz + 1)),
        dma((len(reduces), nz + 2)),
        dma((len(reduces), nz + 2)),
        dma((9,)),
        dma((9,)),
        dma((nz + 13,)),
        dma((nz + 13,)),
        dma((nz + 6,)),
        dma((nz + 6,)),
    ]

    layer_out, grad_tokens, packed, sums = pl.pallas_call(
        functools.partial(fused_body, nz, rows, features, shard, PLAN),
        out_shape=[
            shape((rows, features), BF),
            shape((rows, features), F32),
            shape((3, shard, features), F32),
            shape((16, features), F32),
        ],
        in_specs=[hbm] * 3 + [vmem] * 12 + [smem] * 2 + [vmem] * 2,
        out_specs=[hbm] * 2 + [vmem] * 2,
        scratch_shapes=scratch,
        compiler_params=pltpu.CompilerParams(
            collective_id=0, has_side_effects=True, vmem_limit_bytes=64 * 1024 * 1024
        ),
    )(
        tokens,
        cotangent,
        stack,
        w_query,
        w_key,
        w_value,
        w_output,
        w_in,
        w_out.T,
        gain_one,
        shift_one,
        gain_two,
        shift_two,
        bias_in.reshape(1, -1),
        bias_out,
        depth_weights,
        starts,
        jnp.asarray(cos_np.T.copy()),
        jnp.asarray(sin_np.T.copy()),
    )

    steps = 2
    part = rows // steps
    sizes = (
        [(shard, width)] * 3
        + [(width, shard), (shard, features), (shard, features)]
        + [(features,)] * 4
        + [(1, 4 * features), (features,), (1, 5)]
    )

    def fixed(size):
        return pl.BlockSpec(size, lambda i: (0,) * len(size))

    by_rows = pl.BlockSpec((part, features), lambda i: (i, 0))
    outs = pl.pallas_call(
        functools.partial(spread_body, width),
        grid=(steps,),
        out_shape=[
            shape((rows, features), BF),
            shape((rows, features), F32),
            shape((4, rows, features), F32),
        ]
        + [shape(size, F32) for size in sizes],
        in_specs=[by_rows] * 3 + [fixed((3, shard, features)), fixed((16, features)), smem],
        out_specs=[by_rows] * 2
        + [pl.BlockSpec((4, part, features), lambda i: (0, i, 0))]
        + [fixed(size) for size in sizes],
        compiler_params=pltpu.CompilerParams(vmem_limit_bytes=60 * 1024 * 1024),
    )(cotangent, layer_out, grad_tokens, packed, sums, depth_weights)
    return (*outs[:8], outs[8].T, *outs[9:13], outs[13].reshape(-1), outs[14], outs[15].reshape(-1))


def per_device(*arrays):
    rows, features = arrays[0].shape
    shard, width = arrays[4].shape
    dp = lax.axis_size("dp")
    fits = (
        shard % 16 == 0
        and dp % 4 == 0
        and lax.axis_size("tensor") == 4
        and arrays[3].shape[0] == 2
        and arrays[8].shape[1] == features
        and 4 * width == features
        and shard * dp == features
    )
    return fused_device(*arrays) if fits else plain_device(*arrays)


def solution(mesh):
    in_specs = (
        P(("dp", "tensor"), None),
        P(None, ("dp", "tensor"), None),
        P(("dp", "tensor"), None),
        P("dp", None),
        P("dp", "tensor"),
        P("dp", "tensor"),
        P("dp", "tensor"),
        P("tensor", "dp"),
        P("dp", "tensor"),
        P("tensor", "dp"),
        P(),
        P(),
        P(),
        P(),
        P(),
        P(),
        P(),
    )
    out_specs = (
        P(("dp", "tensor"), None),
        P(("dp", "tensor"), None),
        P(None, ("dp", "tensor"), None),
        P("dp", "tensor"),
        P("dp", "tensor"),
        P("dp", "tensor"),
        P("tensor", "dp"),
        P("dp", "tensor"),
        P("tensor", "dp"),
        P(),
        P(),
        P(),
        P(),
        P(),
        P(),
        P(),
    )
    return jax.shard_map(
        per_device, mesh=mesh, in_specs=in_specs, out_specs=out_specs, check_vma=False
    )
```
